512 devices in a mesh: fsdp: 16 (over y, x_lo), ed: 32 (over x_hi, z, core).
Axes of the slice: x: 4 (x_hi: 2, x_lo: 2; x = x_hi * 2 + x_lo), y: 8, z: 8, core: 2. Of those that a mesh axis runs over, the one named last changes fastest.
Arguments:
- tokens: bfloat16 [9216, 6144], P('ed', 'fsdp'), may hold values from -6 to 6
- expert_ids: int32 [9216, 2], P('ed'), may hold values from 0 to 7, all different within a row; in each aligned block of 288 rows (0 to 287, 288 to 575, ...) at most 81 rows name the same one
- route_weights: float32 [9216, 2], P('ed'), may hold values from 0.1 to 1
- w_gate: bfloat16 [1, 6144, 8192], P(None, 'fsdp', 'ed'), may hold values from -0.078125 to 0.078125
- w_up: bfloat16 [1, 6144, 8192], P(None, 'fsdp', 'ed'), may hold values from -0.078125 to 0.078125
- w_down: bfloat16 [1, 8192, 6144], P(None, 'ed', 'fsdp'), may hold values from -0.0625 to 0.0625
Outputs:
- mixed: bfloat16 [9216, 6144], P('ed', 'fsdp')
The draws below stay inside these ranges and needn't reach their ends.
Inputs may be any that keep to these rules, and one draw needn't show every extreme that they name: `expert_ids`: each row names two different experts. In each block of 288 rows that one index of ed holds, no expert is named by more than 81 rows, a bound that some block reaches.
All inputs are finite; a program needn't handle non-finite values.
Results may differ from the reference program's by a relative error of at most 0.025.
Values may be sent and summed in bfloat16 or wider, within the bound.
A program may use at most 64 MiB of HBM per device.

```python
import math
import jax
import jax.numpy as jnp
import numpy as np
from jax import lax

D = 6144
EXPERTS = 8
FF = 8192
EW = 1
TOK_DEV = 288
CAP = 81
TOKENS = 9216
N_ED = 32


def steps_of(rng, extent, split, low, largest):
    level, own = 1.0, jax.random.fold_in(rng, 6)
    for dim, parts in split:
        draws = jnp.exp(jax.random.uniform(jax.random.fold_in(own, dim), (parts,), jnp.float32, low / len(split), largest / len(split)))
        level = level * jnp.repeat(draws, extent[dim] // parts).reshape([-1 if axis == dim else 1 for axis in range(len(extent))])
    return level


def assign_block(own_key, own, number, rows, amount, top, bound, lean):
    order = jax.random.permutation(own_key, amount)
    crowded, ordinary = portions_of(amount, rows * top, bound, lean, True), portions_of(amount, rows * top, bound, lean, False)
    places = jnp.arange(amount)

    def named(tallies, rotation):
        used = int((tallies > 0).sum())
        fixed = max(1, used // 4)
        moved = fixed + (places - fixed + rotation * (used - fixed)) % max(1, amount - fixed)
        return jnp.zeros((amount,), jnp.int32).at[order[jnp.where(places < fixed, places, moved)]].set(jnp.asarray(tallies, jnp.int32))

    tallies = jnp.where(number % 4 == 0, named(crowded, number // 4), named(ordinary, number - number // 4 - 1))
    mixed = jax.random.permutation(jax.random.fold_in(own, 3), amount)
    donor, receiver = mixed[0:amount // 2 * 2:2], mixed[1:amount // 2 * 2:2]
    slack = jnp.minimum(tallies[donor] - 1, bound - tallies[receiver]) // 2
    slack = jnp.where((donor == order[0]) | (receiver == order[0]) | (tallies[receiver] == 0), 0, jnp.maximum(slack, 0))
    moved = jax.random.randint(jax.random.fold_in(own, 4), (amount // 2,), 0, 1 << 20) % (slack + 1)
    tallies = tallies.at[donor].add(-moved).at[receiver].add(moved)
    items = jnp.searchsorted(jnp.cumsum(tallies), jnp.arange(rows * top), side="right").astype(jnp.int32)
    table = items.reshape(top, rows).T
    table = table[jax.random.permutation(jax.random.fold_in(own, 1), rows)]
    rotation = jax.random.randint(jax.random.fold_in(own, 2), (rows, 1), 0, top)
    return jnp.take_along_axis(table, (jnp.arange(top)[None, :] + rotation) % top, axis=1)


def portions_of(number_of, total, limit, slope, full):
    loads = [(1 << 20) // math.isqrt(standing ** slope) + 1 for standing in range(1, number_of + 1)]
    largest = limit if full else min(limit, max(-(-total // number_of), total * loads[0] // sum(loads)))
    least = 1 if total - largest >= number_of - 1 else 0
    given, surplus = [largest] + [least] * (number_of - 1), total - largest - least * (number_of - 1)
    while surplus > 0:
        movable = [i for i in range(1, number_of) if given[i] < largest] or [i for i in range(1, number_of) if given[i] < limit]
        pool, budget = sum([loads[i] for i in movable]), surplus
        for i in movable:
            more = min(limit - given[i], max(1, budget * loads[i] // pool), surplus)
            given[i] = given[i] + more
            surplus = surplus - more
    return np.array(given)


def scatter_about(rng, dims, width, most, split=(), kind=jnp.bfloat16):
    drawn = jax.random.normal(rng, dims, jnp.float32) * width
    if len(split) > 0:
        drawn = steps_of(rng, dims, split, -0.22, 0.18) * drawn
    return jnp.clip(drawn, min=-most, max=most).astype(kind)


def setup_inputs(seed: int = 0) -> dict:
    key_of = jax.random.split(jax.random.key(seed), 7)
    tokens = scatter_about(key_of[0], (TOKENS, D), 1.0, 6.0, ((0, 32), (1, 16)))
    expert_ids_keys = jax.random.split(jax.random.fold_in(key_of[1], 1), TOKENS // TOK_DEV)
    expert_ids_turns = jax.random.permutation(jax.random.fold_in(key_of[1], 3), TOKENS // TOK_DEV)
    expert_ids = jax.vmap(lambda own, number: assign_block(jax.random.fold_in(key_of[1], 2), own, number, TOK_DEV, EXPERTS, 2, CAP, 1))(expert_ids_keys, expert_ids_turns).reshape((TOKENS, 2))
    route_weights = jnp.clip(0.1 + 0.9 * jax.random.uniform(key_of[2], (TOKENS, 2), jnp.float32) ** steps_of(key_of[2], (TOKENS, 2), ((0, 32),), -0.2, 0.2), 0.1, 1.0)
    w_gate = scatter_about(key_of[3], (EW, D, FF), D ** -0.5, 0.078125, ((1, 16), (2, 32)))
    w_up = scatter_about(key_of[4], (EW, D, FF), D ** -0.5, 0.078125, ((1, 16), (2, 32)))
    w_down = scatter_about(key_of[5], (EW, FF, D), FF ** -0.5, 0.0625, ((1, 32), (2, 16)))
    return {"tokens": tokens, "expert_ids": expert_ids, "route_weights": route_weights, "w_gate": w_gate, "w_up": w_up, "w_down": w_down}


def slot_match(routes, window, capacity):
    window_ids = jnp.arange(window, dtype=jnp.int32)
    routed = jnp.any(routes[:, :, None, :] == window_ids[None, None, :, None], axis=3)
    position = jnp.cumsum(routed.astype(jnp.int32), axis=1) - 1
    slot_ids = jnp.arange(capacity, dtype=jnp.int32)
    hits = routed[:, :, :, None] & (position[:, :, :, None] == slot_ids[None, None, None, :])
    return hits.astype(jnp.int32)


def take_block(block_rows, row_list):
    return jnp.take(block_rows, row_list, axis=0)


def pick_rows(blocks, routes, window, capacity):
    match = slot_match(routes, window, capacity)
    row_numbers = jnp.arange(blocks.shape[1], dtype=jnp.int32)
    source_row = jnp.sum(match * row_numbers[None, :, None, None], axis=1).reshape(blocks.shape[0], window * capacity)
    filled = jnp.sum(match, axis=1).reshape(blocks.shape[0], window * capacity)
    picked = jax.vmap(take_block)(blocks, source_row)
    picked = jnp.where(filled[:, :, None] > 0, picked, jnp.zeros_like(picked))
    return picked.reshape(blocks.shape[0], window, capacity, blocks.shape[2])


def combine_matrix(routes, weights, window, capacity):
    match = slot_match(routes[None], window, capacity)[0]
    window_ids = jnp.arange(window, dtype=jnp.int32)
    per_expert = jnp.sum(jnp.where(routes[:, None, :] == window_ids[None, :, None], weights[:, None, :], jnp.zeros_like(weights[:, None, :])), axis=2)
    return (per_expert[:, :, None] * match.astype(weights.dtype)).reshape(routes.shape[0], window * capacity)


def reference(tokens, expert_ids, route_weights, w_gate, w_up, w_down):
    blocks = tokens.reshape(N_ED, TOK_DEV, D)
    route_blocks = expert_ids.reshape(N_ED, TOK_DEV, 2)
    weight_blocks = route_weights.reshape(N_ED, TOK_DEV, 2)
    selected = pick_rows(blocks, route_blocks, EW, CAP)
    selected = selected.transpose(1, 0, 2, 3).reshape(EW, N_ED * CAP, D)
    hidden_piece = FF // N_ED
    slot_total = N_ED * CAP

    def one_expert(operands):
        slot_rows_x, gate_weight, up_weight, down_weight = operands
        gate = jnp.dot(slot_rows_x, gate_weight, preferred_element_type=jnp.float32)
        up = jnp.dot(slot_rows_x, up_weight, preferred_element_type=jnp.float32)
        activation = (jax.nn.silu(gate) * up).astype(jnp.bfloat16)
        terms = jnp.einsum("rqk,qkd->qrd", activation.astype(jnp.float32).reshape(slot_total, N_ED, hidden_piece), down_weight.astype(jnp.float32).reshape(N_ED, hidden_piece, D))
        rounded = lax.optimization_barrier(terms.astype(jnp.bfloat16))
        return jnp.sum(rounded.astype(jnp.float32), axis=0)

    slot_out = lax.map(one_expert, (selected, w_gate, w_up, w_down))
    slot_out = slot_out.reshape(EW, N_ED, CAP, D).transpose(1, 0, 2, 3).reshape(N_ED, EW * CAP, D)
    matrices = jax.vmap(combine_matrix, in_axes=(0, 0, None, None))(route_blocks, weight_blocks, EW, CAP)
    mixed = jnp.einsum("stk,skd->std", matrices, slot_out, precision=lax.Precision.HIGHEST)
    return mixed.reshape(TOKENS, D).astype(jnp.bfloat16)
```

```python
import jax
import jax.numpy as jnp
from jax import lax
from jax.sharding import PartitionSpec as P

CAP = 81


def slot_match(routes, window, capacity):
    window_ids = jnp.arange(window, dtype=jnp.int32)
    routed = jnp.any(routes[:, :, None, :] == window_ids[None, None, :, None], axis=3)
    position = jnp.cumsum(routed.astype(jnp.int32), axis=1) - 1
    slot_ids = jnp.arange(capacity, dtype=jnp.int32)
    hits = routed[:, :, :, None] & (position[:, :, :, None] == slot_ids[None, None, None, :])
    return hits.astype(jnp.int32)


def take_block(block_rows, row_list):
    return jnp.take(block_rows, row_list, axis=0)


def pick_rows(blocks, routes, window, capacity):
    match = slot_match(routes, window, capacity)
    row_numbers = jnp.arange(blocks.shape[1], dtype=jnp.int32)
    source_row = jnp.sum(match * row_numbers[None, :, None, None], axis=1).reshape(
        blocks.shape[0], window * capacity
    )
    filled = jnp.sum(match, axis=1).reshape(blocks.shape[0], window * capacity)
    picked = jax.vmap(take_block)(blocks, source_row)
    picked = jnp.where(filled[:, :, None] > 0, picked, jnp.zeros_like(picked))
    return picked.reshape(blocks.shape[0], window, capacity, blocks.shape[2])


def combine_matrix(routes, weights, window, capacity):
    match = slot_match(routes[None], window, capacity)[0]
    window_ids = jnp.arange(window, dtype=jnp.int32)
    per_expert = jnp.sum(
        jnp.where(
            routes[:, None, :] == window_ids[None, :, None],
            weights[:, None, :],
            jnp.zeros_like(weights[:, None, :]),
        ),
        axis=2,
    )
    return (per_expert[:, :, None] * match.astype(weights.dtype)).reshape(
        routes.shape[0], window * capacity
    )


def local(tokens, expert_ids, route_weights, w_gate, w_up, w_down):
    window = w_gate.shape[0]
    features_dev = tokens.shape[1]
    hidden_dev = w_gate.shape[2]
    n_ed = lax.axis_size("ed")
    own_slots = pick_rows(tokens[None], expert_ids[None], window, CAP)[0, 0]
    selected = lax.all_gather(own_slots, "ed", axis=0, tiled=True)
    both = jnp.concatenate([w_gate[0], w_up[0]], axis=1)
    partial = jnp.dot(selected, both, preferred_element_type=jnp.float32)
    n_fsdp = lax.axis_size("fsdp")
    rows = partial.shape[0]
    band = -(-rows // (8 * n_fsdp)) * 8
    partial = jnp.pad(partial, ((0, band * n_fsdp - rows), (0, 0)))
    summed = lax.psum_scatter(partial, "fsdp", scatter_dimension=0, tiled=True)
    gate_part = summed[:, :hidden_dev]
    up_part = summed[:, hidden_dev:]
    activation = (jax.nn.silu(gate_part) * up_part).astype(jnp.bfloat16)
    act_rows = lax.all_gather(activation, "fsdp", axis=0, tiled=True)[:rows]
    term = jnp.dot(act_rows, w_down[0], preferred_element_type=jnp.float32)
    term = term.astype(jnp.bfloat16).reshape(n_ed, CAP, features_dev)
    arrived = lax.all_to_all(term, "ed", split_axis=0, concat_axis=0, tiled=True)
    slot_out = jnp.sum(arrived.astype(jnp.float32), axis=0)
    weights_matrix = combine_matrix(expert_ids, route_weights, window, CAP)
    mixed = jnp.dot(
        weights_matrix,
        slot_out.reshape(window * CAP, features_dev),
        precision=lax.Precision.HIGHEST,
        preferred_element_type=jnp.float32,
    )
    return mixed.astype(jnp.bfloat16)


def solution(mesh):
    return jax.shard_map(
        local,
        mesh=mesh,
        in_specs=(
            P("ed", "fsdp"),
            P("ed", None),
            P("ed", None),
            P(None, "fsdp", "ed"),
            P(None, "fsdp", "ed"),
            P(None, "ed", "fsdp"),
        ),
        out_specs=P("ed", "fsdp"),
        check_vma=False,
    )
```

```python
import functools

import jax
import jax.numpy as jnp
from jax import lax
from jax.experimental import pallas as pl
from jax.experimental.pallas import tpu as pltpu
from jax.sharding import PartitionSpec as P

CAP = 81
MESH = pl.DeviceIdType.MESH


def slot_match(routes, window, capacity):
    window_ids = jnp.arange(window, dtype=jnp.int32)
    routed = jnp.any(routes[:, :, None, :] == window_ids[None, None, :, None], axis=3)
    position = jnp.cumsum(routed.astype(jnp.int32), axis=1) - 1
    slot_ids = jnp.arange(capacity, dtype=jnp.int32)
    hits = routed[:, :, :, None] & (position[:, :, :, None] == slot_ids[None, None, None, :])
    return hits.astype(jnp.int32)


def take_block(block_rows, row_list):
    return jnp.take(block_rows, row_list, axis=0)


def pick_rows(blocks, routes, window, capacity):
    match = slot_match(routes, window, capacity)
    row_numbers = jnp.arange(blocks.shape[1], dtype=jnp.int32)
    source_row = jnp.sum(match * row_numbers[None, :, None, None], axis=1).reshape(
        blocks.shape[0], window * capacity
    )
    filled = jnp.sum(match, axis=1).reshape(blocks.shape[0], window * capacity)
    picked = jax.vmap(take_block)(blocks, source_row)
    picked = jnp.where(filled[:, :, None] > 0, picked, jnp.zeros_like(picked))
    return picked.reshape(blocks.shape[0], window, capacity, blocks.shape[2])


def combine_matrix(routes, weights, window, capacity):
    match = slot_match(routes[None], window, capacity)[0]
    window_ids = jnp.arange(window, dtype=jnp.int32)
    per_expert = jnp.sum(
        jnp.where(
            routes[:, None, :] == window_ids[None, :, None],
            weights[:, None, :],
            jnp.zeros_like(weights[:, None, :]),
        ),
        axis=2,
    )
    return (per_expert[:, :, None] * match.astype(weights.dtype)).reshape(
        routes.shape[0], window * capacity
    )


def _exchange_kernel(axis, n, gather, x_ref, o_ref, send_sem, recv_sem, own_sem):
    me = lax.axis_index(axis)

    def peer_of(i):
        return lax.rem(me + 1 + i, n)

    def source(peer):
        return x_ref if gather else x_ref.at[peer]

    def outgoing(peer):
        return pltpu.make_async_remote_copy(
            src_ref=source(peer),
            dst_ref=o_ref.at[me],
            send_sem=send_sem.at[peer],
            recv_sem=recv_sem.at[me],
            device_id={axis: peer},
            device_id_type=MESH,
        )

    def incoming(peer):
        return pltpu.make_async_remote_copy(
            src_ref=source(peer),
            dst_ref=o_ref.at[peer],
            send_sem=send_sem.at[peer],
            recv_sem=recv_sem.at[peer],
            device_id={axis: peer},
            device_id_type=MESH,
        )

    barrier = pltpu.get_barrier_semaphore()

    def greet(i, carry):
        pl.semaphore_signal(barrier, 1, device_id={axis: peer_of(i)}, device_id_type=MESH)
        return carry

    lax.fori_loop(0, n - 1, greet, 0)
    pl.semaphore_wait(barrier, n - 1)

    def send(i, carry):
        outgoing(peer_of(i)).start()
        return carry

    lax.fori_loop(0, n - 1, send, 0)
    own = pltpu.make_async_copy(source(me), o_ref.at[me], own_sem)
    own.start()

    def finish(i, carry):
        peer = peer_of(i)
        outgoing(peer).wait_send()
        incoming(peer).wait_recv()
        return carry

    lax.fori_loop(0, n - 1, finish, 0)
    own.wait()


def exchange(x, axis, n, gather, cid):
    block = x.shape if gather else x.shape[1:]
    return pl.pallas_call(
        functools.partial(_exchange_kernel, axis, n, gather),
        out_shape=jax.ShapeDtypeStruct((n,) + tuple(block), x.dtype),
        in_specs=[pl.BlockSpec(memory_space=pl.ANY)],
        out_specs=pl.BlockSpec(memory_space=pl.ANY),
        scratch_shapes=[
            pltpu.SemaphoreType.DMA((n,)),
            pltpu.SemaphoreType.DMA((n,)),
            pltpu.SemaphoreType.DMA,
        ],
        compiler_params=pltpu.CompilerParams(collective_id=cid, has_side_effects=True),
    )(x)


def local(tokens, expert_ids, route_weights, w_gate, w_up, w_down):
    window = w_gate.shape[0]
    features_dev = tokens.shape[1]
    hidden_dev = w_gate.shape[2]
    n_ed = lax.axis_size("ed")
    n_fsdp = lax.axis_size("fsdp")
    per_band = n_ed // n_fsdp
    own_slots = pick_rows(tokens[None], expert_ids[None], window, CAP)[0, 0]
    selected = exchange(own_slots, "ed", n_ed, True, 0)
    selected = selected.reshape(n_fsdp, per_band, CAP, features_dev)
    both = jnp.concatenate([w_gate[0], w_up[0]], axis=1)
    partial = jnp.einsum("fbri,ih->fbrh", selected, both, preferred_element_type=jnp.float32)
    arrived = exchange(partial, "fsdp", n_fsdp, False, 1)
    summed = jnp.sum(arrived, axis=0)
    gate_part = summed[..., :hidden_dev]
    up_part = summed[..., hidden_dev:]
    activation = (jax.nn.silu(gate_part) * up_part).astype(jnp.bfloat16)
    act_rows = exchange(activation, "fsdp", n_fsdp, True, 2)
    act_rows = act_rows.reshape(n_ed, CAP, hidden_dev)
    term = jnp.einsum("brh,hd->brd", act_rows, w_down[0], preferred_element_type=jnp.float32)
    term = term.astype(jnp.bfloat16)
    pieces = exchange(term, "ed", n_ed, False, 3)
    slot_out = jnp.sum(pieces.astype(jnp.float32), axis=0)
    weights_matrix = combine_matrix(expert_ids, route_weights, window, CAP)
    mixed = jnp.dot(
        weights_matrix,
        slot_out.reshape(window * CAP, features_dev),
        precision=lax.Precision.HIGHEST,
        preferred_element_type=jnp.float32,
    )
    return mixed.astype(jnp.bfloat16)


def solution(mesh):
    return jax.shard_map(
        local,
        mesh=mesh,
        in_specs=(
            P("ed", "fsdp"),
            P("ed", None),
            P("ed", None),
            P(None, "fsdp", "ed"),
            P(None, "fsdp", "ed"),
            P(None, "ed", "fsdp"),
        ),
        out_specs=P("ed", "fsdp"),
        check_vma=False,
    )
```

```python
import functools

import jax
import jax.numpy as jnp
from jax import lax
from jax.experimental import pallas as pl
from jax.experimental.pallas import tpu as pltpu
from jax.sharding import PartitionSpec as P

CAP = 81
MESH = pl.DeviceIdType.MESH


def slot_match(routes, window, capacity):
    window_ids = jnp.arange(window, dtype=jnp.int32)
    routed = jnp.any(routes[:, :, None, :] == window_ids[None, None, :, None], axis=3)
    position = jnp.cumsum(routed.astype(jnp.int32), axis=1) - 1
    slot_ids = jnp.arange(capacity, dtype=jnp.int32)
    hits = routed[:, :, :, None] & (position[:, :, :, None] == slot_ids[None, None, None, :])
    return hits.astype(jnp.int32)


def take_block(block_rows, row_list):
    return jnp.take(block_rows, row_list, axis=0)


def pick_rows(blocks, routes, window, capacity):
    match = slot_match(routes, window, capacity)
    row_numbers = jnp.arange(blocks.shape[1], dtype=jnp.int32)
    source_row = jnp.sum(match * row_numbers[None, :, None, None], axis=1).reshape(
        blocks.shape[0], window * capacity
    )
    filled = jnp.sum(match, axis=1).reshape(blocks.shape[0], window * capacity)
    picked = jax.vmap(take_block)(blocks, source_row)
    picked = jnp.where(filled[:, :, None] > 0, picked, jnp.zeros_like(picked))
    return picked.reshape(blocks.shape[0], window, capacity, blocks.shape[2])


def combine_matrix(routes, weights, window, capacity):
    match = slot_match(routes[None], window, capacity)[0]
    window_ids = jnp.arange(window, dtype=jnp.int32)
    per_expert = jnp.sum(
        jnp.where(
            routes[:, None, :] == window_ids[None, :, None],
            weights[:, None, :],
            jnp.zeros_like(weights[:, None, :]),
        ),
        axis=2,
    )
    return (per_expert[:, :, None] * match.astype(weights.dtype)).reshape(
        routes.shape[0], window * capacity
    )


def _exchange_kernel(axis, n, gather, x_ref, o_ref, send_sem, recv_sem, own_sem):
    me = lax.axis_index(axis)

    def peer_of(i):
        return lax.rem(me + 1 + i, n)

    def source(peer):
        return x_ref if gather else x_ref.at[peer]

    def outgoing(peer):
        return pltpu.make_async_remote_copy(
            src_ref=source(peer),
            dst_ref=o_ref.at[me],
            send_sem=send_sem.at[peer],
            recv_sem=recv_sem.at[me],
            device_id={axis: peer},
            device_id_type=MESH,
        )

    def incoming(peer):
        return pltpu.make_async_remote_copy(
            src_ref=source(peer),
            dst_ref=o_ref.at[peer],
            send_sem=send_sem.at[peer],
            recv_sem=recv_sem.at[peer],
            device_id={axis: peer},
            device_id_type=MESH,
        )

    barrier = pltpu.get_barrier_semaphore()

    def greet(i, carry):
        pl.semaphore_signal(barrier, 1, device_id={axis: peer_of(i)}, device_id_type=MESH)
        return carry

    lax.fori_loop(0, n - 1, greet, 0)
    pl.semaphore_wait(barrier, n - 1)

    def send(i, carry):
        outgoing(peer_of(i)).start()
        return carry

    lax.fori_loop(0, n - 1, send, 0)
    own = pltpu.make_async_copy(source(me), o_ref.at[me], own_sem)
    own.start()

    def finish(i, carry):
        peer = peer_of(i)
        outgoing(peer).wait_send()
        incoming(peer).wait_recv()
        return carry

    lax.fori_loop(0, n - 1, finish, 0)
    own.wait()


def exchange(x, axis, n, gather, cid):
    block = x.shape if gather else x.shape[1:]
    return pl.pallas_call(
        functools.partial(_exchange_kernel, axis, n, gather),
        out_shape=jax.ShapeDtypeStruct((n,) + tuple(block), x.dtype),
        in_specs=[pl.BlockSpec(memory_space=pl.ANY)],
        out_specs=pl.BlockSpec(memory_space=pl.ANY),
        scratch_shapes=[
            pltpu.SemaphoreType.DMA((n,)),
            pltpu.SemaphoreType.DMA((n,)),
            pltpu.SemaphoreType.DMA,
        ],
        compiler_params=pltpu.CompilerParams(collective_id=cid, has_side_effects=True),
    )(x)


def local(tokens, expert_ids, route_weights, w_gate, w_up, w_down):
    window = w_gate.shape[0]
    features_dev = tokens.shape[1]
    hidden_dev = w_gate.shape[2]
    n_ed = lax.axis_size("ed")
    n_fsdp = lax.axis_size("fsdp")
    per_band = n_ed // n_fsdp
    own_slots = pick_rows(tokens[None], expert_ids[None], window, CAP)[0, 0]
    selected = exchange(own_slots, "ed", n_ed, True, 0)
    selected = selected.reshape(n_fsdp, per_band, CAP, features_dev)
    both = jnp.concatenate([w_gate[0], w_up[0]], axis=1)
    partial = jnp.einsum("fbri,ih->fbrh", selected, both, preferred_element_type=jnp.float32)
    arrived = exchange(partial.astype(jnp.bfloat16), "fsdp", n_fsdp, False, 1)
    summed = jnp.sum(arrived.astype(jnp.float32), axis=0)
    gate_part = summed[..., :hidden_dev]
    up_part = summed[..., hidden_dev:]
    activation = (jax.nn.silu(gate_part) * up_part).astype(jnp.bfloat16)
    act_rows = exchange(activation, "fsdp", n_fsdp, True, 2)
    act_rows = act_rows.reshape(n_ed, CAP, hidden_dev)
    term = jnp.einsum("brh,hd->brd", act_rows, w_down[0], preferred_element_type=jnp.float32)
    term = term.astype(jnp.bfloat16)
    pieces = exchange(term, "ed", n_ed, False, 3)
    slot_out = jnp.sum(pieces.astype(jnp.float32), axis=0)
    weights_matrix = combine_matrix(expert_ids, route_weights, window, CAP)
    mixed = jnp.dot(
        weights_matrix,
        slot_out.reshape(window * CAP, features_dev),
        precision=lax.Precision.HIGHEST,
        preferred_element_type=jnp.float32,
    )
    return mixed.astype(jnp.bfloat16)


def solution(mesh):
    return jax.shard_map(
        local,
        mesh=mesh,
        in_specs=(
            P("ed", "fsdp"),
            P("ed", None),
            P("ed", None),
            P(None, "fsdp", "ed"),
            P(None, "fsdp", "ed"),
            P(None, "ed", "fsdp"),
        ),
        out_specs=P("ed", "fsdp"),
        check_vma=False,
    )
```

```python
import functools

import jax
import jax.numpy as jnp
from jax import lax
from jax.experimental import pallas as pl
from jax.experimental.pallas import tpu as pltpu
from jax.sharding import PartitionSpec as P

CAP = 81
MESH = pl.DeviceIdType.MESH


def slot_match(routes, window, capacity):
    window_ids = jnp.arange(window, dtype=jnp.int32)
    routed = jnp.any(routes[:, :, None, :] == window_ids[None, None, :, None], axis=3)
    position = jnp.cumsum(routed.astype(jnp.int32), axis=1) - 1
    slot_ids = jnp.arange(capacity, dtype=jnp.int32)
    hits = routed[:, :, :, None] & (position[:, :, :, None] == slot_ids[None, None, None, :])
    return hits.astype(jnp.int32)


def take_block(block_rows, row_list):
    return jnp.take(block_rows, row_list, axis=0)


def pick_rows(blocks, routes, window, capacity):
    match = slot_match(routes, window, capacity)
    row_numbers = jnp.arange(blocks.shape[1], dtype=jnp.int32)
    source_row = jnp.sum(match * row_numbers[None, :, None, None], axis=1).reshape(
        blocks.shape[0], window * capacity
    )
    filled = jnp.sum(match, axis=1).reshape(blocks.shape[0], window * capacity)
    picked = jax.vmap(take_block)(blocks, source_row)
    picked = jnp.where(filled[:, :, None] > 0, picked, jnp.zeros_like(picked))
    return picked.reshape(blocks.shape[0], window, capacity, blocks.shape[2])


def combine_matrix(routes, weights, window, capacity):
    match = slot_match(routes[None], window, capacity)[0]
    window_ids = jnp.arange(window, dtype=jnp.int32)
    per_expert = jnp.sum(
        jnp.where(
            routes[:, None, :] == window_ids[None, :, None],
            weights[:, None, :],
            jnp.zeros_like(weights[:, None, :]),
        ),
        axis=2,
    )
    return (per_expert[:, :, None] * match.astype(weights.dtype)).reshape(
        routes.shape[0], window * capacity
    )


def _exchange_kernel(axis, m, stride, gather, x_ref, o_ref, send_sem, recv_sem, own_sem):
    me = lax.axis_index(axis)
    k = lax.rem(me // stride, m)
    base = me - k * stride

    def member(i):
        return lax.rem(k + 1 + i, m)

    def device(j):
        return {axis: base + j * stride}

    def source(j):
        return x_ref if gather else x_ref.at[j]

    def outgoing(j):
        return pltpu.make_async_remote_copy(
            src_ref=source(j),
            dst_ref=o_ref.at[k],
            send_sem=send_sem.at[j],
            recv_sem=recv_sem.at[k],
            device_id=device(j),
            device_id_type=MESH,
        )

    def incoming(j):
        return pltpu.make_async_remote_copy(
            src_ref=source(j),
            dst_ref=o_ref.at[j],
            send_sem=send_sem.at[j],
            recv_sem=recv_sem.at[j],
            device_id=device(j),
            device_id_type=MESH,
        )

    barrier = pltpu.get_barrier_semaphore()

    def greet(i, carry):
        pl.semaphore_signal(barrier, 1, device_id=device(member(i)), device_id_type=MESH)
        return carry

    lax.fori_loop(0, m - 1, greet, 0)
    pl.semaphore_wait(barrier, m - 1)

    def send(i, carry):
        outgoing(member(i)).start()
        return carry

    lax.fori_loop(0, m - 1, send, 0)
    own = pltpu.make_async_copy(source(k), o_ref.at[k], own_sem)
    own.start()

    def finish(i, carry):
        j = member(i)
        outgoing(j).wait_send()
        incoming(j).wait_recv()
        return carry

    lax.fori_loop(0, m - 1, finish, 0)
    own.wait()


def exchange(x, axis, m, stride, gather, cid):
    block = x.shape if gather else x.shape[1:]
    return pl.pallas_call(
        functools.partial(_exchange_kernel, axis, m, stride, gather),
        out_shape=jax.ShapeDtypeStruct((m,) + tuple(block), x.dtype),
        in_specs=[pl.BlockSpec(memory_space=pl.ANY)],
        out_specs=pl.BlockSpec(memory_space=pl.ANY),
        scratch_shapes=[
            pltpu.SemaphoreType.DMA((m,)),
            pltpu.SemaphoreType.DMA((m,)),
            pltpu.SemaphoreType.DMA,
        ],
        compiler_params=pltpu.CompilerParams(collective_id=cid, has_side_effects=True),
    )(x)


def local(tokens, expert_ids, route_weights, w_gate, w_up, w_down):
    window = w_gate.shape[0]
    features_dev = tokens.shape[1]
    hidden_dev = w_gate.shape[2]
    n_ed = lax.axis_size("ed")
    n_fsdp = lax.axis_size("fsdp")
    chips = n_ed // 2
    per_band = n_ed // n_fsdp
    own_slots = pick_rows(tokens[None], expert_ids[None], window, CAP)[0, 0]
    same_core = exchange(own_slots, "ed", chips, 2, True, 0)
    selected = exchange(same_core, "ed", 2, 1, True, 1)
    selected = selected.reshape(n_fsdp, per_band, CAP, features_dev)
    both = jnp.concatenate([w_gate[0], w_up[0]], axis=1)
    partial = jnp.einsum("fbri,ih->fbrh", selected, both, preferred_element_type=jnp.float32)
    arrived = exchange(partial.astype(jnp.bfloat16), "fsdp", n_fsdp, 1, False, 2)
    summed = jnp.sum(arrived.astype(jnp.float32), axis=0)
    gate_part = summed[..., :hidden_dev]
    up_part = summed[..., hidden_dev:]
    activation = (jax.nn.silu(gate_part) * up_part).astype(jnp.bfloat16)
    act_rows = exchange(activation, "fsdp", n_fsdp, 1, True, 3)
    act_rows = act_rows.reshape(2, chips, CAP, hidden_dev)
    term = jnp.einsum("cbrh,hd->cbrd", act_rows, w_down[0], preferred_element_type=jnp.float32)
    term = term.astype(jnp.bfloat16)
    pair = exchange(term, "ed", 2, 1, False, 4)
    pair = (pair[0].astype(jnp.float32) + pair[1].astype(jnp.float32)).astype(jnp.bfloat16)
    pieces = exchange(pair, "ed", chips, 2, False, 5)
    slot_out = jnp.sum(pieces.astype(jnp.float32), axis=0)
    weights_matrix = combine_matrix(expert_ids, route_weights, window, CAP)
    mixed = jnp.dot(
        weights_matrix,
        slot_out.reshape(window * CAP, features_dev),
        precision=lax.Precision.HIGHEST,
        preferred_element_type=jnp.float32,
    )
    return mixed.astype(jnp.bfloat16)


def solution(mesh):
    return jax.shard_map(
        local,
        mesh=mesh,
        in_specs=(
            P("ed", "fsdp"),
            P("ed", None),
            P("ed", None),
            P(None, "fsdp", "ed"),
            P(None, "fsdp", "ed"),
            P(None, "ed", "fsdp"),
        ),
        out_specs=P("ed", "fsdp"),
        check_vma=False,
    )
```

```python
import functools

import jax
import jax.numpy as jnp
from jax import lax
from jax.experimental import pallas as pl
from jax.experimental.pallas import tpu as pltpu
from jax.sharding import PartitionSpec as P

CAP = 81
MESH = pl.DeviceIdType.MESH


def slot_match(routes, window, capacity):
    window_ids = jnp.arange(window, dtype=jnp.int32)
    routed = jnp.any(routes[:, :, None, :] == window_ids[None, None, :, None], axis=3)
    position = jnp.cumsum(routed.astype(jnp.int32), axis=1) - 1
    slot_ids = jnp.arange(capacity, dtype=jnp.int32)
    hits = routed[:, :, :, None] & (position[:, :, :, None] == slot_ids[None, None, None, :])
    return hits.astype(jnp.int32)


def take_block(block_rows, row_list):
    return jnp.take(block_rows, row_list, axis=0)


def pick_rows(blocks, routes, window, capacity):
    match = slot_match(routes, window, capacity)
    row_numbers = jnp.arange(blocks.shape[1], dtype=jnp.int32)
    source_row = jnp.sum(match * row_numbers[None, :, None, None], axis=1).reshape(
        blocks.shape[0], window * capacity
    )
    filled = jnp.sum(match, axis=1).reshape(blocks.shape[0], window * capacity)
    picked = jax.vmap(take_block)(blocks, source_row)
    picked = jnp.where(filled[:, :, None] > 0, picked, jnp.zeros_like(picked))
    return picked.reshape(blocks.shape[0], window, capacity, blocks.shape[2])


def combine_matrix(routes, weights, window, capacity):
    match = slot_match(routes[None], window, capacity)[0]
    window_ids = jnp.arange(window, dtype=jnp.int32)
    per_expert = jnp.sum(
        jnp.where(
            routes[:, None, :] == window_ids[None, :, None],
            weights[:, None, :],
            jnp.zeros_like(weights[:, None, :]),
        ),
        axis=2,
    )
    return (per_expert[:, :, None] * match.astype(weights.dtype)).reshape(
        routes.shape[0], window * capacity
    )


def _exchange_kernel(axis, m, stride, gather, x_ref, o_ref, send_sem, recv_sem, own_sem):
    me = lax.axis_index(axis)
    k = lax.rem(me // stride, m)
    base = me - k * stride

    def member(i):
        return lax.rem(k + 1 + i, m)

    def device(j):
        return {axis: base + j * stride}

    def source(j):
        return x_ref if gather else x_ref.at[j]

    def outgoing(j):
        return pltpu.make_async_remote_copy(
            src_ref=source(j),
            dst_ref=o_ref.at[k],
            send_sem=send_sem.at[j],
            recv_sem=recv_sem.at[k],
            device_id=device(j),
            device_id_type=MESH,
        )

    def incoming(j):
        return pltpu.make_async_remote_copy(
            src_ref=source(j),
            dst_ref=o_ref.at[j],
            send_sem=send_sem.at[j],
            recv_sem=recv_sem.at[j],
            device_id=device(j),
            device_id_type=MESH,
        )

    barrier = pltpu.get_barrier_semaphore()

    def greet(i, carry):
        pl.semaphore_signal(barrier, 1, device_id=device(member(i)), device_id_type=MESH)
        return carry

    lax.fori_loop(0, m - 1, greet, 0)
    pl.semaphore_wait(barrier, m - 1)

    def send(i, carry):
        outgoing(member(i)).start()
        return carry

    lax.fori_loop(0, m - 1, send, 0)
    own = pltpu.make_async_copy(source(k), o_ref.at[k], own_sem)
    own.start()

    def finish(i, carry):
        j = member(i)
        outgoing(j).wait_send()
        incoming(j).wait_recv()
        return carry

    lax.fori_loop(0, m - 1, finish, 0)
    own.wait()


def exchange(x, axis, m, stride, gather, cid):
    block = x.shape if gather else x.shape[1:]
    return pl.pallas_call(
        functools.partial(_exchange_kernel, axis, m, stride, gather),
        out_shape=jax.ShapeDtypeStruct((m,) + tuple(block), x.dtype),
        in_specs=[pl.BlockSpec(memory_space=pltpu.VMEM)],
        out_specs=pl.BlockSpec(memory_space=pltpu.VMEM),
        scratch_shapes=[
            pltpu.SemaphoreType.DMA((m,)),
            pltpu.SemaphoreType.DMA((m,)),
            pltpu.SemaphoreType.DMA,
        ],
        compiler_params=pltpu.CompilerParams(collective_id=cid, has_side_effects=True),
    )(x)


def local(tokens, expert_ids, route_weights, w_gate, w_up, w_down):
    window = w_gate.shape[0]
    features_dev = tokens.shape[1]
    hidden_dev = w_gate.shape[2]
    n_ed = lax.axis_size("ed")
    n_fsdp = lax.axis_size("fsdp")
    chips = n_ed // 2
    per_band = n_ed // n_fsdp
    own_slots = pick_rows(tokens[None], expert_ids[None], window, CAP)[0, 0]
    same_core = exchange(own_slots, "ed", chips, 2, True, 0)
    selected = exchange(same_core, "ed", 2, 1, True, 1)
    selected = selected.reshape(n_fsdp, per_band, CAP, features_dev)
    both = jnp.concatenate([w_gate[0], w_up[0]], axis=1)
    partial = jnp.einsum("fbri,ih->fbrh", selected, both, preferred_element_type=jnp.float32)
    arrived = exchange(partial.astype(jnp.bfloat16), "fsdp", n_fsdp, 1, False, 2)
    summed = jnp.sum(arrived.astype(jnp.float32), axis=0)
    gate_part = summed[..., :hidden_dev]
    up_part = summed[..., hidden_dev:]
    activation = (jax.nn.silu(gate_part) * up_part).astype(jnp.bfloat16)
    act_rows = exchange(activation, "fsdp", n_fsdp, 1, True, 3)
    act_rows = act_rows.reshape(2, chips, CAP, hidden_dev)
    term = jnp.einsum("cbrh,hd->cbrd", act_rows, w_down[0], preferred_element_type=jnp.float32)
    term = term.astype(jnp.bfloat16)
    pair = exchange(term, "ed", 2, 1, False, 4)
    pair = (pair[0].astype(jnp.float32) + pair[1].astype(jnp.float32)).astype(jnp.bfloat16)
    pieces = exchange(pair, "ed", chips, 2, False, 5)
    slot_out = jnp.sum(pieces.astype(jnp.float32), axis=0)
    weights_matrix = combine_matrix(expert_ids, route_weights, window, CAP)
    mixed = jnp.dot(
        weights_matrix,
        slot_out.reshape(window * CAP, features_dev),
        precision=lax.Precision.HIGHEST,
        preferred_element_type=jnp.float32,
    )
    return mixed.astype(jnp.bfloat16)


def solution(mesh):
    return jax.shard_map(
        local,
        mesh=mesh,
        in_specs=(
            P("ed", "fsdp"),
            P("ed", None),
            P("ed", None),
            P(None, "fsdp", "ed"),
            P(None, "fsdp", "ed"),
            P(None, "ed", "fsdp"),
        ),
        out_specs=P("ed", "fsdp"),
        check_vma=False,
    )
```

```python
import functools

import jax
import jax.numpy as jnp
from jax import lax
from jax.experimental import pallas as pl
from jax.experimental.pallas import tpu as pltpu
from jax.sharding import PartitionSpec as P

CAP = 81
MESH = pl.DeviceIdType.MESH


def slot_match(routes, window, capacity):
    window_ids = jnp.arange(window, dtype=jnp.int32)
    routed = jnp.any(routes[:, :, None, :] == window_ids[None, None, :, None], axis=3)
    position = jnp.cumsum(routed.astype(jnp.int32), axis=1) - 1
    slot_ids = jnp.arange(capacity, dtype=jnp.int32)
    hits = routed[:, :, :, None] & (position[:, :, :, None] == slot_ids[None, None, None, :])
    return hits.astype(jnp.int32)


def take_block(block_rows, row_list):
    return jnp.take(block_rows, row_list, axis=0)


def pick_rows(blocks, routes, window, capacity):
    match = slot_match(routes, window, capacity)
    row_numbers = jnp.arange(blocks.shape[1], dtype=jnp.int32)
    source_row = jnp.sum(match * row_numbers[None, :, None, None], axis=1).reshape(
        blocks.shape[0], window * capacity
    )
    filled = jnp.sum(match, axis=1).reshape(blocks.shape[0], window * capacity)
    picked = jax.vmap(take_block)(blocks, source_row)
    picked = jnp.where(filled[:, :, None] > 0, picked, jnp.zeros_like(picked))
    return picked.reshape(blocks.shape[0], window, capacity, blocks.shape[2])


def combine_matrix(routes, weights, window, capacity):
    match = slot_match(routes[None], window, capacity)[0]
    window_ids = jnp.arange(window, dtype=jnp.int32)
    per_expert = jnp.sum(
        jnp.where(
            routes[:, None, :] == window_ids[None, :, None],
            weights[:, None, :],
            jnp.zeros_like(weights[:, None, :]),
        ),
        axis=2,
    )
    return (per_expert[:, :, None] * match.astype(weights.dtype)).reshape(
        routes.shape[0], window * capacity
    )


def _exchange_kernel(axis, m, stride, gather, x_ref, o_ref, send_sem, recv_sem, own_sem):
    me = lax.axis_index(axis)
    k = lax.rem(me // stride, m)
    base = me - k * stride

    def member(i):
        return lax.rem(k + 1 + i, m)

    def device(j):
        return {axis: base + j * stride}

    def source(j):
        return x_ref if gather else x_ref.at[j]

    def outgoing(j):
        return pltpu.make_async_remote_copy(
            src_ref=source(j),
            dst_ref=o_ref.at[k],
            send_sem=send_sem.at[j],
            recv_sem=recv_sem.at[k],
            device_id=device(j),
            device_id_type=MESH,
        )

    def incoming(j):
        return pltpu.make_async_remote_copy(
            src_ref=source(j),
            dst_ref=o_ref.at[j],
            send_sem=send_sem.at[j],
            recv_sem=recv_sem.at[j],
            device_id=device(j),
            device_id_type=MESH,
        )

    barrier = pltpu.get_barrier_semaphore()

    def greet(i, carry):
        pl.semaphore_signal(barrier, 1, device_id=device(member(i)), device_id_type=MESH)
        return carry

    lax.fori_loop(0, m - 1, greet, 0)
    pl.semaphore_wait(barrier, m - 1)

    def send(i, carry):
        outgoing(member(i)).start()
        return carry

    lax.fori_loop(0, m - 1, send, 0)
    own = pltpu.make_async_copy(source(k), o_ref.at[k], own_sem)
    own.start()

    def finish(i, carry):
        j = member(i)
        outgoing(j).wait_send()
        incoming(j).wait_recv()
        return carry

    lax.fori_loop(0, m - 1, finish, 0)
    own.wait()


def exchange(x, axis, m, stride, gather, cid):
    block = x.shape if gather else x.shape[1:]
    return pl.pallas_call(
        functools.partial(_exchange_kernel, axis, m, stride, gather),
        out_shape=jax.ShapeDtypeStruct((m,) + tuple(block), x.dtype),
        in_specs=[pl.BlockSpec(memory_space=pltpu.VMEM)],
        out_specs=pl.BlockSpec(memory_space=pltpu.VMEM),
        scratch_shapes=[
            pltpu.SemaphoreType.DMA((m,)),
            pltpu.SemaphoreType.DMA((m,)),
            pltpu.SemaphoreType.DMA,
        ],
        compiler_params=pltpu.CompilerParams(collective_id=cid, has_side_effects=True),
    )(x)


def local(tokens, expert_ids, route_weights, w_gate, w_up, w_down):
    window = w_gate.shape[0]
    features_dev = tokens.shape[1]
    hidden_dev = w_gate.shape[2]
    n_ed = lax.axis_size("ed")
    n_fsdp = lax.axis_size("fsdp")
    chips = n_ed // 2
    per_band = n_ed // n_fsdp
    own_slots = pick_rows(tokens[None], expert_ids[None], window, CAP)[0, 0]
    same_core = exchange(own_slots, "ed", chips, 2, True, 0)
    selected = exchange(same_core, "ed", 2, 1, True, 1)
    pairs = 2
    rings = n_fsdp // pairs
    selected = selected.reshape(pairs, rings, per_band, CAP, features_dev)
    both = jnp.concatenate([w_gate[0], w_up[0]], axis=1)
    partial = jnp.einsum("xybri,ih->xybrh", selected, both, preferred_element_type=jnp.float32)
    half = exchange(partial.astype(jnp.bfloat16), "fsdp", pairs, 1, False, 2)
    half = (half[0].astype(jnp.float32) + half[1].astype(jnp.float32)).astype(jnp.bfloat16)
    arrived = exchange(half, "fsdp", rings, pairs, False, 3)
    summed = jnp.sum(arrived.astype(jnp.float32), axis=0)
    gate_part = summed[..., :hidden_dev]
    up_part = summed[..., hidden_dev:]
    activation = (jax.nn.silu(gate_part) * up_part).astype(jnp.bfloat16)
    act_ring = exchange(activation, "fsdp", rings, pairs, True, 4)
    act_rows = exchange(act_ring, "fsdp", pairs, 1, True, 5)
    act_rows = act_rows.reshape(2, chips, CAP, hidden_dev)
    term = jnp.einsum("cbrh,hd->cbrd", act_rows, w_down[0], preferred_element_type=jnp.float32)
    term = term.astype(jnp.bfloat16)
    pair = exchange(term, "ed", 2, 1, False, 6)
    pair = (pair[0].astype(jnp.float32) + pair[1].astype(jnp.float32)).astype(jnp.bfloat16)
    pieces = exchange(pair, "ed", chips, 2, False, 7)
    slot_out = jnp.sum(pieces.astype(jnp.float32), axis=0)
    weights_matrix = combine_matrix(expert_ids, route_weights, window, CAP)
    mixed = jnp.dot(
        weights_matrix,
        slot_out.reshape(window * CAP, features_dev),
        precision=lax.Precision.HIGHEST,
        preferred_element_type=jnp.float32,
    )
    return mixed.astype(jnp.bfloat16)


def solution(mesh):
    return jax.shard_map(
        local,
        mesh=mesh,
        in_specs=(
            P("ed", "fsdp"),
            P("ed", None),
            P("ed", None),
            P(None, "fsdp", "ed"),
            P(None, "fsdp", "ed"),
            P(None, "ed", "fsdp"),
        ),
        out_specs=P("ed", "fsdp"),
        check_vma=False,
    )
```

```python
import functools

import jax
import jax.numpy as jnp
from jax import lax
from jax.experimental import pallas as pl
from jax.experimental.pallas import tpu as pltpu
from jax.sharding import PartitionSpec as P

CAP = 81
MESH = pl.DeviceIdType.MESH


def slot_match(routes, window, capacity):
    window_ids = jnp.arange(window, dtype=jnp.int32)
    routed = jnp.any(routes[:, :, None, :] == window_ids[None, None, :, None], axis=3)
    position = jnp.cumsum(routed.astype(jnp.int32), axis=1) - 1
    slot_ids = jnp.arange(capacity, dtype=jnp.int32)
    hits = routed[:, :, :, None] & (position[:, :, :, None] == slot_ids[None, None, None, :])
    return hits.astype(jnp.int32)


def take_block(block_rows, row_list):
    return jnp.take(block_rows, row_list, axis=0)


def pick_rows(blocks, routes, window, capacity):
    match = slot_match(routes, window, capacity)
    row_numbers = jnp.arange(blocks.shape[1], dtype=jnp.int32)
    source_row = jnp.sum(match * row_numbers[None, :, None, None], axis=1).reshape(
        blocks.shape[0], window * capacity
    )
    filled = jnp.sum(match, axis=1).reshape(blocks.shape[0], window * capacity)
    picked = jax.vmap(take_block)(blocks, source_row)
    picked = jnp.where(filled[:, :, None] > 0, picked, jnp.zeros_like(picked))
    return picked.reshape(blocks.shape[0], window, capacity, blocks.shape[2])


def combine_matrix(routes, weights, window, capacity):
    match = slot_match(routes[None], window, capacity)[0]
    window_ids = jnp.arange(window, dtype=jnp.int32)
    per_expert = jnp.sum(
        jnp.where(
            routes[:, None, :] == window_ids[None, :, None],
            weights[:, None, :],
            jnp.zeros_like(weights[:, None, :]),
        ),
        axis=2,
    )
    return (per_expert[:, :, None] * match.astype(weights.dtype)).reshape(
        routes.shape[0], window * capacity
    )


def _exchange_kernel(axis, m, stride, gather, x_ref, o_ref, send_sem, recv_sem, own_sem):
    me = lax.axis_index(axis)
    k = lax.rem(me // stride, m)
    base = me - k * stride

    def member(i):
        return lax.rem(k + 1 + i, m)

    def device(j):
        return {axis: base + j * stride}

    def source(j):
        return x_ref if gather else x_ref.at[j]

    def outgoing(j):
        return pltpu.make_async_remote_copy(
            src_ref=source(j),
            dst_ref=o_ref.at[k],
            send_sem=send_sem.at[j],
            recv_sem=recv_sem.at[k],
            device_id=device(j),
            device_id_type=MESH,
        )

    def incoming(j):
        return pltpu.make_async_remote_copy(
            src_ref=source(j),
            dst_ref=o_ref.at[j],
            send_sem=send_sem.at[j],
            recv_sem=recv_sem.at[j],
            device_id=device(j),
            device_id_type=MESH,
        )

    barrier = pltpu.get_barrier_semaphore()

    def greet(i, carry):
        pl.semaphore_signal(barrier, 1, device_id=device(member(i)), device_id_type=MESH)
        return carry

    lax.fori_loop(0, m - 1, greet, 0)
    pl.semaphore_wait(barrier, m - 1)

    def send(i, carry):
        outgoing(member(i)).start()
        return carry

    lax.fori_loop(0, m - 1, send, 0)
    own = pltpu.make_async_copy(source(k), o_ref.at[k], own_sem)
    own.start()

    def finish(i, carry):
        j = member(i)
        outgoing(j).wait_send()
        incoming(j).wait_recv()
        return carry

    lax.fori_loop(0, m - 1, finish, 0)
    own.wait()


def exchange(x, axis, m, stride, gather, cid):
    block = x.shape if gather else x.shape[1:]
    return pl.pallas_call(
        functools.partial(_exchange_kernel, axis, m, stride, gather),
        out_shape=jax.ShapeDtypeStruct((m,) + tuple(block), x.dtype),
        in_specs=[pl.BlockSpec(memory_space=pltpu.VMEM)],
        out_specs=pl.BlockSpec(memory_space=pltpu.VMEM),
        scratch_shapes=[
            pltpu.SemaphoreType.DMA((m,)),
            pltpu.SemaphoreType.DMA((m,)),
            pltpu.SemaphoreType.DMA,
        ],
        compiler_params=pltpu.CompilerParams(collective_id=cid, has_side_effects=True),
    )(x)


def local(tokens, expert_ids, route_weights, w_gate, w_up, w_down):
    window = w_gate.shape[0]
    features_dev = tokens.shape[1]
    hidden_dev = w_gate.shape[2]
    n_ed = lax.axis_size("ed")
    n_fsdp = lax.axis_size("fsdp")
    chips = n_ed // 2
    per_band = n_ed // n_fsdp
    own_slots = pick_rows(tokens[None], expert_ids[None], window, CAP)[0, 0]
    same_core = exchange(own_slots, "ed", chips, 2, True, 0)
    selected = exchange(same_core, "ed", 2, 1, True, 1)
    selected = selected.reshape(n_fsdp, per_band, CAP, features_dev)
    both = jnp.concatenate([w_gate[0], w_up[0]], axis=1)
    partial = jnp.einsum("fbri,ih->fbrh", selected, both, preferred_element_type=jnp.float32)
    arrived = exchange(partial[..., :hidden_dev].astype(jnp.bfloat16), "fsdp", n_fsdp, 1, False, 2)
    gate_part = jnp.sum(arrived.astype(jnp.float32), axis=0)
    up_sum = lax.psum_scatter(partial[..., hidden_dev:].astype(jnp.bfloat16), "fsdp", scatter_dimension=0, tiled=True)
    up_part = up_sum[0].astype(jnp.float32)
    activation = (jax.nn.silu(gate_part) * up_part).astype(jnp.bfloat16)
    act_rows = exchange(activation, "fsdp", n_fsdp, 1, True, 3)
    act_rows = act_rows.reshape(2, chips, CAP, hidden_dev)
    term = jnp.einsum("cbrh,hd->cbrd", act_rows, w_down[0], preferred_element_type=jnp.float32)
    term = term.astype(jnp.bfloat16)
    pair = exchange(term, "ed", 2, 1, False, 4)
    pair = (pair[0].astype(jnp.float32) + pair[1].astype(jnp.float32)).astype(jnp.bfloat16)
    pieces = exchange(pair, "ed", chips, 2, False, 5)
    slot_out = jnp.sum(pieces.astype(jnp.float32), axis=0)
    weights_matrix = combine_matrix(expert_ids, route_weights, window, CAP)
    mixed = jnp.dot(
        weights_matrix,
        slot_out.reshape(window * CAP, features_dev),
        precision=lax.Precision.HIGHEST,
        preferred_element_type=jnp.float32,
    )
    return mixed.astype(jnp.bfloat16)


def solution(mesh):
    return jax.shard_map(
        local,
        mesh=mesh,
        in_specs=(
            P("ed", "fsdp"),
            P("ed", None),
            P("ed", None),
            P(None, "fsdp", "ed"),
            P(None, "fsdp", "ed"),
            P(None, "ed", "fsdp"),
        ),
        out_specs=P("ed", "fsdp"),
        check_vma=False,
    )
```

```python
import functools

import jax
import jax.numpy as jnp
from jax import lax
from jax.experimental import pallas as pl
from jax.experimental.pallas import tpu as pltpu
from jax.sharding import PartitionSpec as P

CAP = 81
MESH = pl.DeviceIdType.MESH


def slot_match(routes, window, capacity):
    window_ids = jnp.arange(window, dtype=jnp.int32)
    routed = jnp.any(routes[:, :, None, :] == window_ids[None, None, :, None], axis=3)
    position = jnp.cumsum(routed.astype(jnp.int32), axis=1) - 1
    slot_ids = jnp.arange(capacity, dtype=jnp.int32)
    hits = routed[:, :, :, None] & (position[:, :, :, None] == slot_ids[None, None, None, :])
    return hits.astype(jnp.int32)


def take_block(block_rows, row_list):
    return jnp.take(block_rows, row_list, axis=0)


def pick_rows(blocks, routes, window, capacity):
    match = slot_match(routes, window, capacity)
    row_numbers = jnp.arange(blocks.shape[1], dtype=jnp.int32)
    source_row = jnp.sum(match * row_numbers[None, :, None, None], axis=1).reshape(
        blocks.shape[0], window * capacity
    )
    filled = jnp.sum(match, axis=1).reshape(blocks.shape[0], window * capacity)
    picked = jax.vmap(take_block)(blocks, source_row)
    picked = jnp.where(filled[:, :, None] > 0, picked, jnp.zeros_like(picked))
    return picked.reshape(blocks.shape[0], window, capacity, blocks.shape[2])


def combine_matrix(routes, weights, window, capacity):
    match = slot_match(routes[None], window, capacity)[0]
    window_ids = jnp.arange(window, dtype=jnp.int32)
    per_expert = jnp.sum(
        jnp.where(
            routes[:, None, :] == window_ids[None, :, None],
            weights[:, None, :],
            jnp.zeros_like(weights[:, None, :]),
        ),
        axis=2,
    )
    return (per_expert[:, :, None] * match.astype(weights.dtype)).reshape(
        routes.shape[0], window * capacity
    )


def _exchange_kernel(axis, m, stride, gather, x_ref, o_ref, send_sem, recv_sem, own_sem):
    me = lax.axis_index(axis)
    k = lax.rem(me // stride, m)
    base = me - k * stride

    def member(i):
        return lax.rem(k + 1 + i, m)

    def device(j):
        return {axis: base + j * stride}

    def source(j):
        return x_ref if gather else x_ref.at[j]

    def outgoing(j):
        return pltpu.make_async_remote_copy(
            src_ref=source(j),
            dst_ref=o_ref.at[k],
            send_sem=send_sem.at[j],
            recv_sem=recv_sem.at[k],
            device_id=device(j),
            device_id_type=MESH,
        )

    def incoming(j):
        return pltpu.make_async_remote_copy(
            src_ref=source(j),
            dst_ref=o_ref.at[j],
            send_sem=send_sem.at[j],
            recv_sem=recv_sem.at[j],
            device_id=device(j),
            device_id_type=MESH,
        )

    barrier = pltpu.get_barrier_semaphore()

    def greet(i, carry):
        pl.semaphore_signal(barrier, 1, device_id=device(member(i)), device_id_type=MESH)
        return carry

    lax.fori_loop(0, m - 1, greet, 0)
    pl.semaphore_wait(barrier, m - 1)

    def send(i, carry):
        outgoing(member(i)).start()
        return carry

    lax.fori_loop(0, m - 1, send, 0)
    own = pltpu.make_async_copy(source(k), o_ref.at[k], own_sem)
    own.start()

    def finish(i, carry):
        j = member(i)
        outgoing(j).wait_send()
        incoming(j).wait_recv()
        return carry

    lax.fori_loop(0, m - 1, finish, 0)
    own.wait()


def exchange(x, axis, m, stride, gather, cid):
    block = x.shape if gather else x.shape[1:]
    return pl.pallas_call(
        functools.partial(_exchange_kernel, axis, m, stride, gather),
        out_shape=jax.ShapeDtypeStruct((m,) + tuple(block), x.dtype),
        in_specs=[pl.BlockSpec(memory_space=pltpu.VMEM)],
        out_specs=pl.BlockSpec(memory_space=pltpu.VMEM),
        scratch_shapes=[
            pltpu.SemaphoreType.DMA((m,)),
            pltpu.SemaphoreType.DMA((m,)),
            pltpu.SemaphoreType.DMA,
        ],
        compiler_params=pltpu.CompilerParams(collective_id=cid, has_side_effects=True),
    )(x)


def _gate_kernel(axis, m, hidden, sel_ref, w_ref, o_ref, out_buf, in_buf, acc, send_sem, recv_sem):
    me = lax.axis_index(axis)
    bands = sel_ref.shape[1]

    def member(i):
        return lax.rem(me + 1 + i, m)

    def copy(j, slot):
        return pltpu.make_async_remote_copy(
            src_ref=out_buf.at[j],
            dst_ref=in_buf.at[slot],
            send_sem=send_sem.at[j],
            recv_sem=recv_sem.at[slot],
            device_id={axis: j},
            device_id_type=MESH,
        )

    def partial(j, b):
        return jnp.dot(sel_ref[j, b], w_ref[...], preferred_element_type=jnp.float32)

    barrier = pltpu.get_barrier_semaphore()

    def greet(i, carry):
        pl.semaphore_signal(barrier, 1, device_id={axis: member(i)}, device_id_type=MESH)
        return carry

    lax.fori_loop(0, m - 1, greet, 0)
    pl.semaphore_wait(barrier, m - 1)

    def send(i, carry):
        j = member(i)
        for b in range(bands):
            out_buf[j, b] = partial(j, b).astype(out_buf.dtype)
        copy(j, me).start()
        return carry

    lax.fori_loop(0, m - 1, send, 0)
    for b in range(bands):
        acc[b] = partial(me, b)

    def gather(i, carry):
        j = member(i)
        copy(j, me).wait_send()
        copy(j, j).wait_recv()
        acc[...] += in_buf[j].astype(jnp.float32)
        return carry

    lax.fori_loop(0, m - 1, gather, 0)
    total = acc[...]
    gate = total[..., :hidden]
    up = total[..., hidden:]
    o_ref[...] = (jax.nn.silu(gate) * up).astype(o_ref.dtype)


def gate_act(sel, w, axis, m, cid):
    _, bands, rows, _ = sel.shape
    hidden = w.shape[1] // 2
    return pl.pallas_call(
        functools.partial(_gate_kernel, axis, m, hidden),
        out_shape=jax.ShapeDtypeStruct((bands, rows, hidden), jnp.bfloat16),
        in_specs=[pl.BlockSpec(memory_space=pltpu.VMEM)] * 2,
        out_specs=pl.BlockSpec(memory_space=pltpu.VMEM),
        scratch_shapes=[
            pltpu.VMEM((m, bands, rows, 2 * hidden), jnp.bfloat16),
            pltpu.VMEM((m, bands, rows, 2 * hidden), jnp.bfloat16),
            pltpu.VMEM((bands, rows, 2 * hidden), jnp.float32),
            pltpu.SemaphoreType.DMA((m,)),
            pltpu.SemaphoreType.DMA((m,)),
        ],
        compiler_params=pltpu.CompilerParams(collective_id=cid, has_side_effects=True),
    )(sel, w)


def local(tokens, expert_ids, route_weights, w_gate, w_up, w_down):
    window = w_gate.shape[0]
    features_dev = tokens.shape[1]
    hidden_dev = w_gate.shape[2]
    n_ed = lax.axis_size("ed")
    n_fsdp = lax.axis_size("fsdp")
    chips = n_ed // 2
    per_band = n_ed // n_fsdp
    own_slots = pick_rows(tokens[None], expert_ids[None], window, CAP)[0, 0]
    same_core = exchange(own_slots, "ed", chips, 2, True, 0)
    selected = exchange(same_core, "ed", 2, 1, True, 1)
    selected = selected.reshape(n_fsdp, per_band, CAP, features_dev)
    both = jnp.concatenate([w_gate[0], w_up[0]], axis=1)
    activation = gate_act(selected, both, "fsdp", n_fsdp, 2)
    act_rows = exchange(activation, "fsdp", n_fsdp, 1, True, 3)
    act_rows = act_rows.reshape(2, chips, CAP, hidden_dev)
    term = jnp.einsum("cbrh,hd->cbrd", act_rows, w_down[0], preferred_element_type=jnp.float32)
    term = term.astype(jnp.bfloat16)
    pair = exchange(term, "ed", 2, 1, False, 4)
    pair = (pair[0].astype(jnp.float32) + pair[1].astype(jnp.float32)).astype(jnp.bfloat16)
    pieces = exchange(pair, "ed", chips, 2, False, 5)
    slot_out = jnp.sum(pieces.astype(jnp.float32), axis=0)
    weights_matrix = combine_matrix(expert_ids, route_weights, window, CAP)
    mixed = jnp.dot(
        weights_matrix,
        slot_out.reshape(window * CAP, features_dev),
        precision=lax.Precision.HIGHEST,
        preferred_element_type=jnp.float32,
    )
    return mixed.astype(jnp.bfloat16)


def solution(mesh):
    return jax.shard_map(
        local,
        mesh=mesh,
        in_specs=(
            P("ed", "fsdp"),
            P("ed", None),
            P("ed", None),
            P(None, "fsdp", "ed"),
            P(None, "fsdp", "ed"),
            P(None, "ed", "fsdp"),
        ),
        out_specs=P("ed", "fsdp"),
        check_vma=False,
    )
```

```python
import functools

import jax
import jax.numpy as jnp
from jax import lax
from jax.experimental import pallas as pl
from jax.experimental.pallas import tpu as pltpu
from jax.sharding import PartitionSpec as P

CAP = 81
MESH = pl.DeviceIdType.MESH


def slot_match(routes, window, capacity):
    window_ids = jnp.arange(window, dtype=jnp.int32)
    routed = jnp.any(routes[:, :, None, :] == window_ids[None, None, :, None], axis=3)
    position = jnp.cumsum(routed.astype(jnp.int32), axis=1) - 1
    slot_ids = jnp.arange(capacity, dtype=jnp.int32)
    hits = routed[:, :, :, None] & (position[:, :, :, None] == slot_ids[None, None, None, :])
    return hits.astype(jnp.int32)


def take_block(block_rows, row_list):
    return jnp.take(block_rows, row_list, axis=0)


def pick_rows(blocks, routes, window, capacity):
    match = slot_match(routes, window, capacity)
    row_numbers = jnp.arange(blocks.shape[1], dtype=jnp.int32)
    source_row = jnp.sum(match * row_numbers[None, :, None, None], axis=1).reshape(
        blocks.shape[0], window * capacity
    )
    filled = jnp.sum(match, axis=1).reshape(blocks.shape[0], window * capacity)
    picked = jax.vmap(take_block)(blocks, source_row)
    picked = jnp.where(filled[:, :, None] > 0, picked, jnp.zeros_like(picked))
    return picked.reshape(blocks.shape[0], window, capacity, blocks.shape[2])


def combine_matrix(routes, weights, window, capacity):
    match = slot_match(routes[None], window, capacity)[0]
    window_ids = jnp.arange(window, dtype=jnp.int32)
    per_expert = jnp.sum(
        jnp.where(
            routes[:, None, :] == window_ids[None, :, None],
            weights[:, None, :],
            jnp.zeros_like(weights[:, None, :]),
        ),
        axis=2,
    )
    return (per_expert[:, :, None] * match.astype(weights.dtype)).reshape(
        routes.shape[0], window * capacity
    )


def _exchange_kernel(axis, m, stride, gather, x_ref, o_ref, send_sem, recv_sem, own_sem):
    me = lax.axis_index(axis)
    k = lax.rem(me // stride, m)
    base = me - k * stride

    def member(i):
        return lax.rem(k + 1 + i, m)

    def device(j):
        return {axis: base + j * stride}

    def source(j):
        return x_ref if gather else x_ref.at[j]

    def outgoing(j):
        return pltpu.make_async_remote_copy(
            src_ref=source(j),
            dst_ref=o_ref.at[k],
            send_sem=send_sem.at[j],
            recv_sem=recv_sem.at[k],
            device_id=device(j),
            device_id_type=MESH,
        )

    def incoming(j):
        return pltpu.make_async_remote_copy(
            src_ref=source(j),
            dst_ref=o_ref.at[j],
            send_sem=send_sem.at[j],
            recv_sem=recv_sem.at[j],
            device_id=device(j),
            device_id_type=MESH,
        )

    barrier = pltpu.get_barrier_semaphore()

    def greet(i, carry):
        pl.semaphore_signal(barrier, 1, device_id=device(member(i)), device_id_type=MESH)
        return carry

    lax.fori_loop(0, m - 1, greet, 0)
    pl.semaphore_wait(barrier, m - 1)

    def send(i, carry):
        outgoing(member(i)).start()
        return carry

    lax.fori_loop(0, m - 1, send, 0)
    own = pltpu.make_async_copy(source(k), o_ref.at[k], own_sem)
    own.start()

    def finish(i, carry):
        j = member(i)
        outgoing(j).wait_send()
        incoming(j).wait_recv()
        return carry

    lax.fori_loop(0, m - 1, finish, 0)
    own.wait()


def exchange(x, axis, m, stride, gather, cid):
    block = x.shape if gather else x.shape[1:]
    return pl.pallas_call(
        functools.partial(_exchange_kernel, axis, m, stride, gather),
        out_shape=jax.ShapeDtypeStruct((m,) + tuple(block), x.dtype),
        in_specs=[pl.BlockSpec(memory_space=pltpu.VMEM)],
        out_specs=pl.BlockSpec(memory_space=pltpu.VMEM),
        scratch_shapes=[
            pltpu.SemaphoreType.DMA((m,)),
            pltpu.SemaphoreType.DMA((m,)),
            pltpu.SemaphoreType.DMA,
        ],
        compiler_params=pltpu.CompilerParams(collective_id=cid, has_side_effects=True),
    )(x)


def _gate_kernel(axis, m, hidden, sel_ref, w_ref, o_ref, out_buf, in_buf, acc, send_sem, recv_sem):
    me = lax.axis_index(axis)
    bands = sel_ref.shape[1]

    def member(i):
        return lax.rem(me + 1 + i, m)

    def copy(j, slot):
        return pltpu.make_async_remote_copy(
            src_ref=out_buf.at[j],
            dst_ref=in_buf.at[slot],
            send_sem=send_sem.at[j],
            recv_sem=recv_sem.at[slot],
            device_id={axis: j},
            device_id_type=MESH,
        )

    def partial(j, b):
        return jnp.dot(sel_ref[j, b], w_ref[...], preferred_element_type=jnp.float32)

    barrier = pltpu.get_barrier_semaphore()

    def greet(i, carry):
        pl.semaphore_signal(barrier, 1, device_id={axis: member(i)}, device_id_type=MESH)
        return carry

    lax.fori_loop(0, m - 1, greet, 0)
    pl.semaphore_wait(barrier, m - 1)

    def send(i, carry):
        j = member(i)
        for b in range(bands):
            out_buf[j, b] = partial(j, b).astype(out_buf.dtype)
        copy(j, me).start()
        return carry

    lax.fori_loop(0, m - 1, send, 0)
    for b in range(bands):
        acc[b] = partial(me, b)

    def gather(i, carry):
        j = member(i)
        copy(j, me).wait_send()
        copy(j, j).wait_recv()
        acc[...] += in_buf[j].astype(jnp.float32)
        return carry

    lax.fori_loop(0, m - 1, gather, 0)
    total = acc[...]
    gate = total[..., :hidden]
    up = total[..., hidden:]
    o_ref[...] = (jax.nn.silu(gate) * up).astype(o_ref.dtype)


def gate_act(sel, w, axis, m, cid):
    _, bands, rows, _ = sel.shape
    hidden = w.shape[1] // 2
    return pl.pallas_call(
        functools.partial(_gate_kernel, axis, m, hidden),
        out_shape=jax.ShapeDtypeStruct((bands, rows, hidden), jnp.bfloat16),
        in_specs=[pl.BlockSpec(memory_space=pltpu.VMEM)] * 2,
        out_specs=pl.BlockSpec(memory_space=pltpu.VMEM),
        scratch_shapes=[
            pltpu.VMEM((m, bands, rows, 2 * hidden), jnp.bfloat16),
            pltpu.VMEM((m, bands, rows, 2 * hidden), jnp.bfloat16),
            pltpu.VMEM((bands, rows, 2 * hidden), jnp.float32),
            pltpu.SemaphoreType.DMA((m,)),
            pltpu.SemaphoreType.DMA((m,)),
        ],
        compiler_params=pltpu.CompilerParams(collective_id=cid, has_side_effects=True),
    )(sel, w)


def _down_kernel(nf, chips, act_ref, wd_ref, o_ref, act_buf, term_buf, sib_buf, pre_buf, in_buf,
                 a_send, a_recv, s_send, s_recv, e_send, e_recv):
    bands = act_ref.shape[0]
    f = lax.axis_index("fsdp")
    e = lax.axis_index("ed")
    core = lax.rem(e, 2)
    chip = e // 2
    sib = e + 1 - 2 * core

    def fsdp_peer(i):
        return lax.rem(f + 1 + i, nf)

    def chip_peer(i):
        return lax.rem(chip + 1 + i, chips)

    def act_copy(g, slot):
        return pltpu.make_async_remote_copy(
            src_ref=act_ref,
            dst_ref=act_buf.at[slot],
            send_sem=a_send.at[g],
            recv_sem=a_recv.at[slot],
            device_id={"fsdp": g},
            device_id_type=MESH,
        )

    def piece_copy(h, slot):
        return pltpu.make_async_remote_copy(
            src_ref=pre_buf.at[h],
            dst_ref=in_buf.at[slot],
            send_sem=e_send.at[h],
            recv_sem=e_recv.at[slot],
            device_id={"ed": h * 2 + core},
            device_id_type=MESH,
        )

    barrier = pltpu.get_barrier_semaphore()

    def greet_fsdp(i, carry):
        pl.semaphore_signal(barrier, 1, device_id={"fsdp": fsdp_peer(i)}, device_id_type=MESH)
        return carry

    def greet_ed(i, carry):
        pl.semaphore_signal(barrier, 1, device_id={"ed": chip_peer(i) * 2 + core}, device_id_type=MESH)
        return carry

    lax.fori_loop(0, nf - 1, greet_fsdp, 0)
    lax.fori_loop(0, chips - 1, greet_ed, 0)
    pl.semaphore_signal(barrier, 1, device_id={"ed": sib}, device_id_type=MESH)
    pl.semaphore_wait(barrier, nf - 1 + chips)

    def send_act(i, carry):
        act_copy(fsdp_peer(i), f).start()
        return carry

    lax.fori_loop(0, nf - 1, send_act, 0)
    for b in range(bands):
        term_buf[f * bands + b] = jnp.dot(
            act_ref[b], wd_ref[...], preferred_element_type=jnp.float32
        ).astype(term_buf.dtype)

    def take_act(i, carry):
        g = fsdp_peer(i)
        act_copy(g, f).wait_send()
        act_copy(g, g).wait_recv()
        for b in range(bands):
            term_buf[g * bands + b] = jnp.dot(
                act_buf[g, b], wd_ref[...], preferred_element_type=jnp.float32
            ).astype(term_buf.dtype)
        return carry

    lax.fori_loop(0, nf - 1, take_act, 0)

    pair = pltpu.make_async_remote_copy(
        src_ref=term_buf.at[pl.ds((1 - core) * chips, chips)],
        dst_ref=sib_buf,
        send_sem=s_send,
        recv_sem=s_recv,
        device_id={"ed": sib},
        device_id_type=MESH,
    )
    pair.start()
    pair.wait_send()
    pair.wait_recv()
    mine = term_buf[pl.ds(core * chips, chips)].astype(jnp.float32)
    pre_buf[...] = (mine + sib_buf[...].astype(jnp.float32)).astype(pre_buf.dtype)

    def send_piece(i, carry):
        piece_copy(chip_peer(i), chip).start()
        return carry

    lax.fori_loop(0, chips - 1, send_piece, 0)
    o_ref[...] = pre_buf[chip].astype(jnp.float32)

    def take_piece(i, carry):
        h = chip_peer(i)
        piece_copy(h, chip).wait_send()
        piece_copy(h, h).wait_recv()
        o_ref[...] += in_buf[h].astype(jnp.float32)
        return carry

    lax.fori_loop(0, chips - 1, take_piece, 0)


def down_terms(act, wd, nf, chips, cid):
    bands, rows, hidden = act.shape
    d = wd.shape[1]
    blocks = nf * bands
    return pl.pallas_call(
        functools.partial(_down_kernel, nf, chips),
        out_shape=jax.ShapeDtypeStruct((rows, d), jnp.float32),
        in_specs=[pl.BlockSpec(memory_space=pltpu.VMEM)] * 2,
        out_specs=pl.BlockSpec(memory_space=pltpu.VMEM),
        scratch_shapes=[
            pltpu.VMEM((nf, bands, rows, hidden), jnp.bfloat16),
            pltpu.VMEM((blocks, rows, d), jnp.bfloat16),
            pltpu.VMEM((chips, rows, d), jnp.bfloat16),
            pltpu.VMEM((chips, rows, d), jnp.bfloat16),
            pltpu.VMEM((chips, rows, d), jnp.bfloat16),
            pltpu.SemaphoreType.DMA((nf,)),
            pltpu.SemaphoreType.DMA((nf,)),
            pltpu.SemaphoreType.DMA,
            pltpu.SemaphoreType.DMA,
            pltpu.SemaphoreType.DMA((chips,)),
            pltpu.SemaphoreType.DMA((chips,)),
        ],
        compiler_params=pltpu.CompilerParams(collective_id=cid, has_side_effects=True),
    )(act, wd)


def local(tokens, expert_ids, route_weights, w_gate, w_up, w_down):
    window = w_gate.shape[0]
    features_dev = tokens.shape[1]
    hidden_dev = w_gate.shape[2]
    n_ed = lax.axis_size("ed")
    n_fsdp = lax.axis_size("fsdp")
    chips = n_ed // 2
    per_band = n_ed // n_fsdp
    own_slots = pick_rows(tokens[None], expert_ids[None], window, CAP)[0, 0]
    same_core = exchange(own_slots, "ed", chips, 2, True, 0)
    selected = exchange(same_core, "ed", 2, 1, True, 1)
    selected = selected.reshape(n_fsdp, per_band, CAP, features_dev)
    both = jnp.concatenate([w_gate[0], w_up[0]], axis=1)
    activation = gate_act(selected, both, "fsdp", n_fsdp, 2)
    slot_out = down_terms(activation, w_down[0], n_fsdp, chips, 3)
    weights_matrix = combine_matrix(expert_ids, route_weights, window, CAP)
    mixed = jnp.dot(
        weights_matrix,
        slot_out.reshape(window * CAP, features_dev),
        precision=lax.Precision.HIGHEST,
        preferred_element_type=jnp.float32,
    )
    return mixed.astype(jnp.bfloat16)


def solution(mesh):
    return jax.shard_map(
        local,
        mesh=mesh,
        in_specs=(
            P("ed", "fsdp"),
            P("ed", None),
            P("ed", None),
            P(None, "fsdp", "ed"),
            P(None, "fsdp", "ed"),
            P(None, "ed", "fsdp"),
        ),
        out_specs=P("ed", "fsdp"),
        check_vma=False,
    )
```

```python
import functools

import jax
import jax.numpy as jnp
from jax import lax
from jax.experimental import pallas as pl
from jax.experimental.pallas import tpu as pltpu
from jax.sharding import PartitionSpec as P

CAP = 81
MESH = pl.DeviceIdType.MESH


def slot_match(routes, window, capacity):
    window_ids = jnp.arange(window, dtype=jnp.int32)
    routed = jnp.any(routes[:, :, None, :] == window_ids[None, None, :, None], axis=3)
    position = jnp.cumsum(routed.astype(jnp.int32), axis=1) - 1
    slot_ids = jnp.arange(capacity, dtype=jnp.int32)
    hits = routed[:, :, :, None] & (position[:, :, :, None] == slot_ids[None, None, None, :])
    return hits.astype(jnp.int32)


def take_block(block_rows, row_list):
    return jnp.take(block_rows, row_list, axis=0)


def pick_rows(blocks, routes, window, capacity):
    match = slot_match(routes, window, capacity)
    row_numbers = jnp.arange(blocks.shape[1], dtype=jnp.int32)
    source_row = jnp.sum(match * row_numbers[None, :, None, None], axis=1).reshape(
        blocks.shape[0], window * capacity
    )
    filled = jnp.sum(match, axis=1).reshape(blocks.shape[0], window * capacity)
    picked = jax.vmap(take_block)(blocks, source_row)
    picked = jnp.where(filled[:, :, None] > 0, picked, jnp.zeros_like(picked))
    return picked.reshape(blocks.shape[0], window, capacity, blocks.shape[2])


def combine_matrix(routes, weights, window, capacity):
    match = slot_match(routes[None], window, capacity)[0]
    window_ids = jnp.arange(window, dtype=jnp.int32)
    per_expert = jnp.sum(
        jnp.where(
            routes[:, None, :] == window_ids[None, :, None],
            weights[:, None, :],
            jnp.zeros_like(weights[:, None, :]),
        ),
        axis=2,
    )
    return (per_expert[:, :, None] * match.astype(weights.dtype)).reshape(
        routes.shape[0], window * capacity
    )


def _exchange_kernel(axis, m, stride, gather, x_ref, o_ref, send_sem, recv_sem, own_sem):
    me = lax.axis_index(axis)
    k = lax.rem(me // stride, m)
    base = me - k * stride

    def member(i):
        return lax.rem(k + 1 + i, m)

    def device(j):
        return {axis: base + j * stride}

    def source(j):
        return x_ref if gather else x_ref.at[j]

    def outgoing(j):
        return pltpu.make_async_remote_copy(
            src_ref=source(j),
            dst_ref=o_ref.at[k],
            send_sem=send_sem.at[j],
            recv_sem=recv_sem.at[k],
            device_id=device(j),
            device_id_type=MESH,
        )

    def incoming(j):
        return pltpu.make_async_remote_copy(
            src_ref=source(j),
            dst_ref=o_ref.at[j],
            send_sem=send_sem.at[j],
            recv_sem=recv_sem.at[j],
            device_id=device(j),
            device_id_type=MESH,
        )

    barrier = pltpu.get_barrier_semaphore()

    def greet(i, carry):
        pl.semaphore_signal(barrier, 1, device_id=device(member(i)), device_id_type=MESH)
        return carry

    lax.fori_loop(0, m - 1, greet, 0)
    pl.semaphore_wait(barrier, m - 1)

    def send(i, carry):
        outgoing(member(i)).start()
        return carry

    lax.fori_loop(0, m - 1, send, 0)
    own = pltpu.make_async_copy(source(k), o_ref.at[k], own_sem)
    own.start()

    def finish(i, carry):
        j = member(i)
        outgoing(j).wait_send()
        incoming(j).wait_recv()
        return carry

    lax.fori_loop(0, m - 1, finish, 0)
    own.wait()


def exchange(x, axis, m, stride, gather, cid):
    block = x.shape if gather else x.shape[1:]
    return pl.pallas_call(
        functools.partial(_exchange_kernel, axis, m, stride, gather),
        out_shape=jax.ShapeDtypeStruct((m,) + tuple(block), x.dtype),
        in_specs=[pl.BlockSpec(memory_space=pltpu.VMEM)],
        out_specs=pl.BlockSpec(memory_space=pltpu.VMEM),
        scratch_shapes=[
            pltpu.SemaphoreType.DMA((m,)),
            pltpu.SemaphoreType.DMA((m,)),
            pltpu.SemaphoreType.DMA,
        ],
        compiler_params=pltpu.CompilerParams(collective_id=cid, has_side_effects=True),
    )(x)


def _gate_kernel(axis, m, hidden, sel_ref, w_ref, o_ref, out_buf, in_buf, acc, send_sem, recv_sem):
    me = lax.axis_index(axis)
    bands = sel_ref.shape[1]

    def member(i):
        return lax.rem(me + 1 + i, m)

    def copy(j, slot):
        return pltpu.make_async_remote_copy(
            src_ref=out_buf.at[j],
            dst_ref=in_buf.at[slot],
            send_sem=send_sem.at[j],
            recv_sem=recv_sem.at[slot],
            device_id={axis: j},
            device_id_type=MESH,
        )

    def partial(j, b):
        return jnp.dot(sel_ref[j, b], w_ref[...], preferred_element_type=jnp.float32)

    barrier = pltpu.get_barrier_semaphore()

    def greet(i, carry):
        pl.semaphore_signal(barrier, 1, device_id={axis: member(i)}, device_id_type=MESH)
        return carry

    lax.fori_loop(0, m - 1, greet, 0)
    pl.semaphore_wait(barrier, m - 1)

    def send(i, carry):
        j = member(i)
        for b in range(bands):
            out_buf[j, b] = partial(j, b).astype(out_buf.dtype)
        copy(j, me).start()
        return carry

    lax.fori_loop(0, m - 1, send, 0)
    for b in range(bands):
        acc[b] = partial(me, b)

    def gather(i, carry):
        j = member(i)
        copy(j, me).wait_send()
        copy(j, j).wait_recv()
        acc[...] += in_buf[j].astype(jnp.float32)
        return carry

    lax.fori_loop(0, m - 1, gather, 0)
    total = acc[...]
    gate = total[..., :hidden]
    up = total[..., hidden:]
    o_ref[...] = (jax.nn.silu(gate) * up).astype(o_ref.dtype)


def gate_act(sel, w, axis, m, cid):
    _, bands, rows, _ = sel.shape
    hidden = w.shape[1] // 2
    return pl.pallas_call(
        functools.partial(_gate_kernel, axis, m, hidden),
        out_shape=jax.ShapeDtypeStruct((bands, rows, hidden), jnp.bfloat16),
        in_specs=[pl.BlockSpec(memory_space=pltpu.VMEM)] * 2,
        out_specs=pl.BlockSpec(memory_space=pltpu.VMEM),
        scratch_shapes=[
            pltpu.VMEM((m, bands, rows, 2 * hidden), jnp.bfloat16),
            pltpu.VMEM((m, bands, rows, 2 * hidden), jnp.bfloat16),
            pltpu.VMEM((bands, rows, 2 * hidden), jnp.float32),
            pltpu.SemaphoreType.DMA((m,)),
            pltpu.SemaphoreType.DMA((m,)),
        ],
        compiler_params=pltpu.CompilerParams(collective_id=cid, has_side_effects=True),
    )(sel, w)


def _down_kernel(nf, chips, act_ref, wd_ref, o_ref, act_buf, term_buf, sib_buf, pre_buf, in_buf,
                 a_send, a_recv, s_send, s_recv, e_send, e_recv):
    bands = act_ref.shape[0]
    f = lax.axis_index("fsdp")
    e = lax.axis_index("ed")
    core = lax.rem(e, 2)
    chip = e // 2
    sib = e + 1 - 2 * core

    def fsdp_peer(i):
        return lax.rem(f + 1 + i, nf)

    def chip_peer(i):
        return lax.rem(chip + 1 + i, chips)

    def act_copy(g, slot):
        return pltpu.make_async_remote_copy(
            src_ref=act_ref,
            dst_ref=act_buf.at[slot],
            send_sem=a_send.at[g],
            recv_sem=a_recv.at[slot],
            device_id={"fsdp": g},
            device_id_type=MESH,
        )

    def piece_copy(h, slot):
        return pltpu.make_async_remote_copy(
            src_ref=pre_buf.at[h],
            dst_ref=in_buf.at[slot],
            send_sem=e_send.at[h],
            recv_sem=e_recv.at[slot],
            device_id={"ed": h * 2 + core},
            device_id_type=MESH,
        )

    barrier = pltpu.get_barrier_semaphore()

    def greet_fsdp(i, carry):
        pl.semaphore_signal(barrier, 1, device_id={"fsdp": fsdp_peer(i)}, device_id_type=MESH)
        return carry

    def greet_ed(i, carry):
        pl.semaphore_signal(barrier, 1, device_id={"ed": chip_peer(i) * 2 + core}, device_id_type=MESH)
        return carry

    lax.fori_loop(0, nf - 1, greet_fsdp, 0)
    lax.fori_loop(0, chips - 1, greet_ed, 0)
    pl.semaphore_signal(barrier, 1, device_id={"ed": sib}, device_id_type=MESH)
    pl.semaphore_wait(barrier, nf - 1 + chips)

    def send_act(i, carry):
        act_copy(fsdp_peer(i), f).start()
        return carry

    lax.fori_loop(0, nf - 1, send_act, 0)
    for b in range(bands):
        term_buf[f * bands + b] = jnp.dot(
            act_ref[b], wd_ref[...], preferred_element_type=jnp.float32
        ).astype(term_buf.dtype)

    def take_act(i, carry):
        g = fsdp_peer(i)
        act_copy(g, f).wait_send()
        act_copy(g, g).wait_recv()
        for b in range(bands):
            term_buf[g * bands + b] = jnp.dot(
                act_buf[g, b], wd_ref[...], preferred_element_type=jnp.float32
            ).astype(term_buf.dtype)
        return carry

    lax.fori_loop(0, nf - 1, take_act, 0)

    pair = pltpu.make_async_remote_copy(
        src_ref=term_buf.at[pl.ds((1 - core) * chips, chips)],
        dst_ref=sib_buf,
        send_sem=s_send,
        recv_sem=s_recv,
        device_id={"ed": sib},
        device_id_type=MESH,
    )
    pair.start()
    pair.wait_send()
    pair.wait_recv()
    mine = term_buf[pl.ds(core * chips, chips)].astype(jnp.float32)
    pre_buf[...] = (mine + sib_buf[...].astype(jnp.float32)).astype(pre_buf.dtype)

    def send_piece(i, carry):
        piece_copy(chip_peer(i), chip).start()
        return carry

    lax.fori_loop(0, chips - 1, send_piece, 0)
    o_ref[...] = pre_buf[chip].astype(jnp.float32)

    def take_piece(i, carry):
        h = chip_peer(i)
        piece_copy(h, chip).wait_send()
        piece_copy(h, h).wait_recv()
        o_ref[...] += in_buf[h].astype(jnp.float32)
        return carry

    lax.fori_loop(0, chips - 1, take_piece, 0)


def down_terms(act, wd, nf, chips, cid):
    bands, rows, hidden = act.shape
    d = wd.shape[1]
    blocks = nf * bands
    return pl.pallas_call(
        functools.partial(_down_kernel, nf, chips),
        out_shape=jax.ShapeDtypeStruct((rows, d), jnp.float32),
        in_specs=[pl.BlockSpec(memory_space=pltpu.VMEM)] * 2,
        out_specs=pl.BlockSpec(memory_space=pltpu.VMEM),
        scratch_shapes=[
            pltpu.VMEM((nf, bands, rows, hidden), jnp.bfloat16),
            pltpu.VMEM((blocks, rows, d), jnp.bfloat16),
            pltpu.VMEM((chips, rows, d), jnp.bfloat16),
            pltpu.VMEM((chips, rows, d), jnp.bfloat16),
            pltpu.VMEM((chips, rows, d), jnp.bfloat16),
            pltpu.SemaphoreType.DMA((nf,)),
            pltpu.SemaphoreType.DMA((nf,)),
            pltpu.SemaphoreType.DMA,
            pltpu.SemaphoreType.DMA,
            pltpu.SemaphoreType.DMA((chips,)),
            pltpu.SemaphoreType.DMA((chips,)),
        ],
        compiler_params=pltpu.CompilerParams(collective_id=cid, has_side_effects=True),
    )(act, wd)


def _up_kernel(nf, chips, slot_ref, w_ref, o_ref, sel_buf, out_buf, in_buf, acc,
               e_send, s_send, fwd_send, sel_recv, f_send, f_recv):
    bands = o_ref.shape[0]
    hidden = o_ref.shape[2]
    f = lax.axis_index("fsdp")
    e = lax.axis_index("ed")
    core = lax.rem(e, 2)
    chip = e // 2
    sib = e + 1 - 2 * core
    mine = core * chips + chip

    def fsdp_peer(i):
        return lax.rem(f + 1 + i, nf)

    def chip_peer(i):
        return lax.rem(chip + 1 + i, chips)

    def direct(h):
        return pltpu.make_async_remote_copy(
            src_ref=slot_ref,
            dst_ref=sel_buf.at[mine],
            send_sem=e_send.at[h],
            recv_sem=sel_recv.at[mine],
            device_id={"ed": h * 2 + core},
            device_id_type=MESH,
        )

    def forward(blk):
        return pltpu.make_async_remote_copy(
            src_ref=sel_buf.at[blk],
            dst_ref=sel_buf.at[blk],
            send_sem=fwd_send.at[lax.rem(blk, chips)],
            recv_sem=sel_recv.at[blk],
            device_id={"ed": sib},
            device_id_type=MESH,
        )

    def partial_copy(g, slot):
        return pltpu.make_async_remote_copy(
            src_ref=out_buf.at[g],
            dst_ref=in_buf.at[slot],
            send_sem=f_send.at[g],
            recv_sem=f_recv.at[slot],
            device_id={"fsdp": g},
            device_id_type=MESH,
        )

    barrier = pltpu.get_barrier_semaphore()

    def greet_fsdp(i, carry):
        pl.semaphore_signal(barrier, 1, device_id={"fsdp": fsdp_peer(i)}, device_id_type=MESH)
        return carry

    def greet_ed(i, carry):
        pl.semaphore_signal(barrier, 1, device_id={"ed": chip_peer(i) * 2 + core}, device_id_type=MESH)
        return carry

    lax.fori_loop(0, nf - 1, greet_fsdp, 0)
    lax.fori_loop(0, chips - 1, greet_ed, 0)
    pl.semaphore_signal(barrier, 1, device_id={"ed": sib}, device_id_type=MESH)
    pl.semaphore_wait(barrier, nf - 1 + chips)

    def send_slots(i, carry):
        direct(chip_peer(i)).start()
        return carry

    lax.fori_loop(0, chips - 1, send_slots, 0)
    to_sib = pltpu.make_async_remote_copy(
        src_ref=slot_ref,
        dst_ref=sel_buf.at[mine],
        send_sem=s_send,
        recv_sem=sel_recv.at[mine],
        device_id={"ed": sib},
        device_id_type=MESH,
    )
    to_sib.start()
    sel_buf[mine] = slot_ref[...]

    def band(i, carry):
        j = lax.rem(f + 1 + i, nf)
        for t in range(bands):
            blk = j * bands + t
            same_core = (blk // chips) == core
            not_mine = blk != mine

            @pl.when(same_core & not_mine)
            def _():
                forward(blk).wait_recv()
                forward(blk).start()

            @pl.when(jnp.logical_not(same_core))
            def _():
                forward(blk).wait_recv()

        for t in range(bands):
            blk = j * bands + t
            out_buf[j, t] = jnp.dot(
                sel_buf[blk], w_ref[...], preferred_element_type=jnp.float32
            ).astype(out_buf.dtype)

        @pl.when(j != f)
        def _():
            partial_copy(j, f).start()

        return carry

    lax.fori_loop(0, nf, band, 0)
    acc[...] = out_buf[f].astype(jnp.float32)

    def gather(i, carry):
        g = fsdp_peer(i)
        partial_copy(g, f).wait_send()
        partial_copy(g, g).wait_recv()
        acc[...] += in_buf[g].astype(jnp.float32)
        return carry

    lax.fori_loop(0, nf - 1, gather, 0)

    def drain(i, carry):
        h = chip_peer(i)
        direct(h).wait_send()
        forward(core * chips + h).wait_send()
        return carry

    lax.fori_loop(0, chips - 1, drain, 0)
    to_sib.wait_send()
    total = acc[...]
    o_ref[...] = (jax.nn.silu(total[..., :hidden]) * total[..., hidden:]).astype(o_ref.dtype)


def slots_to_act(slots, w, nf, chips, cid):
    rows, d = slots.shape
    hidden = w.shape[1] // 2
    bands = 2 * chips // nf
    return pl.pallas_call(
        functools.partial(_up_kernel, nf, chips),
        out_shape=jax.ShapeDtypeStruct((bands, rows, hidden), jnp.bfloat16),
        in_specs=[pl.BlockSpec(memory_space=pltpu.VMEM)] * 2,
        out_specs=pl.BlockSpec(memory_space=pltpu.VMEM),
        scratch_shapes=[
            pltpu.VMEM((2 * chips, rows, d), jnp.bfloat16),
            pltpu.VMEM((nf, bands, rows, 2 * hidden), jnp.bfloat16),
            pltpu.VMEM((nf, bands, rows, 2 * hidden), jnp.bfloat16),
            pltpu.VMEM((bands, rows, 2 * hidden), jnp.float32),
            pltpu.SemaphoreType.DMA((chips,)),
            pltpu.SemaphoreType.DMA,
            pltpu.SemaphoreType.DMA((chips,)),
            pltpu.SemaphoreType.DMA((2 * chips,)),
            pltpu.SemaphoreType.DMA((nf,)),
            pltpu.SemaphoreType.DMA((nf,)),
        ],
        compiler_params=pltpu.CompilerParams(collective_id=cid, has_side_effects=True),
    )(slots, w)


def local(tokens, expert_ids, route_weights, w_gate, w_up, w_down):
    window = w_gate.shape[0]
    features_dev = tokens.shape[1]
    hidden_dev = w_gate.shape[2]
    n_ed = lax.axis_size("ed")
    n_fsdp = lax.axis_size("fsdp")
    chips = n_ed // 2
    per_band = n_ed // n_fsdp
    own_slots = pick_rows(tokens[None], expert_ids[None], window, CAP)[0, 0]
    both = jnp.concatenate([w_gate[0], w_up[0]], axis=1)
    activation = slots_to_act(own_slots, both, n_fsdp, chips, 2)
    slot_out = down_terms(activation, w_down[0], n_fsdp, chips, 3)
    weights_matrix = combine_matrix(expert_ids, route_weights, window, CAP)
    mixed = jnp.dot(
        weights_matrix,
        slot_out.reshape(window * CAP, features_dev),
        precision=lax.Precision.HIGHEST,
        preferred_element_type=jnp.float32,
    )
    return mixed.astype(jnp.bfloat16)


def solution(mesh):
    return jax.shard_map(
        local,
        mesh=mesh,
        in_specs=(
            P("ed", "fsdp"),
            P("ed", None),
            P("ed", None),
            P(None, "fsdp", "ed"),
            P(None, "fsdp", "ed"),
            P(None, "ed", "fsdp"),
        ),
        out_specs=P("ed", "fsdp"),
        check_vma=False,
    )
```

```python
import functools

import jax
import jax.numpy as jnp
from jax import lax
from jax.experimental import pallas as pl
from jax.experimental.pallas import tpu as pltpu
from jax.sharding import PartitionSpec as P

CAP = 81
MESH = pl.DeviceIdType.MESH


def slot_match(routes, window, capacity):
    window_ids = jnp.arange(window, dtype=jnp.int32)
    routed = jnp.any(routes[:, :, None, :] == window_ids[None, None, :, None], axis=3)
    position = jnp.cumsum(routed.astype(jnp.int32), axis=1) - 1
    slot_ids = jnp.arange(capacity, dtype=jnp.int32)
    hits = routed[:, :, :, None] & (position[:, :, :, None] == slot_ids[None, None, None, :])
    return hits.astype(jnp.int32)


def take_block(block_rows, row_list):
    return jnp.take(block_rows, row_list, axis=0)


def pick_rows(blocks, routes, window, capacity):
    match = slot_match(routes, window, capacity)
    row_numbers = jnp.arange(blocks.shape[1], dtype=jnp.int32)
    source_row = jnp.sum(match * row_numbers[None, :, None, None], axis=1).reshape(
        blocks.shape[0], window * capacity
    )
    filled = jnp.sum(match, axis=1).reshape(blocks.shape[0], window * capacity)
    picked = jax.vmap(take_block)(blocks, source_row)
    picked = jnp.where(filled[:, :, None] > 0, picked, jnp.zeros_like(picked))
    return picked.reshape(blocks.shape[0], window, capacity, blocks.shape[2])


def combine_matrix(routes, weights, window, capacity):
    match = slot_match(routes[None], window, capacity)[0]
    window_ids = jnp.arange(window, dtype=jnp.int32)
    per_expert = jnp.sum(
        jnp.where(
            routes[:, None, :] == window_ids[None, :, None],
            weights[:, None, :],
            jnp.zeros_like(weights[:, None, :]),
        ),
        axis=2,
    )
    return (per_expert[:, :, None] * match.astype(weights.dtype)).reshape(
        routes.shape[0], window * capacity
    )


def _exchange_kernel(axis, m, stride, gather, x_ref, o_ref, send_sem, recv_sem, own_sem):
    me = lax.axis_index(axis)
    k = lax.rem(me // stride, m)
    base = me - k * stride

    def member(i):
        return lax.rem(k + 1 + i, m)

    def device(j):
        return {axis: base + j * stride}

    def source(j):
        return x_ref if gather else x_ref.at[j]

    def outgoing(j):
        return pltpu.make_async_remote_copy(
            src_ref=source(j),
            dst_ref=o_ref.at[k],
            send_sem=send_sem.at[j],
            recv_sem=recv_sem.at[k],
            device_id=device(j),
            device_id_type=MESH,
        )

    def incoming(j):
        return pltpu.make_async_remote_copy(
            src_ref=source(j),
            dst_ref=o_ref.at[j],
            send_sem=send_sem.at[j],
            recv_sem=recv_sem.at[j],
            device_id=device(j),
            device_id_type=MESH,
        )

    barrier = pltpu.get_barrier_semaphore()

    def greet(i, carry):
        pl.semaphore_signal(barrier, 1, device_id=device(member(i)), device_id_type=MESH)
        return carry

    lax.fori_loop(0, m - 1, greet, 0)
    pl.semaphore_wait(barrier, m - 1)

    def send(i, carry):
        outgoing(member(i)).start()
        return carry

    lax.fori_loop(0, m - 1, send, 0)
    own = pltpu.make_async_copy(source(k), o_ref.at[k], own_sem)
    own.start()

    def finish(i, carry):
        j = member(i)
        outgoing(j).wait_send()
        incoming(j).wait_recv()
        return carry

    lax.fori_loop(0, m - 1, finish, 0)
    own.wait()


def exchange(x, axis, m, stride, gather, cid):
    block = x.shape if gather else x.shape[1:]
    return pl.pallas_call(
        functools.partial(_exchange_kernel, axis, m, stride, gather),
        out_shape=jax.ShapeDtypeStruct((m,) + tuple(block), x.dtype),
        in_specs=[pl.BlockSpec(memory_space=pltpu.VMEM)],
        out_specs=pl.BlockSpec(memory_space=pltpu.VMEM),
        scratch_shapes=[
            pltpu.SemaphoreType.DMA((m,)),
            pltpu.SemaphoreType.DMA((m,)),
            pltpu.SemaphoreType.DMA,
        ],
        compiler_params=pltpu.CompilerParams(collective_id=cid, has_side_effects=True),
    )(x)


def _gate_kernel(axis, m, hidden, sel_ref, w_ref, o_ref, out_buf, in_buf, acc, send_sem, recv_sem):
    me = lax.axis_index(axis)
    bands = sel_ref.shape[1]

    def member(i):
        return lax.rem(me + 1 + i, m)

    def copy(j, slot):
        return pltpu.make_async_remote_copy(
            src_ref=out_buf.at[j],
            dst_ref=in_buf.at[slot],
            send_sem=send_sem.at[j],
            recv_sem=recv_sem.at[slot],
            device_id={axis: j},
            device_id_type=MESH,
        )

    def partial(j, b):
        return jnp.dot(sel_ref[j, b], w_ref[...], preferred_element_type=jnp.float32)

    barrier = pltpu.get_barrier_semaphore()

    def greet(i, carry):
        pl.semaphore_signal(barrier, 1, device_id={axis: member(i)}, device_id_type=MESH)
        return carry

    lax.fori_loop(0, m - 1, greet, 0)
    pl.semaphore_wait(barrier, m - 1)

    def send(i, carry):
        j = member(i)
        for b in range(bands):
            out_buf[j, b] = partial(j, b).astype(out_buf.dtype)
        copy(j, me).start()
        return carry

    lax.fori_loop(0, m - 1, send, 0)
    for b in range(bands):
        acc[b] = partial(me, b)

    def gather(i, carry):
        j = member(i)
        copy(j, me).wait_send()
        copy(j, j).wait_recv()
        acc[...] += in_buf[j].astype(jnp.float32)
        return carry

    lax.fori_loop(0, m - 1, gather, 0)
    total = acc[...]
    gate = total[..., :hidden]
    up = total[..., hidden:]
    o_ref[...] = (jax.nn.silu(gate) * up).astype(o_ref.dtype)


def gate_act(sel, w, axis, m, cid):
    _, bands, rows, _ = sel.shape
    hidden = w.shape[1] // 2
    return pl.pallas_call(
        functools.partial(_gate_kernel, axis, m, hidden),
        out_shape=jax.ShapeDtypeStruct((bands, rows, hidden), jnp.bfloat16),
        in_specs=[pl.BlockSpec(memory_space=pltpu.VMEM)] * 2,
        out_specs=pl.BlockSpec(memory_space=pltpu.VMEM),
        scratch_shapes=[
            pltpu.VMEM((m, bands, rows, 2 * hidden), jnp.bfloat16),
            pltpu.VMEM((m, bands, rows, 2 * hidden), jnp.bfloat16),
            pltpu.VMEM((bands, rows, 2 * hidden), jnp.float32),
            pltpu.SemaphoreType.DMA((m,)),
            pltpu.SemaphoreType.DMA((m,)),
        ],
        compiler_params=pltpu.CompilerParams(collective_id=cid, has_side_effects=True),
    )(sel, w)


def _down_kernel(nf, chips, act_ref, wd_ref, o_ref, act_buf, term_buf, sib_buf, pre_buf, in_buf,
                 a_send, a_recv, s_send, s_recv, e_send, e_recv):
    bands = act_ref.shape[0]
    f = lax.axis_index("fsdp")
    e = lax.axis_index("ed")
    core = lax.rem(e, 2)
    chip = e // 2
    sib = e + 1 - 2 * core

    def fsdp_peer(i):
        return lax.rem(f + 1 + i, nf)

    def chip_peer(i):
        return lax.rem(chip + 1 + i, chips)

    def act_copy(g, slot):
        return pltpu.make_async_remote_copy(
            src_ref=act_ref,
            dst_ref=act_buf.at[slot],
            send_sem=a_send.at[g],
            recv_sem=a_recv.at[slot],
            device_id={"fsdp": g},
            device_id_type=MESH,
        )

    def piece_copy(h, slot):
        return pltpu.make_async_remote_copy(
            src_ref=pre_buf.at[h],
            dst_ref=in_buf.at[slot],
            send_sem=e_send.at[h],
            recv_sem=e_recv.at[slot],
            device_id={"ed": h * 2 + core},
            device_id_type=MESH,
        )

    barrier = pltpu.get_barrier_semaphore()

    def greet_fsdp(i, carry):
        pl.semaphore_signal(barrier, 1, device_id={"fsdp": fsdp_peer(i)}, device_id_type=MESH)
        return carry

    def greet_ed(i, carry):
        pl.semaphore_signal(barrier, 1, device_id={"ed": chip_peer(i) * 2 + core}, device_id_type=MESH)
        return carry

    lax.fori_loop(0, nf - 1, greet_fsdp, 0)
    lax.fori_loop(0, chips - 1, greet_ed, 0)
    pl.semaphore_signal(barrier, 1, device_id={"ed": sib}, device_id_type=MESH)
    pl.semaphore_wait(barrier, nf - 1 + chips)

    def send_act(i, carry):
        act_copy(fsdp_peer(i), f).start()
        return carry

    lax.fori_loop(0, nf - 1, send_act, 0)
    for b in range(bands):
        term_buf[f * bands + b] = jnp.dot(
            act_ref[b], wd_ref[...], preferred_element_type=jnp.float32
        ).astype(term_buf.dtype)

    def take_act(i, carry):
        g = fsdp_peer(i)
        act_copy(g, f).wait_send()
        act_copy(g, g).wait_recv()
        for b in range(bands):
            term_buf[g * bands + b] = jnp.dot(
                act_buf[g, b], wd_ref[...], preferred_element_type=jnp.float32
            ).astype(term_buf.dtype)
        return carry

    lax.fori_loop(0, nf - 1, take_act, 0)

    pair = pltpu.make_async_remote_copy(
        src_ref=term_buf.at[pl.ds((1 - core) * chips, chips)],
        dst_ref=sib_buf,
        send_sem=s_send,
        recv_sem=s_recv,
        device_id={"ed": sib},
        device_id_type=MESH,
    )
    pair.start()
    pair.wait_send()
    pair.wait_recv()
    mine = term_buf[pl.ds(core * chips, chips)].astype(jnp.float32)
    pre_buf[...] = (mine + sib_buf[...].astype(jnp.float32)).astype(pre_buf.dtype)

    def send_piece(i, carry):
        piece_copy(chip_peer(i), chip).start()
        return carry

    lax.fori_loop(0, chips - 1, send_piece, 0)
    o_ref[...] = pre_buf[chip].astype(jnp.float32)

    def take_piece(i, carry):
        h = chip_peer(i)
        piece_copy(h, chip).wait_send()
        piece_copy(h, h).wait_recv()
        o_ref[...] += in_buf[h].astype(jnp.float32)
        return carry

    lax.fori_loop(0, chips - 1, take_piece, 0)


def down_terms(act, wd, nf, chips, cid):
    bands, rows, hidden = act.shape
    d = wd.shape[1]
    blocks = nf * bands
    return pl.pallas_call(
        functools.partial(_down_kernel, nf, chips),
        out_shape=jax.ShapeDtypeStruct((rows, d), jnp.float32),
        in_specs=[pl.BlockSpec(memory_space=pltpu.VMEM)] * 2,
        out_specs=pl.BlockSpec(memory_space=pltpu.VMEM),
        scratch_shapes=[
            pltpu.VMEM((nf, bands, rows, hidden), jnp.bfloat16),
            pltpu.VMEM((blocks, rows, d), jnp.bfloat16),
            pltpu.VMEM((chips, rows, d), jnp.bfloat16),
            pltpu.VMEM((chips, rows, d), jnp.bfloat16),
            pltpu.VMEM((chips, rows, d), jnp.bfloat16),
            pltpu.SemaphoreType.DMA((nf,)),
            pltpu.SemaphoreType.DMA((nf,)),
            pltpu.SemaphoreType.DMA,
            pltpu.SemaphoreType.DMA,
            pltpu.SemaphoreType.DMA((chips,)),
            pltpu.SemaphoreType.DMA((chips,)),
        ],
        compiler_params=pltpu.CompilerParams(collective_id=cid, has_side_effects=True),
    )(act, wd)


def _up_kernel(nf, chips, slot_ref, wg_ref, wu_ref, o_ref, sel_buf, out_buf, in_buf, acc,
               e_send, s_send, fwd_send, sel_recv, f_send, f_recv):
    bands = o_ref.shape[0]
    hidden = o_ref.shape[2]
    f = lax.axis_index("fsdp")
    e = lax.axis_index("ed")
    core = lax.rem(e, 2)
    chip = e // 2
    sib = e + 1 - 2 * core
    mine = core * chips + chip

    def fsdp_peer(i):
        return lax.rem(f + 1 + i, nf)

    def chip_peer(i):
        return lax.rem(chip + 1 + i, chips)

    def direct(h):
        return pltpu.make_async_remote_copy(
            src_ref=slot_ref,
            dst_ref=sel_buf.at[mine],
            send_sem=e_send.at[h],
            recv_sem=sel_recv.at[mine],
            device_id={"ed": h * 2 + core},
            device_id_type=MESH,
        )

    def forward(blk):
        return pltpu.make_async_remote_copy(
            src_ref=sel_buf.at[blk],
            dst_ref=sel_buf.at[blk],
            send_sem=fwd_send.at[lax.rem(blk, chips)],
            recv_sem=sel_recv.at[blk],
            device_id={"ed": sib},
            device_id_type=MESH,
        )

    def partial_copy(g, slot):
        return pltpu.make_async_remote_copy(
            src_ref=out_buf.at[g],
            dst_ref=in_buf.at[slot],
            send_sem=f_send.at[g],
            recv_sem=f_recv.at[slot],
            device_id={"fsdp": g},
            device_id_type=MESH,
        )

    barrier = pltpu.get_barrier_semaphore()

    def greet_fsdp(i, carry):
        pl.semaphore_signal(barrier, 1, device_id={"fsdp": fsdp_peer(i)}, device_id_type=MESH)
        return carry

    def greet_ed(i, carry):
        pl.semaphore_signal(barrier, 1, device_id={"ed": chip_peer(i) * 2 + core}, device_id_type=MESH)
        return carry

    lax.fori_loop(0, nf - 1, greet_fsdp, 0)
    lax.fori_loop(0, chips - 1, greet_ed, 0)
    pl.semaphore_signal(barrier, 1, device_id={"ed": sib}, device_id_type=MESH)
    pl.semaphore_wait(barrier, nf - 1 + chips)

    def send_slots(i, carry):
        direct(chip_peer(i)).start()
        return carry

    lax.fori_loop(0, chips - 1, send_slots, 0)
    to_sib = pltpu.make_async_remote_copy(
        src_ref=slot_ref,
        dst_ref=sel_buf.at[mine],
        send_sem=s_send,
        recv_sem=sel_recv.at[mine],
        device_id={"ed": sib},
        device_id_type=MESH,
    )
    to_sib.start()
    sel_buf[mine] = slot_ref[...]

    def band(i, carry):
        j = lax.rem(f + 1 + i, nf)
        for t in range(bands):
            blk = j * bands + t
            same_core = (blk // chips) == core
            not_mine = blk != mine

            @pl.when(same_core & not_mine)
            def _():
                forward(blk).wait_recv()
                forward(blk).start()

            @pl.when(jnp.logical_not(same_core))
            def _():
                forward(blk).wait_recv()

        for t in range(bands):
            blk = j * bands + t
            rows_in = sel_buf[blk]
            out_buf[j, t, :, :hidden] = jnp.dot(
                rows_in, wg_ref[...], preferred_element_type=jnp.float32
            ).astype(out_buf.dtype)
            out_buf[j, t, :, hidden:] = jnp.dot(
                rows_in, wu_ref[...], preferred_element_type=jnp.float32
            ).astype(out_buf.dtype)

        @pl.when(j != f)
        def _():
            partial_copy(j, f).start()

        return carry

    lax.fori_loop(0, nf, band, 0)
    acc[...] = out_buf[f].astype(jnp.float32)

    def gather(i, carry):
        g = fsdp_peer(i)
        partial_copy(g, f).wait_send()
        partial_copy(g, g).wait_recv()
        acc[...] += in_buf[g].astype(jnp.float32)
        return carry

    lax.fori_loop(0, nf - 1, gather, 0)

    def drain(i, carry):
        h = chip_peer(i)
        direct(h).wait_send()
        forward(core * chips + h).wait_send()
        return carry

    lax.fori_loop(0, chips - 1, drain, 0)
    to_sib.wait_send()
    total = acc[...]
    o_ref[...] = (jax.nn.silu(total[..., :hidden]) * total[..., hidden:]).astype(o_ref.dtype)


def slots_to_act(slots, wg, wu, nf, chips, cid):
    rows, d = slots.shape
    hidden = wg.shape[1]
    bands = 2 * chips // nf
    return pl.pallas_call(
        functools.partial(_up_kernel, nf, chips),
        out_shape=jax.ShapeDtypeStruct((bands, rows, hidden), jnp.bfloat16),
        in_specs=[pl.BlockSpec(memory_space=pltpu.VMEM)] * 3,
        out_specs=pl.BlockSpec(memory_space=pltpu.VMEM),
        scratch_shapes=[
            pltpu.VMEM((2 * chips, rows, d), jnp.bfloat16),
            pltpu.VMEM((nf, bands, rows, 2 * hidden), jnp.bfloat16),
            pltpu.VMEM((nf, bands, rows, 2 * hidden), jnp.bfloat16),
            pltpu.VMEM((bands, rows, 2 * hidden), jnp.float32),
            pltpu.SemaphoreType.DMA((chips,)),
            pltpu.SemaphoreType.DMA,
            pltpu.SemaphoreType.DMA((chips,)),
            pltpu.SemaphoreType.DMA((2 * chips,)),
            pltpu.SemaphoreType.DMA((nf,)),
            pltpu.SemaphoreType.DMA((nf,)),
        ],
        compiler_params=pltpu.CompilerParams(collective_id=cid, has_side_effects=True),
    )(slots, wg, wu)


def local(tokens, expert_ids, route_weights, w_gate, w_up, w_down):
    window = w_gate.shape[0]
    features_dev = tokens.shape[1]
    hidden_dev = w_gate.shape[2]
    n_ed = lax.axis_size("ed")
    n_fsdp = lax.axis_size("fsdp")
    chips = n_ed // 2
    per_band = n_ed // n_fsdp
    tok_dev = tokens.shape[0]
    order = jnp.arange(tok_dev, dtype=jnp.int32)
    routed = jnp.any(expert_ids == 0, axis=1)
    lower = (order[:, None] >= order[None, :]).astype(jnp.bfloat16)
    count = jnp.dot(lower, routed.astype(jnp.bfloat16), preferred_element_type=jnp.float32)
    slot_ids = jnp.arange(CAP, dtype=jnp.float32)
    match = routed[None, :] & (count[None, :] - 1.0 == slot_ids[:, None])
    own_slots = jnp.dot(
        match.astype(jnp.bfloat16), tokens, preferred_element_type=jnp.float32
    ).astype(jnp.bfloat16)
    activation = slots_to_act(own_slots, w_gate[0], w_up[0], n_fsdp, chips, 2)
    slot_out = down_terms(activation, w_down[0], n_fsdp, chips, 3)
    per_expert = jnp.sum(
        jnp.where(expert_ids == 0, route_weights, jnp.zeros_like(route_weights)), axis=1
    )
    weights_matrix = match.T.astype(jnp.float32) * per_expert[:, None]
    mixed = jnp.dot(
        weights_matrix,
        slot_out.reshape(window * CAP, features_dev),
        precision=lax.Precision.HIGHEST,
        preferred_element_type=jnp.float32,
    )
    return mixed.astype(jnp.bfloat16)


def solution(mesh):
    return jax.shard_map(
        local,
        mesh=mesh,
        in_specs=(
            P("ed", "fsdp"),
            P("ed", None),
            P("ed", None),
            P(None, "fsdp", "ed"),
            P(None, "fsdp", "ed"),
            P(None, "ed", "fsdp"),
        ),
        out_specs=P("ed", "fsdp"),
        check_vma=False,
    )
```

```python
import functools

import jax
import jax.numpy as jnp
from jax import lax
from jax.experimental import pallas as pl
from jax.experimental.pallas import tpu as pltpu
from jax.sharding import PartitionSpec as P

CAP = 81
MESH = pl.DeviceIdType.MESH


def slot_match(routes, window, capacity):
    window_ids = jnp.arange(window, dtype=jnp.int32)
    routed = jnp.any(routes[:, :, None, :] == window_ids[None, None, :, None], axis=3)
    position = jnp.cumsum(routed.astype(jnp.int32), axis=1) - 1
    slot_ids = jnp.arange(capacity, dtype=jnp.int32)
    hits = routed[:, :, :, None] & (position[:, :, :, None] == slot_ids[None, None, None, :])
    return hits.astype(jnp.int32)


def take_block(block_rows, row_list):
    return jnp.take(block_rows, row_list, axis=0)


def pick_rows(blocks, routes, window, capacity):
    match = slot_match(routes, window, capacity)
    row_numbers = jnp.arange(blocks.shape[1], dtype=jnp.int32)
    source_row = jnp.sum(match * row_numbers[None, :, None, None], axis=1).reshape(
        blocks.shape[0], window * capacity
    )
    filled = jnp.sum(match, axis=1).reshape(blocks.shape[0], window * capacity)
    picked = jax.vmap(take_block)(blocks, source_row)
    picked = jnp.where(filled[:, :, None] > 0, picked, jnp.zeros_like(picked))
    return picked.reshape(blocks.shape[0], window, capacity, blocks.shape[2])


def combine_matrix(routes, weights, window, capacity):
    match = slot_match(routes[None], window, capacity)[0]
    window_ids = jnp.arange(window, dtype=jnp.int32)
    per_expert = jnp.sum(
        jnp.where(
            routes[:, None, :] == window_ids[None, :, None],
            weights[:, None, :],
            jnp.zeros_like(weights[:, None, :]),
        ),
        axis=2,
    )
    return (per_expert[:, :, None] * match.astype(weights.dtype)).reshape(
        routes.shape[0], window * capacity
    )


def _exchange_kernel(axis, m, stride, gather, x_ref, o_ref, send_sem, recv_sem, own_sem):
    me = lax.axis_index(axis)
    k = lax.rem(me // stride, m)
    base = me - k * stride

    def member(i):
        return lax.rem(k + 1 + i, m)

    def device(j):
        return {axis: base + j * stride}

    def source(j):
        return x_ref if gather else x_ref.at[j]

    def outgoing(j):
        return pltpu.make_async_remote_copy(
            src_ref=source(j),
            dst_ref=o_ref.at[k],
            send_sem=send_sem.at[j],
            recv_sem=recv_sem.at[k],
            device_id=device(j),
            device_id_type=MESH,
        )

    def incoming(j):
        return pltpu.make_async_remote_copy(
            src_ref=source(j),
            dst_ref=o_ref.at[j],
            send_sem=send_sem.at[j],
            recv_sem=recv_sem.at[j],
            device_id=device(j),
            device_id_type=MESH,
        )

    barrier = pltpu.get_barrier_semaphore()

    def greet(i, carry):
        pl.semaphore_signal(barrier, 1, device_id=device(member(i)), device_id_type=MESH)
        return carry

    lax.fori_loop(0, m - 1, greet, 0)
    pl.semaphore_wait(barrier, m - 1)

    def send(i, carry):
        outgoing(member(i)).start()
        return carry

    lax.fori_loop(0, m - 1, send, 0)
    own = pltpu.make_async_copy(source(k), o_ref.at[k], own_sem)
    own.start()

    def finish(i, carry):
        j = member(i)
        outgoing(j).wait_send()
        incoming(j).wait_recv()
        return carry

    lax.fori_loop(0, m - 1, finish, 0)
    own.wait()


def exchange(x, axis, m, stride, gather, cid):
    block = x.shape if gather else x.shape[1:]
    return pl.pallas_call(
        functools.partial(_exchange_kernel, axis, m, stride, gather),
        out_shape=jax.ShapeDtypeStruct((m,) + tuple(block), x.dtype),
        in_specs=[pl.BlockSpec(memory_space=pltpu.VMEM)],
        out_specs=pl.BlockSpec(memory_space=pltpu.VMEM),
        scratch_shapes=[
            pltpu.SemaphoreType.DMA((m,)),
            pltpu.SemaphoreType.DMA((m,)),
            pltpu.SemaphoreType.DMA,
        ],
        compiler_params=pltpu.CompilerParams(collective_id=cid, has_side_effects=True),
    )(x)


def _gate_kernel(axis, m, hidden, sel_ref, w_ref, o_ref, out_buf, in_buf, acc, send_sem, recv_sem):
    me = lax.axis_index(axis)
    bands = sel_ref.shape[1]

    def member(i):
        return lax.rem(me + 1 + i, m)

    def copy(j, slot):
        return pltpu.make_async_remote_copy(
            src_ref=out_buf.at[j],
            dst_ref=in_buf.at[slot],
            send_sem=send_sem.at[j],
            recv_sem=recv_sem.at[slot],
            device_id={axis: j},
            device_id_type=MESH,
        )

    def partial(j, b):
        return jnp.dot(sel_ref[j, b], w_ref[...], preferred_element_type=jnp.float32)

    barrier = pltpu.get_barrier_semaphore()

    def greet(i, carry):
        pl.semaphore_signal(barrier, 1, device_id={axis: member(i)}, device_id_type=MESH)
        return carry

    lax.fori_loop(0, m - 1, greet, 0)
    pl.semaphore_wait(barrier, m - 1)

    def send(i, carry):
        j = member(i)
        for b in range(bands):
            out_buf[j, b] = partial(j, b).astype(out_buf.dtype)
        copy(j, me).start()
        return carry

    lax.fori_loop(0, m - 1, send, 0)
    for b in range(bands):
        acc[b] = partial(me, b)

    def gather(i, carry):
        j = member(i)
        copy(j, me).wait_send()
        copy(j, j).wait_recv()
        acc[...] += in_buf[j].astype(jnp.float32)
        return carry

    lax.fori_loop(0, m - 1, gather, 0)
    total = acc[...]
    gate = total[..., :hidden]
    up = total[..., hidden:]
    o_ref[...] = (jax.nn.silu(gate) * up).astype(o_ref.dtype)


def gate_act(sel, w, axis, m, cid):
    _, bands, rows, _ = sel.shape
    hidden = w.shape[1] // 2
    return pl.pallas_call(
        functools.partial(_gate_kernel, axis, m, hidden),
        out_shape=jax.ShapeDtypeStruct((bands, rows, hidden), jnp.bfloat16),
        in_specs=[pl.BlockSpec(memory_space=pltpu.VMEM)] * 2,
        out_specs=pl.BlockSpec(memory_space=pltpu.VMEM),
        scratch_shapes=[
            pltpu.VMEM((m, bands, rows, 2 * hidden), jnp.bfloat16),
            pltpu.VMEM((m, bands, rows, 2 * hidden), jnp.bfloat16),
            pltpu.VMEM((bands, rows, 2 * hidden), jnp.float32),
            pltpu.SemaphoreType.DMA((m,)),
            pltpu.SemaphoreType.DMA((m,)),
        ],
        compiler_params=pltpu.CompilerParams(collective_id=cid, has_side_effects=True),
    )(sel, w)


def _down_kernel(nf, chips, act_ref, wd_ref, o_ref, act_buf, term_buf, sib_buf, pre_buf, in_buf,
                 a_send, a_recv, s_send, s_recv, e_send, e_recv, greet=True):
    bands = act_ref.shape[0]
    f = lax.axis_index("fsdp")
    e = lax.axis_index("ed")
    core = lax.rem(e, 2)
    chip = e // 2
    sib = e + 1 - 2 * core

    def fsdp_peer(i):
        return lax.rem(f + 1 + i, nf)

    def chip_peer(i):
        return lax.rem(chip + 1 + i, chips)

    def act_copy(g, slot):
        return pltpu.make_async_remote_copy(
            src_ref=act_ref,
            dst_ref=act_buf.at[slot],
            send_sem=a_send.at[g],
            recv_sem=a_recv.at[slot],
            device_id={"fsdp": g},
            device_id_type=MESH,
        )

    def piece_copy(h, slot):
        return pltpu.make_async_remote_copy(
            src_ref=pre_buf.at[h],
            dst_ref=in_buf.at[slot],
            send_sem=e_send.at[h],
            recv_sem=e_recv.at[slot],
            device_id={"ed": h * 2 + core},
            device_id_type=MESH,
        )

    barrier = pltpu.get_barrier_semaphore()

    def greet_fsdp(i, carry):
        pl.semaphore_signal(barrier, 1, device_id={"fsdp": fsdp_peer(i)}, device_id_type=MESH)
        return carry

    def greet_ed(i, carry):
        pl.semaphore_signal(barrier, 1, device_id={"ed": chip_peer(i) * 2 + core}, device_id_type=MESH)
        return carry

    if greet:
        lax.fori_loop(0, nf - 1, greet_fsdp, 0)
        lax.fori_loop(0, chips - 1, greet_ed, 0)
        pl.semaphore_signal(barrier, 1, device_id={"ed": sib}, device_id_type=MESH)
        pl.semaphore_wait(barrier, nf - 1 + chips)

    def send_act(i, carry):
        act_copy(fsdp_peer(i), f).start()
        return carry

    lax.fori_loop(0, nf - 1, send_act, 0)
    for b in range(bands):
        term_buf[f * bands + b] = jnp.dot(
            act_ref[b], wd_ref[...], preferred_element_type=jnp.float32
        ).astype(term_buf.dtype)

    def take_act(i, carry):
        g = fsdp_peer(i)
        act_copy(g, f).wait_send()
        act_copy(g, g).wait_recv()
        for b in range(bands):
            term_buf[g * bands + b] = jnp.dot(
                act_buf[g, b], wd_ref[...], preferred_element_type=jnp.float32
            ).astype(term_buf.dtype)
        return carry

    lax.fori_loop(0, nf - 1, take_act, 0)

    pair = pltpu.make_async_remote_copy(
        src_ref=term_buf.at[pl.ds((1 - core) * chips, chips)],
        dst_ref=sib_buf,
        send_sem=s_send,
        recv_sem=s_recv,
        device_id={"ed": sib},
        device_id_type=MESH,
    )
    pair.start()
    pair.wait_send()
    pair.wait_recv()
    mine = term_buf[pl.ds(core * chips, chips)].astype(jnp.float32)
    pre_buf[...] = (mine + sib_buf[...].astype(jnp.float32)).astype(pre_buf.dtype)

    def send_piece(i, carry):
        piece_copy(chip_peer(i), chip).start()
        return carry

    lax.fori_loop(0, chips - 1, send_piece, 0)
    o_ref[...] = pre_buf[chip].astype(jnp.float32)

    def take_piece(i, carry):
        h = chip_peer(i)
        piece_copy(h, chip).wait_send()
        piece_copy(h, h).wait_recv()
        o_ref[...] += in_buf[h].astype(jnp.float32)
        return carry

    lax.fori_loop(0, chips - 1, take_piece, 0)


def down_terms(act, wd, nf, chips, cid):
    bands, rows, hidden = act.shape
    d = wd.shape[1]
    blocks = nf * bands
    return pl.pallas_call(
        functools.partial(_down_kernel, nf, chips),
        out_shape=jax.ShapeDtypeStruct((rows, d), jnp.float32),
        in_specs=[pl.BlockSpec(memory_space=pltpu.VMEM)] * 2,
        out_specs=pl.BlockSpec(memory_space=pltpu.VMEM),
        scratch_shapes=[
            pltpu.VMEM((nf, bands, rows, hidden), jnp.bfloat16),
            pltpu.VMEM((blocks, rows, d), jnp.bfloat16),
            pltpu.VMEM((chips, rows, d), jnp.bfloat16),
            pltpu.VMEM((chips, rows, d), jnp.bfloat16),
            pltpu.VMEM((chips, rows, d), jnp.bfloat16),
            pltpu.SemaphoreType.DMA((nf,)),
            pltpu.SemaphoreType.DMA((nf,)),
            pltpu.SemaphoreType.DMA,
            pltpu.SemaphoreType.DMA,
            pltpu.SemaphoreType.DMA((chips,)),
            pltpu.SemaphoreType.DMA((chips,)),
        ],
        compiler_params=pltpu.CompilerParams(collective_id=cid, has_side_effects=True),
    )(act, wd)


def _up_kernel(nf, chips, slot_ref, wg_ref, wu_ref, o_ref, sel_buf, out_buf, in_buf, acc,
               e_send, s_send, fwd_send, sel_recv, f_send, f_recv):
    bands = o_ref.shape[0]
    hidden = o_ref.shape[2]
    f = lax.axis_index("fsdp")
    e = lax.axis_index("ed")
    core = lax.rem(e, 2)
    chip = e // 2
    sib = e + 1 - 2 * core
    mine = core * chips + chip

    def fsdp_peer(i):
        return lax.rem(f + 1 + i, nf)

    def chip_peer(i):
        return lax.rem(chip + 1 + i, chips)

    def direct(h):
        return pltpu.make_async_remote_copy(
            src_ref=slot_ref,
            dst_ref=sel_buf.at[mine],
            send_sem=e_send.at[h],
            recv_sem=sel_recv.at[mine],
            device_id={"ed": h * 2 + core},
            device_id_type=MESH,
        )

    def forward(blk):
        return pltpu.make_async_remote_copy(
            src_ref=sel_buf.at[blk],
            dst_ref=sel_buf.at[blk],
            send_sem=fwd_send.at[lax.rem(blk, chips)],
            recv_sem=sel_recv.at[blk],
            device_id={"ed": sib},
            device_id_type=MESH,
        )

    def partial_copy(g, slot):
        return pltpu.make_async_remote_copy(
            src_ref=out_buf.at[g],
            dst_ref=in_buf.at[slot],
            send_sem=f_send.at[g],
            recv_sem=f_recv.at[slot],
            device_id={"fsdp": g},
            device_id_type=MESH,
        )

    barrier = pltpu.get_barrier_semaphore()

    def greet_fsdp(i, carry):
        pl.semaphore_signal(barrier, 1, device_id={"fsdp": fsdp_peer(i)}, device_id_type=MESH)
        return carry

    def greet_ed(i, carry):
        pl.semaphore_signal(barrier, 1, device_id={"ed": chip_peer(i) * 2 + core}, device_id_type=MESH)
        return carry

    lax.fori_loop(0, nf - 1, greet_fsdp, 0)
    lax.fori_loop(0, chips - 1, greet_ed, 0)
    pl.semaphore_signal(barrier, 1, device_id={"ed": sib}, device_id_type=MESH)
    pl.semaphore_wait(barrier, nf - 1 + chips)

    def send_slots(i, carry):
        direct(chip_peer(i)).start()
        return carry

    lax.fori_loop(0, chips - 1, send_slots, 0)
    to_sib = pltpu.make_async_remote_copy(
        src_ref=slot_ref,
        dst_ref=sel_buf.at[mine],
        send_sem=s_send,
        recv_sem=sel_recv.at[mine],
        device_id={"ed": sib},
        device_id_type=MESH,
    )
    to_sib.start()
    sel_buf[mine] = slot_ref[...]

    def band(i, carry):
        j = lax.rem(f + 1 + i, nf)
        for t in range(bands):
            blk = j * bands + t
            same_core = (blk // chips) == core
            not_mine = blk != mine

            @pl.when(same_core & not_mine)
            def _():
                forward(blk).wait_recv()
                forward(blk).start()

            @pl.when(jnp.logical_not(same_core))
            def _():
                forward(blk).wait_recv()

        for t in range(bands):
            blk = j * bands + t
            rows_in = sel_buf[blk]
            out_buf[j, t, :, :hidden] = jnp.dot(
                rows_in, wg_ref[...], preferred_element_type=jnp.float32
            ).astype(out_buf.dtype)
            out_buf[j, t, :, hidden:] = jnp.dot(
                rows_in, wu_ref[...], preferred_element_type=jnp.float32
            ).astype(out_buf.dtype)

        @pl.when(j != f)
        def _():
            partial_copy(j, f).start()

        return carry

    lax.fori_loop(0, nf, band, 0)
    acc[...] = out_buf[f].astype(jnp.float32)

    def gather(i, carry):
        g = fsdp_peer(i)
        partial_copy(g, f).wait_send()
        partial_copy(g, g).wait_recv()
        acc[...] += in_buf[g].astype(jnp.float32)
        return carry

    lax.fori_loop(0, nf - 1, gather, 0)

    def drain(i, carry):
        h = chip_peer(i)
        direct(h).wait_send()
        forward(core * chips + h).wait_send()
        return carry

    lax.fori_loop(0, chips - 1, drain, 0)
    to_sib.wait_send()
    total = acc[...]
    o_ref[...] = (jax.nn.silu(total[..., :hidden]) * total[..., hidden:]).astype(o_ref.dtype)


def slots_to_act(slots, wg, wu, nf, chips, cid):
    rows, d = slots.shape
    hidden = wg.shape[1]
    bands = 2 * chips // nf
    return pl.pallas_call(
        functools.partial(_up_kernel, nf, chips),
        out_shape=jax.ShapeDtypeStruct((bands, rows, hidden), jnp.bfloat16),
        in_specs=[pl.BlockSpec(memory_space=pltpu.VMEM)] * 3,
        out_specs=pl.BlockSpec(memory_space=pltpu.VMEM),
        scratch_shapes=[
            pltpu.VMEM((2 * chips, rows, d), jnp.bfloat16),
            pltpu.VMEM((nf, bands, rows, 2 * hidden), jnp.bfloat16),
            pltpu.VMEM((nf, bands, rows, 2 * hidden), jnp.bfloat16),
            pltpu.VMEM((bands, rows, 2 * hidden), jnp.float32),
            pltpu.SemaphoreType.DMA((chips,)),
            pltpu.SemaphoreType.DMA,
            pltpu.SemaphoreType.DMA((chips,)),
            pltpu.SemaphoreType.DMA((2 * chips,)),
            pltpu.SemaphoreType.DMA((nf,)),
            pltpu.SemaphoreType.DMA((nf,)),
        ],
        compiler_params=pltpu.CompilerParams(collective_id=cid, has_side_effects=True),
    )(slots, wg, wu)

def _layer_kernel(nf, chips, slot_ref, wg_ref, wu_ref, wd_ref, comb_ref, o_ref, *scratch):
    up_scratch, act_s, down_scratch, slot_out = scratch[:10], scratch[10], scratch[11:22], scratch[22]
    _up_kernel(nf, chips, slot_ref, wg_ref, wu_ref, act_s, *up_scratch)
    _down_kernel(nf, chips, act_s, wd_ref, slot_out, *down_scratch, greet=False)
    o_ref[...] = jnp.dot(
        comb_ref[...], slot_out[...], precision=lax.Precision.HIGHEST,
        preferred_element_type=jnp.float32,
    ).astype(o_ref.dtype)


def moe_layer(slots, wg, wu, wd, comb, nf, chips, cid):
    rows, d = slots.shape
    hidden = wg.shape[1]
    bands = 2 * chips // nf
    blocks = nf * bands
    tok = comb.shape[0]
    return pl.pallas_call(
        functools.partial(_layer_kernel, nf, chips),
        out_shape=jax.ShapeDtypeStruct((tok, d), jnp.bfloat16),
        in_specs=[pl.BlockSpec(memory_space=pltpu.VMEM)] * 5,
        out_specs=pl.BlockSpec(memory_space=pltpu.VMEM),
        scratch_shapes=[
            pltpu.VMEM((2 * chips, rows, d), jnp.bfloat16),
            pltpu.VMEM((nf, bands, rows, 2 * hidden), jnp.bfloat16),
            pltpu.VMEM((nf, bands, rows, 2 * hidden), jnp.bfloat16),
            pltpu.VMEM((bands, rows, 2 * hidden), jnp.float32),
            pltpu.SemaphoreType.DMA((chips,)),
            pltpu.SemaphoreType.DMA,
            pltpu.SemaphoreType.DMA((chips,)),
            pltpu.SemaphoreType.DMA((2 * chips,)),
            pltpu.SemaphoreType.DMA((nf,)),
            pltpu.SemaphoreType.DMA((nf,)),
            pltpu.VMEM((bands, rows, hidden), jnp.bfloat16),
            pltpu.VMEM((nf, bands, rows, hidden), jnp.bfloat16),
            pltpu.VMEM((blocks, rows, d), jnp.bfloat16),
            pltpu.VMEM((chips, rows, d), jnp.bfloat16),
            pltpu.VMEM((chips, rows, d), jnp.bfloat16),
            pltpu.VMEM((chips, rows, d), jnp.bfloat16),
            pltpu.SemaphoreType.DMA((nf,)),
            pltpu.SemaphoreType.DMA((nf,)),
            pltpu.SemaphoreType.DMA,
            pltpu.SemaphoreType.DMA,
            pltpu.SemaphoreType.DMA((chips,)),
            pltpu.SemaphoreType.DMA((chips,)),
            pltpu.VMEM((rows, d), jnp.float32),
        ],
        compiler_params=pltpu.CompilerParams(collective_id=cid, has_side_effects=True),
    )(slots, wg, wu, wd, comb)


def local(tokens, expert_ids, route_weights, w_gate, w_up, w_down):
    window = w_gate.shape[0]
    features_dev = tokens.shape[1]
    hidden_dev = w_gate.shape[2]
    n_ed = lax.axis_size("ed")
    n_fsdp = lax.axis_size("fsdp")
    chips = n_ed // 2
    per_band = n_ed // n_fsdp
    tok_dev = tokens.shape[0]
    order = jnp.arange(tok_dev, dtype=jnp.int32)
    routed = jnp.any(expert_ids == 0, axis=1)
    lower = (order[:, None] >= order[None, :]).astype(jnp.bfloat16)
    count = jnp.dot(lower, routed.astype(jnp.bfloat16), preferred_element_type=jnp.float32)
    slot_ids = jnp.arange(CAP, dtype=jnp.float32)
    match = routed[None, :] & (count[None, :] - 1.0 == slot_ids[:, None])
    own_slots = jnp.dot(
        match.astype(jnp.bfloat16), tokens, preferred_element_type=jnp.float32
    ).astype(jnp.bfloat16)
    per_expert = jnp.sum(
        jnp.where(expert_ids == 0, route_weights, jnp.zeros_like(route_weights)), axis=1
    )
    weights_matrix = match.T.astype(jnp.float32) * per_expert[:, None]
    return moe_layer(own_slots, w_gate[0], w_up[0], w_down[0], weights_matrix, n_fsdp, chips, 2)


def solution(mesh):
    return jax.shard_map(
        local,
        mesh=mesh,
        in_specs=(
            P("ed", "fsdp"),
            P("ed", None),
            P("ed", None),
            P(None, "fsdp", "ed"),
            P(None, "fsdp", "ed"),
            P(None, "ed", "fsdp"),
        ),
        out_specs=P("ed", "fsdp"),
        check_vma=False,
    )
```

```python
import functools

import jax
import jax.numpy as jnp
from jax import lax
from jax.experimental import pallas as pl
from jax.experimental.pallas import tpu as pltpu
from jax.sharding import PartitionSpec as P

CAP = 81
MESH = pl.DeviceIdType.MESH


def slot_match(routes, window, capacity):
    window_ids = jnp.arange(window, dtype=jnp.int32)
    routed = jnp.any(routes[:, :, None, :] == window_ids[None, None, :, None], axis=3)
    position = jnp.cumsum(routed.astype(jnp.int32), axis=1) - 1
    slot_ids = jnp.arange(capacity, dtype=jnp.int32)
    hits = routed[:, :, :, None] & (position[:, :, :, None] == slot_ids[None, None, None, :])
    return hits.astype(jnp.int32)


def take_block(block_rows, row_list):
    return jnp.take(block_rows, row_list, axis=0)


def pick_rows(blocks, routes, window, capacity):
    match = slot_match(routes, window, capacity)
    row_numbers = jnp.arange(blocks.shape[1], dtype=jnp.int32)
    source_row = jnp.sum(match * row_numbers[None, :, None, None], axis=1).reshape(
        blocks.shape[0], window * capacity
    )
    filled = jnp.sum(match, axis=1).reshape(blocks.shape[0], window * capacity)
    picked = jax.vmap(take_block)(blocks, source_row)
    picked = jnp.where(filled[:, :, None] > 0, picked, jnp.zeros_like(picked))
    return picked.reshape(blocks.shape[0], window, capacity, blocks.shape[2])


def combine_matrix(routes, weights, window, capacity):
    match = slot_match(routes[None], window, capacity)[0]
    window_ids = jnp.arange(window, dtype=jnp.int32)
    per_expert = jnp.sum(
        jnp.where(
            routes[:, None, :] == window_ids[None, :, None],
            weights[:, None, :],
            jnp.zeros_like(weights[:, None, :]),
        ),
        axis=2,
    )
    return (per_expert[:, :, None] * match.astype(weights.dtype)).reshape(
        routes.shape[0], window * capacity
    )


def _down_kernel(nf, chips, act_ref, wd_ref, o_ref, act_buf, term_buf, sib_buf, pre_buf, in_buf,
                 a_send, a_recv, s_send, s_recv, e_send, e_recv):
    bands = act_ref.shape[0]
    f = lax.axis_index("fsdp")
    e = lax.axis_index("ed")
    core = lax.rem(e, 2)
    chip = e // 2
    sib = e + 1 - 2 * core

    def fsdp_peer(i):
        return lax.rem(f + 1 + i, nf)

    def chip_peer(i):
        return lax.rem(chip + 1 + i, chips)

    def act_copy(g, slot):
        return pltpu.make_async_remote_copy(
            src_ref=act_ref,
            dst_ref=act_buf.at[slot],
            send_sem=a_send.at[g],
            recv_sem=a_recv.at[slot],
            device_id={"fsdp": g},
            device_id_type=MESH,
        )

    def to_sibling(blk):
        h = lax.rem(blk, chips)
        return pltpu.make_async_remote_copy(
            src_ref=term_buf.at[blk],
            dst_ref=sib_buf.at[h],
            send_sem=s_send.at[h],
            recv_sem=s_recv.at[h],
            device_id={"ed": sib},
            device_id_type=MESH,
        )

    def piece_copy(h, slot):
        return pltpu.make_async_remote_copy(
            src_ref=pre_buf.at[h],
            dst_ref=in_buf.at[slot],
            send_sem=e_send.at[h],
            recv_sem=e_recv.at[slot],
            device_id={"ed": h * 2 + core},
            device_id_type=MESH,
        )

    def send_act(i, carry):
        act_copy(fsdp_peer(i), f).start()
        return carry

    lax.fori_loop(0, nf - 1, send_act, 0)
    act_buf[f] = act_ref[...]
    o_ref[...] = jnp.zeros_like(o_ref)

    def band(i, carry):
        j = lax.rem(f + i, nf)

        @pl.when(i > 0)
        def _():
            act_copy(j, f).wait_send()
            act_copy(j, j).wait_recv()

        for t in range(bands):
            blk = j * bands + t
            h = lax.rem(blk, chips)
            term_buf[blk] = jnp.dot(
                act_buf[j, t], wd_ref[...], preferred_element_type=jnp.float32
            ).astype(term_buf.dtype)
            same_core = (blk // chips) == core

            @pl.when(jnp.logical_not(same_core))
            def _():
                to_sibling(blk).start()

            @pl.when(same_core)
            def _():
                to_sibling(blk).wait_recv()
                pair = term_buf[blk].astype(jnp.float32) + sib_buf[h].astype(jnp.float32)
                pre_buf[h] = pair.astype(pre_buf.dtype)

                @pl.when(h == chip)
                def _():
                    o_ref[...] += pre_buf[h].astype(jnp.float32)

                @pl.when(h != chip)
                def _():
                    piece_copy(h, chip).start()

        return carry

    lax.fori_loop(0, nf, band, 0)

    def take_piece(i, carry):
        h = chip_peer(i)
        piece_copy(h, chip).wait_send()
        piece_copy(h, h).wait_recv()
        o_ref[...] += in_buf[h].astype(jnp.float32)
        return carry

    lax.fori_loop(0, chips - 1, take_piece, 0)

    def drain(h, carry):
        to_sibling((1 - core) * chips + h).wait_send()
        return carry

    lax.fori_loop(0, chips, drain, 0)


def _up_kernel(nf, chips, slot_ref, wg_ref, wu_ref, o_ref, sel_buf, out_buf, in_buf, acc,
               e_send, s_send, fwd_send, sel_recv, f_send, f_recv):
    bands = o_ref.shape[0]
    hidden = o_ref.shape[2]
    f = lax.axis_index("fsdp")
    e = lax.axis_index("ed")
    core = lax.rem(e, 2)
    chip = e // 2
    sib = e + 1 - 2 * core
    mine = core * chips + chip

    def fsdp_peer(i):
        return lax.rem(f + 1 + i, nf)

    def chip_peer(i):
        return lax.rem(chip + 1 + i, chips)

    def direct(h):
        return pltpu.make_async_remote_copy(
            src_ref=slot_ref,
            dst_ref=sel_buf.at[mine],
            send_sem=e_send.at[h],
            recv_sem=sel_recv.at[mine],
            device_id={"ed": h * 2 + core},
            device_id_type=MESH,
        )

    def forward(blk):
        return pltpu.make_async_remote_copy(
            src_ref=sel_buf.at[blk],
            dst_ref=sel_buf.at[blk],
            send_sem=fwd_send.at[lax.rem(blk, chips)],
            recv_sem=sel_recv.at[blk],
            device_id={"ed": sib},
            device_id_type=MESH,
        )

    def partial_copy(g, slot):
        return pltpu.make_async_remote_copy(
            src_ref=out_buf.at[g],
            dst_ref=in_buf.at[slot],
            send_sem=f_send.at[g],
            recv_sem=f_recv.at[slot],
            device_id={"fsdp": g},
            device_id_type=MESH,
        )

    barrier = pltpu.get_barrier_semaphore()

    def greet_fsdp(i, carry):
        pl.semaphore_signal(barrier, 1, device_id={"fsdp": fsdp_peer(i)}, device_id_type=MESH)
        return carry

    def greet_ed(i, carry):
        pl.semaphore_signal(barrier, 1, device_id={"ed": chip_peer(i) * 2 + core}, device_id_type=MESH)
        return carry

    lax.fori_loop(0, nf - 1, greet_fsdp, 0)
    lax.fori_loop(0, chips - 1, greet_ed, 0)
    pl.semaphore_signal(barrier, 1, device_id={"ed": sib}, device_id_type=MESH)
    pl.semaphore_wait(barrier, nf - 1 + chips)

    def send_slots(i, carry):
        direct(chip_peer(i)).start()
        return carry

    lax.fori_loop(0, chips - 1, send_slots, 0)
    to_sib = pltpu.make_async_remote_copy(
        src_ref=slot_ref,
        dst_ref=sel_buf.at[mine],
        send_sem=s_send,
        recv_sem=sel_recv.at[mine],
        device_id={"ed": sib},
        device_id_type=MESH,
    )
    to_sib.start()
    sel_buf[mine] = slot_ref[...]

    def band(i, carry):
        j = lax.rem(f + 1 + i, nf)
        for t in range(bands):
            blk = j * bands + t
            same_core = (blk // chips) == core
            not_mine = blk != mine

            @pl.when(same_core & not_mine)
            def _():
                forward(blk).wait_recv()
                forward(blk).start()

            @pl.when(jnp.logical_not(same_core))
            def _():
                forward(blk).wait_recv()

        for t in range(bands):
            blk = j * bands + t
            rows_in = sel_buf[blk]
            out_buf[j, t, :, :hidden] = jnp.dot(
                rows_in, wg_ref[...], preferred_element_type=jnp.float32
            ).astype(out_buf.dtype)
            out_buf[j, t, :, hidden:] = jnp.dot(
                rows_in, wu_ref[...], preferred_element_type=jnp.float32
            ).astype(out_buf.dtype)

        @pl.when(j != f)
        def _():
            partial_copy(j, f).start()

        return carry

    lax.fori_loop(0, nf, band, 0)
    acc[...] = out_buf[f].astype(jnp.float32)

    def gather(i, carry):
        g = fsdp_peer(i)
        partial_copy(g, f).wait_send()
        partial_copy(g, g).wait_recv()
        acc[...] += in_buf[g].astype(jnp.float32)
        return carry

    lax.fori_loop(0, nf - 1, gather, 0)

    def drain(i, carry):
        h = chip_peer(i)
        direct(h).wait_send()
        forward(core * chips + h).wait_send()
        return carry

    lax.fori_loop(0, chips - 1, drain, 0)
    to_sib.wait_send()
    total = acc[...]
    o_ref[...] = (jax.nn.silu(total[..., :hidden]) * total[..., hidden:]).astype(o_ref.dtype)


def _layer_kernel(nf, chips, slot_ref, wg_ref, wu_ref, wd_ref, comb_ref, o_ref, *scratch):
    up_scratch, act_s, down_scratch, slot_out = scratch[:10], scratch[10], scratch[11:22], scratch[22]
    _up_kernel(nf, chips, slot_ref, wg_ref, wu_ref, act_s, *up_scratch)
    _down_kernel(nf, chips, act_s, wd_ref, slot_out, *down_scratch)
    o_ref[...] = jnp.dot(
        comb_ref[...], slot_out[...], precision=lax.Precision.HIGHEST,
        preferred_element_type=jnp.float32,
    ).astype(o_ref.dtype)


def moe_layer(slots, wg, wu, wd, comb, nf, chips, cid):
    rows, d = slots.shape
    hidden = wg.shape[1]
    bands = 2 * chips // nf
    blocks = nf * bands
    tok = comb.shape[0]
    return pl.pallas_call(
        functools.partial(_layer_kernel, nf, chips),
        out_shape=jax.ShapeDtypeStruct((tok, d), jnp.bfloat16),
        in_specs=[pl.BlockSpec(memory_space=pltpu.VMEM)] * 5,
        out_specs=pl.BlockSpec(memory_space=pltpu.VMEM),
        scratch_shapes=[
            pltpu.VMEM((2 * chips, rows, d), jnp.bfloat16),
            pltpu.VMEM((nf, bands, rows, 2 * hidden), jnp.bfloat16),
            pltpu.VMEM((nf, bands, rows, 2 * hidden), jnp.bfloat16),
            pltpu.VMEM((bands, rows, 2 * hidden), jnp.float32),
            pltpu.SemaphoreType.DMA((chips,)),
            pltpu.SemaphoreType.DMA,
            pltpu.SemaphoreType.DMA((chips,)),
            pltpu.SemaphoreType.DMA((2 * chips,)),
            pltpu.SemaphoreType.DMA((nf,)),
            pltpu.SemaphoreType.DMA((nf,)),
            pltpu.VMEM((bands, rows, hidden), jnp.bfloat16),
            pltpu.VMEM((nf, bands, rows, hidden), jnp.bfloat16),
            pltpu.VMEM((blocks, rows, d), jnp.bfloat16),
            pltpu.VMEM((chips, rows, d), jnp.bfloat16),
            pltpu.VMEM((chips, rows, d), jnp.bfloat16),
            pltpu.VMEM((chips, rows, d), jnp.bfloat16),
            pltpu.SemaphoreType.DMA((nf,)),
            pltpu.SemaphoreType.DMA((nf,)),
            pltpu.SemaphoreType.DMA((chips,)),
            pltpu.SemaphoreType.DMA((chips,)),
            pltpu.SemaphoreType.DMA((chips,)),
            pltpu.SemaphoreType.DMA((chips,)),
            pltpu.VMEM((rows, d), jnp.float32),
        ],
        compiler_params=pltpu.CompilerParams(collective_id=cid, has_side_effects=True),
    )(slots, wg, wu, wd, comb)


def local(tokens, expert_ids, route_weights, w_gate, w_up, w_down):
    window = w_gate.shape[0]
    features_dev = tokens.shape[1]
    hidden_dev = w_gate.shape[2]
    n_ed = lax.axis_size("ed")
    n_fsdp = lax.axis_size("fsdp")
    chips = n_ed // 2
    per_band = n_ed // n_fsdp
    tok_dev = tokens.shape[0]
    order = jnp.arange(tok_dev, dtype=jnp.int32)
    routed = jnp.any(expert_ids == 0, axis=1)
    lower = (order[:, None] >= order[None, :]).astype(jnp.bfloat16)
    count = jnp.dot(lower, routed.astype(jnp.bfloat16), preferred_element_type=jnp.float32)
    slot_ids = jnp.arange(CAP, dtype=jnp.float32)
    match = routed[None, :] & (count[None, :] - 1.0 == slot_ids[:, None])
    own_slots = jnp.dot(
        match.astype(jnp.bfloat16), tokens, preferred_element_type=jnp.float32
    ).astype(jnp.bfloat16)
    per_expert = jnp.sum(
        jnp.where(expert_ids == 0, route_weights, jnp.zeros_like(route_weights)), axis=1
    )
    weights_matrix = match.T.astype(jnp.float32) * per_expert[:, None]
    return moe_layer(own_slots, w_gate[0], w_up[0], w_down[0], weights_matrix, n_fsdp, chips, 2)


def solution(mesh):
    return jax.shard_map(
        local,
        mesh=mesh,
        in_specs=(
            P("ed", "fsdp"),
            P("ed", None),
            P("ed", None),
            P(None, "fsdp", "ed"),
            P(None, "fsdp", "ed"),
            P(None, "ed", "fsdp"),
        ),
        out_specs=P("ed", "fsdp"),
        check_vma=False,
    )
```

```python
import functools

import jax
import jax.numpy as jnp
from jax import lax
from jax.experimental import pallas as pl
from jax.experimental.pallas import tpu as pltpu
from jax.sharding import PartitionSpec as P

CAP = 81
MESH = pl.DeviceIdType.MESH


def slot_match(routes, window, capacity):
    window_ids = jnp.arange(window, dtype=jnp.int32)
    routed = jnp.any(routes[:, :, None, :] == window_ids[None, None, :, None], axis=3)
    position = jnp.cumsum(routed.astype(jnp.int32), axis=1) - 1
    slot_ids = jnp.arange(capacity, dtype=jnp.int32)
    hits = routed[:, :, :, None] & (position[:, :, :, None] == slot_ids[None, None, None, :])
    return hits.astype(jnp.int32)


def take_block(block_rows, row_list):
    return jnp.take(block_rows, row_list, axis=0)


def pick_rows(blocks, routes, window, capacity):
    match = slot_match(routes, window, capacity)
    row_numbers = jnp.arange(blocks.shape[1], dtype=jnp.int32)
    source_row = jnp.sum(match * row_numbers[None, :, None, None], axis=1).reshape(
        blocks.shape[0], window * capacity
    )
    filled = jnp.sum(match, axis=1).reshape(blocks.shape[0], window * capacity)
    picked = jax.vmap(take_block)(blocks, source_row)
    picked = jnp.where(filled[:, :, None] > 0, picked, jnp.zeros_like(picked))
    return picked.reshape(blocks.shape[0], window, capacity, blocks.shape[2])


def combine_matrix(routes, weights, window, capacity):
    match = slot_match(routes[None], window, capacity)[0]
    window_ids = jnp.arange(window, dtype=jnp.int32)
    per_expert = jnp.sum(
        jnp.where(
            routes[:, None, :] == window_ids[None, :, None],
            weights[:, None, :],
            jnp.zeros_like(weights[:, None, :]),
        ),
        axis=2,
    )
    return (per_expert[:, :, None] * match.astype(weights.dtype)).reshape(
        routes.shape[0], window * capacity
    )


def _down_kernel(nf, chips, act_ref, wd_ref, o_ref, act_buf, term_buf, sib_buf, pre_buf, in_buf,
                 a_send, a_recv, s_send, s_recv, e_send, e_recv):
    bands = act_ref.shape[0]
    f = lax.axis_index("fsdp")
    e = lax.axis_index("ed")
    core = lax.rem(e, 2)
    chip = e // 2
    sib = e + 1 - 2 * core

    def fsdp_peer(i):
        return lax.rem(f + 1 + i, nf)

    def chip_peer(i):
        return lax.rem(chip + 1 + i, chips)

    def act_copy(g, slot):
        return pltpu.make_async_remote_copy(
            src_ref=act_ref,
            dst_ref=act_buf.at[slot],
            send_sem=a_send.at[g],
            recv_sem=a_recv.at[slot],
            device_id={"fsdp": g},
            device_id_type=MESH,
        )

    def to_sibling(blk):
        h = lax.rem(blk, chips)
        return pltpu.make_async_remote_copy(
            src_ref=term_buf.at[blk],
            dst_ref=sib_buf.at[h],
            send_sem=s_send.at[h],
            recv_sem=s_recv.at[h],
            device_id={"ed": sib},
            device_id_type=MESH,
        )

    def piece_copy(h, slot):
        return pltpu.make_async_remote_copy(
            src_ref=pre_buf.at[h],
            dst_ref=in_buf.at[slot],
            send_sem=e_send.at[h],
            recv_sem=e_recv.at[slot],
            device_id={"ed": h * 2 + core},
            device_id_type=MESH,
        )

    shift = nf - lax.rem(chip, nf)

    def send_act(i, carry):
        g = lax.rem(f + shift + nf - i, nf)

        @pl.when(g != f)
        def _():
            act_copy(g, f).start()

        return carry

    lax.fori_loop(0, nf, send_act, 0)
    act_buf[f] = act_ref[...]
    o_ref[...] = jnp.zeros_like(o_ref)

    def band(i, carry):
        j = lax.rem(f + chip + i, nf)

        @pl.when(j != f)
        def _():
            act_copy(j, f).wait_send()
            act_copy(j, j).wait_recv()

        for t in range(bands):
            blk = j * bands + t
            h = lax.rem(blk, chips)
            term_buf[blk] = jnp.dot(
                act_buf[j, t], wd_ref[...], preferred_element_type=jnp.float32
            ).astype(term_buf.dtype)
            same_core = (blk // chips) == core

            @pl.when(jnp.logical_not(same_core))
            def _():
                to_sibling(blk).start()

            @pl.when(same_core)
            def _():
                to_sibling(blk).wait_recv()
                pair = term_buf[blk].astype(jnp.float32) + sib_buf[h].astype(jnp.float32)
                pre_buf[h] = pair.astype(pre_buf.dtype)

                @pl.when(h == chip)
                def _():
                    o_ref[...] += pre_buf[h].astype(jnp.float32)

                @pl.when(h != chip)
                def _():
                    piece_copy(h, chip).start()

        return carry

    lax.fori_loop(0, nf, band, 0)

    def take_piece(i, carry):
        h = chip_peer(i)
        piece_copy(h, chip).wait_send()
        piece_copy(h, h).wait_recv()
        o_ref[...] += in_buf[h].astype(jnp.float32)
        return carry

    lax.fori_loop(0, chips - 1, take_piece, 0)

    def drain(h, carry):
        to_sibling((1 - core) * chips + h).wait_send()
        return carry

    lax.fori_loop(0, chips, drain, 0)


def _up_kernel(nf, chips, slot_ref, wg_ref, wu_ref, o_ref, sel_buf, out_buf, in_buf, acc,
               e_send, s_send, fwd_send, sel_recv, f_send, f_recv):
    bands = o_ref.shape[0]
    hidden = o_ref.shape[2]
    f = lax.axis_index("fsdp")
    e = lax.axis_index("ed")
    core = lax.rem(e, 2)
    chip = e // 2
    sib = e + 1 - 2 * core
    mine = core * chips + chip

    def fsdp_peer(i):
        return lax.rem(f + 1 + i, nf)

    def chip_peer(i):
        return lax.rem(chip + 1 + i, chips)

    def direct(h):
        return pltpu.make_async_remote_copy(
            src_ref=slot_ref,
            dst_ref=sel_buf.at[mine],
            send_sem=e_send.at[h],
            recv_sem=sel_recv.at[mine],
            device_id={"ed": h * 2 + core},
            device_id_type=MESH,
        )

    def forward(blk):
        return pltpu.make_async_remote_copy(
            src_ref=sel_buf.at[blk],
            dst_ref=sel_buf.at[blk],
            send_sem=fwd_send.at[lax.rem(blk, chips)],
            recv_sem=sel_recv.at[blk],
            device_id={"ed": sib},
            device_id_type=MESH,
        )

    def partial_copy(g, slot):
        return pltpu.make_async_remote_copy(
            src_ref=out_buf.at[g],
            dst_ref=in_buf.at[slot],
            send_sem=f_send.at[g],
            recv_sem=f_recv.at[slot],
            device_id={"fsdp": g},
            device_id_type=MESH,
        )

    barrier = pltpu.get_barrier_semaphore()

    def greet_fsdp(i, carry):
        pl.semaphore_signal(barrier, 1, device_id={"fsdp": fsdp_peer(i)}, device_id_type=MESH)
        return carry

    def greet_ed(i, carry):
        pl.semaphore_signal(barrier, 1, device_id={"ed": chip_peer(i) * 2 + core}, device_id_type=MESH)
        return carry

    lax.fori_loop(0, nf - 1, greet_fsdp, 0)
    lax.fori_loop(0, chips - 1, greet_ed, 0)
    pl.semaphore_signal(barrier, 1, device_id={"ed": sib}, device_id_type=MESH)
    pl.semaphore_wait(barrier, nf - 1 + chips)

    def send_slots(i, carry):
        direct(chip_peer(i)).start()
        return carry

    lax.fori_loop(0, chips - 1, send_slots, 0)
    to_sib = pltpu.make_async_remote_copy(
        src_ref=slot_ref,
        dst_ref=sel_buf.at[mine],
        send_sem=s_send,
        recv_sem=sel_recv.at[mine],
        device_id={"ed": sib},
        device_id_type=MESH,
    )
    to_sib.start()
    sel_buf[mine] = slot_ref[...]

    def band(i, carry):
        j = lax.rem(f + 1 + i, nf)
        for t in range(bands):
            blk = j * bands + t
            same_core = (blk // chips) == core
            not_mine = blk != mine

            @pl.when(same_core & not_mine)
            def _():
                forward(blk).wait_recv()
                forward(blk).start()

            @pl.when(jnp.logical_not(same_core))
            def _():
                forward(blk).wait_recv()

        for t in range(bands):
            blk = j * bands + t
            rows_in = sel_buf[blk]
            out_buf[j, t, :, :hidden] = jnp.dot(
                rows_in, wg_ref[...], preferred_element_type=jnp.float32
            ).astype(out_buf.dtype)
            out_buf[j, t, :, hidden:] = jnp.dot(
                rows_in, wu_ref[...], preferred_element_type=jnp.float32
            ).astype(out_buf.dtype)

        @pl.when(j != f)
        def _():
            partial_copy(j, f).start()

        return carry

    lax.fori_loop(0, nf, band, 0)
    acc[...] = out_buf[f].astype(jnp.float32)

    def gather(i, carry):
        g = fsdp_peer(i)
        partial_copy(g, f).wait_send()
        partial_copy(g, g).wait_recv()
        acc[...] += in_buf[g].astype(jnp.float32)
        return carry

    lax.fori_loop(0, nf - 1, gather, 0)

    def drain(i, carry):
        h = chip_peer(i)
        direct(h).wait_send()
        forward(core * chips + h).wait_send()
        return carry

    lax.fori_loop(0, chips - 1, drain, 0)
    to_sib.wait_send()
    total = acc[...]
    o_ref[...] = (jax.nn.silu(total[..., :hidden]) * total[..., hidden:]).astype(o_ref.dtype)


def _layer_kernel(nf, chips, slot_ref, wg_ref, wu_ref, wd_ref, comb_ref, o_ref, *scratch):
    up_scratch, act_s, down_scratch, slot_out = scratch[:10], scratch[10], scratch[11:22], scratch[22]
    _up_kernel(nf, chips, slot_ref, wg_ref, wu_ref, act_s, *up_scratch)
    _down_kernel(nf, chips, act_s, wd_ref, slot_out, *down_scratch)
    o_ref[...] = jnp.dot(
        comb_ref[...], slot_out[...], precision=lax.Precision.HIGHEST,
        preferred_element_type=jnp.float32,
    ).astype(o_ref.dtype)


def moe_layer(slots, wg, wu, wd, comb, nf, chips, cid):
    rows, d = slots.shape
    hidden = wg.shape[1]
    bands = 2 * chips // nf
    blocks = nf * bands
    tok = comb.shape[0]
    return pl.pallas_call(
        functools.partial(_layer_kernel, nf, chips),
        out_shape=jax.ShapeDtypeStruct((tok, d), jnp.bfloat16),
        in_specs=[pl.BlockSpec(memory_space=pltpu.VMEM)] * 5,
        out_specs=pl.BlockSpec(memory_space=pltpu.VMEM),
        scratch_shapes=[
            pltpu.VMEM((2 * chips, rows, d), jnp.bfloat16),
            pltpu.VMEM((nf, bands, rows, 2 * hidden), jnp.bfloat16),
            pltpu.VMEM((nf, bands, rows, 2 * hidden), jnp.bfloat16),
            pltpu.VMEM((bands, rows, 2 * hidden), jnp.float32),
            pltpu.SemaphoreType.DMA((chips,)),
            pltpu.SemaphoreType.DMA,
            pltpu.SemaphoreType.DMA((chips,)),
            pltpu.SemaphoreType.DMA((2 * chips,)),
            pltpu.SemaphoreType.DMA((nf,)),
            pltpu.SemaphoreType.DMA((nf,)),
            pltpu.VMEM((bands, rows, hidden), jnp.bfloat16),
            pltpu.VMEM((nf, bands, rows, hidden), jnp.bfloat16),
            pltpu.VMEM((blocks, rows, d), jnp.bfloat16),
            pltpu.VMEM((chips, rows, d), jnp.bfloat16),
            pltpu.VMEM((chips, rows, d), jnp.bfloat16),
            pltpu.VMEM((chips, rows, d), jnp.bfloat16),
            pltpu.SemaphoreType.DMA((nf,)),
            pltpu.SemaphoreType.DMA((nf,)),
            pltpu.SemaphoreType.DMA((chips,)),
            pltpu.SemaphoreType.DMA((chips,)),
            pltpu.SemaphoreType.DMA((chips,)),
            pltpu.SemaphoreType.DMA((chips,)),
            pltpu.VMEM((rows, d), jnp.float32),
        ],
        compiler_params=pltpu.CompilerParams(collective_id=cid, has_side_effects=True),
    )(slots, wg, wu, wd, comb)


def local(tokens, expert_ids, route_weights, w_gate, w_up, w_down):
    window = w_gate.shape[0]
    features_dev = tokens.shape[1]
    hidden_dev = w_gate.shape[2]
    n_ed = lax.axis_size("ed")
    n_fsdp = lax.axis_size("fsdp")
    chips = n_ed // 2
    per_band = n_ed // n_fsdp
    tok_dev = tokens.shape[0]
    order = jnp.arange(tok_dev, dtype=jnp.int32)
    routed = jnp.any(expert_ids == 0, axis=1)
    lower = (order[:, None] >= order[None, :]).astype(jnp.bfloat16)
    count = jnp.dot(lower, routed.astype(jnp.bfloat16), preferred_element_type=jnp.float32)
    slot_ids = jnp.arange(CAP, dtype=jnp.float32)
    match = routed[None, :] & (count[None, :] - 1.0 == slot_ids[:, None])
    own_slots = jnp.dot(
        match.astype(jnp.bfloat16), tokens, preferred_element_type=jnp.float32
    ).astype(jnp.bfloat16)
    per_expert = jnp.sum(
        jnp.where(expert_ids == 0, route_weights, jnp.zeros_like(route_weights)), axis=1
    )
    weights_matrix = match.T.astype(jnp.float32) * per_expert[:, None]
    return moe_layer(own_slots, w_gate[0], w_up[0], w_down[0], weights_matrix, n_fsdp, chips, 2)


def solution(mesh):
    return jax.shard_map(
        local,
        mesh=mesh,
        in_specs=(
            P("ed", "fsdp"),
            P("ed", None),
            P("ed", None),
            P(None, "fsdp", "ed"),
            P(None, "fsdp", "ed"),
            P(None, "ed", "fsdp"),
        ),
        out_specs=P("ed", "fsdp"),
        check_vma=False,
    )
```

```python
import functools

import jax
import jax.numpy as jnp
from jax import lax
from jax.experimental import pallas as pl
from jax.experimental.pallas import tpu as pltpu
from jax.sharding import PartitionSpec as P

CAP = 81
MESH = pl.DeviceIdType.MESH


def slot_match(routes, window, capacity):
    window_ids = jnp.arange(window, dtype=jnp.int32)
    routed = jnp.any(routes[:, :, None, :] == window_ids[None, None, :, None], axis=3)
    position = jnp.cumsum(routed.astype(jnp.int32), axis=1) - 1
    slot_ids = jnp.arange(capacity, dtype=jnp.int32)
    hits = routed[:, :, :, None] & (position[:, :, :, None] == slot_ids[None, None, None, :])
    return hits.astype(jnp.int32)


def take_block(block_rows, row_list):
    return jnp.take(block_rows, row_list, axis=0)


def pick_rows(blocks, routes, window, capacity):
    match = slot_match(routes, window, capacity)
    row_numbers = jnp.arange(blocks.shape[1], dtype=jnp.int32)
    source_row = jnp.sum(match * row_numbers[None, :, None, None], axis=1).reshape(
        blocks.shape[0], window * capacity
    )
    filled = jnp.sum(match, axis=1).reshape(blocks.shape[0], window * capacity)
    picked = jax.vmap(take_block)(blocks, source_row)
    picked = jnp.where(filled[:, :, None] > 0, picked, jnp.zeros_like(picked))
    return picked.reshape(blocks.shape[0], window, capacity, blocks.shape[2])


def combine_matrix(routes, weights, window, capacity):
    match = slot_match(routes[None], window, capacity)[0]
    window_ids = jnp.arange(window, dtype=jnp.int32)
    per_expert = jnp.sum(
        jnp.where(
            routes[:, None, :] == window_ids[None, :, None],
            weights[:, None, :],
            jnp.zeros_like(weights[:, None, :]),
        ),
        axis=2,
    )
    return (per_expert[:, :, None] * match.astype(weights.dtype)).reshape(
        routes.shape[0], window * capacity
    )


def _down_kernel(nf, chips, act_ref, wd_ref, o_ref, act_buf, term_buf, sib_buf, pre_buf, in_buf,
                 a_send, a_recv, s_send, s_recv, e_send, e_recv):
    bands = act_ref.shape[0]
    f = lax.axis_index("fsdp")
    e = lax.axis_index("ed")
    core = lax.rem(e, 2)
    chip = e // 2
    sib = e + 1 - 2 * core

    def fsdp_peer(i):
        return lax.rem(f + 1 + i, nf)

    def chip_peer(i):
        return lax.rem(chip + 1 + i, chips)

    def act_copy(g, slot):
        return pltpu.make_async_remote_copy(
            src_ref=act_ref,
            dst_ref=act_buf.at[slot],
            send_sem=a_send.at[g],
            recv_sem=a_recv.at[slot],
            device_id={"fsdp": g},
            device_id_type=MESH,
        )

    def to_sibling(blk):
        h = lax.rem(blk, chips)
        return pltpu.make_async_remote_copy(
            src_ref=term_buf.at[blk],
            dst_ref=sib_buf.at[h],
            send_sem=s_send.at[h],
            recv_sem=s_recv.at[h],
            device_id={"ed": sib},
            device_id_type=MESH,
        )

    def piece_copy(h, slot):
        return pltpu.make_async_remote_copy(
            src_ref=pre_buf.at[h],
            dst_ref=in_buf.at[slot],
            send_sem=e_send.at[h],
            recv_sem=e_recv.at[slot],
            device_id={"ed": h * 2 + core},
            device_id_type=MESH,
        )

    shift = nf - lax.rem(chip, nf)

    def send_act(i, carry):
        g = lax.rem(f + shift + nf - i, nf)

        @pl.when(g != f)
        def _():
            act_copy(g, f).start()

        return carry

    lax.fori_loop(0, nf, send_act, 0)
    act_buf[f] = act_ref[...]
    o_ref[...] = jnp.zeros_like(o_ref)

    def band(i, carry):
        j = lax.rem(f + chip + i, nf)

        @pl.when(j != f)
        def _():
            act_copy(j, f).wait_send()
            act_copy(j, j).wait_recv()

        for t in range(bands):
            blk = j * bands + t
            h = lax.rem(blk, chips)
            term_buf[blk] = jnp.dot(
                act_buf[j, t], wd_ref[...], preferred_element_type=jnp.float32
            ).astype(term_buf.dtype)
            same_core = (blk // chips) == core

            @pl.when(jnp.logical_not(same_core))
            def _():
                to_sibling(blk).start()

            @pl.when(same_core)
            def _():
                to_sibling(blk).wait_recv()
                pair = term_buf[blk].astype(jnp.float32) + sib_buf[h].astype(jnp.float32)
                pre_buf[h] = pair.astype(pre_buf.dtype)

                @pl.when(h == chip)
                def _():
                    o_ref[...] += pre_buf[h].astype(jnp.float32)

                @pl.when(h != chip)
                def _():
                    piece_copy(h, chip).start()

        return carry

    lax.fori_loop(0, nf, band, 0)

    def take_piece(i, carry):
        h = chip_peer(i)
        piece_copy(h, chip).wait_send()
        piece_copy(h, h).wait_recv()
        o_ref[...] += in_buf[h].astype(jnp.float32)
        return carry

    lax.fori_loop(0, chips - 1, take_piece, 0)

    def drain(h, carry):
        to_sibling((1 - core) * chips + h).wait_send()
        return carry

    lax.fori_loop(0, chips, drain, 0)


def _up_kernel(nf, chips, slot_ref, wg_ref, wu_ref, o_ref, sel_buf, out_buf, in_buf, acc,
               e_send, s_send, fwd_send, sel_recv, f_send, f_recv):
    bands = o_ref.shape[0]
    hidden = o_ref.shape[2]
    f = lax.axis_index("fsdp")
    e = lax.axis_index("ed")
    core = lax.rem(e, 2)
    chip = e // 2
    sib = e + 1 - 2 * core
    mine = core * chips + chip

    def fsdp_peer(i):
        return lax.rem(f + 1 + i, nf)

    def chip_peer(i):
        return lax.rem(chip + 1 + i, chips)

    def direct(h):
        return pltpu.make_async_remote_copy(
            src_ref=slot_ref,
            dst_ref=sel_buf.at[mine],
            send_sem=e_send.at[h],
            recv_sem=sel_recv.at[mine],
            device_id={"ed": h * 2 + core},
            device_id_type=MESH,
        )

    def forward(blk):
        return pltpu.make_async_remote_copy(
            src_ref=sel_buf.at[blk],
            dst_ref=sel_buf.at[blk],
            send_sem=fwd_send.at[lax.rem(blk, chips)],
            recv_sem=sel_recv.at[blk],
            device_id={"ed": sib},
            device_id_type=MESH,
        )

    def partial_copy(g, slot):
        return pltpu.make_async_remote_copy(
            src_ref=out_buf.at[g],
            dst_ref=in_buf.at[slot],
            send_sem=f_send.at[g],
            recv_sem=f_recv.at[slot],
            device_id={"fsdp": g},
            device_id_type=MESH,
        )

    barrier = pltpu.get_barrier_semaphore()

    def greet_fsdp(i, carry):
        pl.semaphore_signal(barrier, 1, device_id={"fsdp": fsdp_peer(i)}, device_id_type=MESH)
        return carry

    def greet_ed(i, carry):
        pl.semaphore_signal(barrier, 1, device_id={"ed": chip_peer(i) * 2 + core}, device_id_type=MESH)
        return carry

    lax.fori_loop(0, nf - 1, greet_fsdp, 0)
    lax.fori_loop(0, chips - 1, greet_ed, 0)
    pl.semaphore_signal(barrier, 1, device_id={"ed": sib}, device_id_type=MESH)
    pl.semaphore_wait(barrier, nf - 1 + chips)

    own_band = mine // bands
    lift = chips * ((nf + 2 * chips) // chips)

    def send_slots(k, carry):
        h = lax.rem(own_band - f - 1 - k + lift, chips)

        @pl.when(h != chip)
        def _():
            direct(h).start()

        return carry

    to_sib = pltpu.make_async_remote_copy(
        src_ref=slot_ref,
        dst_ref=sel_buf.at[mine],
        send_sem=s_send,
        recv_sem=sel_recv.at[mine],
        device_id={"ed": sib},
        device_id_type=MESH,
    )
    to_sib.start()
    lax.fori_loop(0, chips, send_slots, 0)
    sel_buf[mine] = slot_ref[...]

    def band(i, carry):
        j = lax.rem(f + chip + 1 + i, nf)
        for t in range(bands):
            blk = j * bands + t
            same_core = (blk // chips) == core
            not_mine = blk != mine

            @pl.when(same_core & not_mine)
            def _():
                forward(blk).wait_recv()
                forward(blk).start()

            @pl.when(jnp.logical_not(same_core))
            def _():
                forward(blk).wait_recv()

        for t in range(bands):
            blk = j * bands + t
            rows_in = sel_buf[blk]
            out_buf[j, t, :, :hidden] = jnp.dot(
                rows_in, wg_ref[...], preferred_element_type=jnp.float32
            ).astype(out_buf.dtype)
            out_buf[j, t, :, hidden:] = jnp.dot(
                rows_in, wu_ref[...], preferred_element_type=jnp.float32
            ).astype(out_buf.dtype)

        @pl.when(j != f)
        def _():
            partial_copy(j, f).start()

        return carry

    lax.fori_loop(0, nf, band, 0)
    acc[...] = out_buf[f].astype(jnp.float32)

    lift_f = nf * ((chips + 2 * nf) // nf)

    def gather(i, carry):
        g = lax.rem(f - chip - 1 - i + lift_f, nf)

        @pl.when(g != f)
        def _():
            partial_copy(g, f).wait_send()
            partial_copy(g, g).wait_recv()
            acc[...] += in_buf[g].astype(jnp.float32)

        return carry

    lax.fori_loop(0, nf, gather, 0)

    def drain(i, carry):
        h = chip_peer(i)
        direct(h).wait_send()
        forward(core * chips + h).wait_send()
        return carry

    lax.fori_loop(0, chips - 1, drain, 0)
    to_sib.wait_send()
    total = acc[...]
    o_ref[...] = (jax.nn.silu(total[..., :hidden]) * total[..., hidden:]).astype(o_ref.dtype)


def _layer_kernel(nf, chips, slot_ref, wg_ref, wu_ref, wd_ref, comb_ref, o_ref, *scratch):
    up_scratch, act_s, down_scratch, slot_out = scratch[:10], scratch[10], scratch[11:22], scratch[22]
    _up_kernel(nf, chips, slot_ref, wg_ref, wu_ref, act_s, *up_scratch)
    _down_kernel(nf, chips, act_s, wd_ref, slot_out, *down_scratch)
    o_ref[...] = jnp.dot(
        comb_ref[...], slot_out[...], precision=lax.Precision.HIGHEST,
        preferred_element_type=jnp.float32,
    ).astype(o_ref.dtype)


def moe_layer(slots, wg, wu, wd, comb, nf, chips, cid):
    rows, d = slots.shape
    hidden = wg.shape[1]
    bands = 2 * chips // nf
    blocks = nf * bands
    tok = comb.shape[0]
    return pl.pallas_call(
        functools.partial(_layer_kernel, nf, chips),
        out_shape=jax.ShapeDtypeStruct((tok, d), jnp.bfloat16),
        in_specs=[pl.BlockSpec(memory_space=pltpu.VMEM)] * 5,
        out_specs=pl.BlockSpec(memory_space=pltpu.VMEM),
        scratch_shapes=[
            pltpu.VMEM((2 * chips, rows, d), jnp.bfloat16),
            pltpu.VMEM((nf, bands, rows, 2 * hidden), jnp.bfloat16),
            pltpu.VMEM((nf, bands, rows, 2 * hidden), jnp.bfloat16),
            pltpu.VMEM((bands, rows, 2 * hidden), jnp.float32),
            pltpu.SemaphoreType.DMA((chips,)),
            pltpu.SemaphoreType.DMA,
            pltpu.SemaphoreType.DMA((chips,)),
            pltpu.SemaphoreType.DMA((2 * chips,)),
            pltpu.SemaphoreType.DMA((nf,)),
            pltpu.SemaphoreType.DMA((nf,)),
            pltpu.VMEM((bands, rows, hidden), jnp.bfloat16),
            pltpu.VMEM((nf, bands, rows, hidden), jnp.bfloat16),
            pltpu.VMEM((blocks, rows, d), jnp.bfloat16),
            pltpu.VMEM((chips, rows, d), jnp.bfloat16),
            pltpu.VMEM((chips, rows, d), jnp.bfloat16),
            pltpu.VMEM((chips, rows, d), jnp.bfloat16),
            pltpu.SemaphoreType.DMA((nf,)),
            pltpu.SemaphoreType.DMA((nf,)),
            pltpu.SemaphoreType.DMA((chips,)),
            pltpu.SemaphoreType.DMA((chips,)),
            pltpu.SemaphoreType.DMA((chips,)),
            pltpu.SemaphoreType.DMA((chips,)),
            pltpu.VMEM((rows, d), jnp.float32),
        ],
        compiler_params=pltpu.CompilerParams(collective_id=cid, has_side_effects=True),
    )(slots, wg, wu, wd, comb)


def local(tokens, expert_ids, route_weights, w_gate, w_up, w_down):
    window = w_gate.shape[0]
    features_dev = tokens.shape[1]
    hidden_dev = w_gate.shape[2]
    n_ed = lax.axis_size("ed")
    n_fsdp = lax.axis_size("fsdp")
    chips = n_ed // 2
    per_band = n_ed // n_fsdp
    tok_dev = tokens.shape[0]
    order = jnp.arange(tok_dev, dtype=jnp.int32)
    routed = jnp.any(expert_ids == 0, axis=1)
    lower = (order[:, None] >= order[None, :]).astype(jnp.bfloat16)
    count = jnp.dot(lower, routed.astype(jnp.bfloat16), preferred_element_type=jnp.float32)
    slot_ids = jnp.arange(CAP, dtype=jnp.float32)
    match = routed[None, :] & (count[None, :] - 1.0 == slot_ids[:, None])
    own_slots = jnp.dot(
        match.astype(jnp.bfloat16), tokens, preferred_element_type=jnp.float32
    ).astype(jnp.bfloat16)
    per_expert = jnp.sum(
        jnp.where(expert_ids == 0, route_weights, jnp.zeros_like(route_weights)), axis=1
    )
    weights_matrix = match.T.astype(jnp.float32) * per_expert[:, None]
    return moe_layer(own_slots, w_gate[0], w_up[0], w_down[0], weights_matrix, n_fsdp, chips, 2)


def solution(mesh):
    return jax.shard_map(
        local,
        mesh=mesh,
        in_specs=(
            P("ed", "fsdp"),
            P("ed", None),
            P("ed", None),
            P(None, "fsdp", "ed"),
            P(None, "fsdp", "ed"),
            P(None, "ed", "fsdp"),
        ),
        out_specs=P("ed", "fsdp"),
        check_vma=False,
    )
```

```python
import functools

import jax
import jax.numpy as jnp
from jax import lax
from jax.experimental import pallas as pl
from jax.experimental.pallas import tpu as pltpu
from jax.sharding import PartitionSpec as P

CAP = 81
MESH = pl.DeviceIdType.MESH


def slot_match(routes, window, capacity):
    window_ids = jnp.arange(window, dtype=jnp.int32)
    routed = jnp.any(routes[:, :, None, :] == window_ids[None, None, :, None], axis=3)
    position = jnp.cumsum(routed.astype(jnp.int32), axis=1) - 1
    slot_ids = jnp.arange(capacity, dtype=jnp.int32)
    hits = routed[:, :, :, None] & (position[:, :, :, None] == slot_ids[None, None, None, :])
    return hits.astype(jnp.int32)


def take_block(block_rows, row_list):
    return jnp.take(block_rows, row_list, axis=0)


def pick_rows(blocks, routes, window, capacity):
    match = slot_match(routes, window, capacity)
    row_numbers = jnp.arange(blocks.shape[1], dtype=jnp.int32)
    source_row = jnp.sum(match * row_numbers[None, :, None, None], axis=1).reshape(
        blocks.shape[0], window * capacity
    )
    filled = jnp.sum(match, axis=1).reshape(blocks.shape[0], window * capacity)
    picked = jax.vmap(take_block)(blocks, source_row)
    picked = jnp.where(filled[:, :, None] > 0, picked, jnp.zeros_like(picked))
    return picked.reshape(blocks.shape[0], window, capacity, blocks.shape[2])


def combine_matrix(routes, weights, window, capacity):
    match = slot_match(routes[None], window, capacity)[0]
    window_ids = jnp.arange(window, dtype=jnp.int32)
    per_expert = jnp.sum(
        jnp.where(
            routes[:, None, :] == window_ids[None, :, None],
            weights[:, None, :],
            jnp.zeros_like(weights[:, None, :]),
        ),
        axis=2,
    )
    return (per_expert[:, :, None] * match.astype(weights.dtype)).reshape(
        routes.shape[0], window * capacity
    )


def _down_kernel(nf, chips, act_ref, wd_ref, o_ref, act_buf, term_buf, sib_buf, pre_buf, in_buf,
                 a_send, a_recv, s_send, s_recv, e_send, e_recv):
    bands = act_ref.shape[0]
    f = lax.axis_index("fsdp")
    e = lax.axis_index("ed")
    core = lax.rem(e, 2)
    chip = e // 2
    sib = e + 1 - 2 * core

    def fsdp_peer(i):
        return lax.rem(f + 1 + i, nf)

    def chip_peer(i):
        return lax.rem(chip + 1 + i, chips)

    def act_copy(g, slot):
        return pltpu.make_async_remote_copy(
            src_ref=act_ref,
            dst_ref=act_buf.at[slot],
            send_sem=a_send.at[g],
            recv_sem=a_recv.at[slot],
            device_id={"fsdp": g},
            device_id_type=MESH,
        )

    def to_sibling(blk):
        h = lax.rem(blk, chips)
        return pltpu.make_async_remote_copy(
            src_ref=term_buf.at[blk],
            dst_ref=sib_buf.at[h],
            send_sem=s_send.at[h],
            recv_sem=s_recv.at[h],
            device_id={"ed": sib},
            device_id_type=MESH,
        )

    def piece_copy(h, slot):
        return pltpu.make_async_remote_copy(
            src_ref=pre_buf.at[h],
            dst_ref=in_buf.at[slot],
            send_sem=e_send.at[h],
            recv_sem=e_recv.at[slot],
            device_id={"ed": h * 2 + core},
            device_id_type=MESH,
        )

    shift = nf - lax.rem(chip, nf)

    def send_act(i, carry):
        g = lax.rem(f + shift + nf - i, nf)

        @pl.when(g != f)
        def _():
            act_copy(g, f).start()

        return carry

    lax.fori_loop(0, nf, send_act, 0)
    act_buf[f] = act_ref[...]
    o_ref[...] = jnp.zeros_like(o_ref)

    def band(i, carry):
        j = lax.rem(f + chip + i, nf)

        @pl.when(j != f)
        def _():
            act_copy(j, f).wait_send()
            act_copy(j, j).wait_recv()

        for t in range(bands):
            blk = j * bands + t
            h = lax.rem(blk, chips)
            term_buf[blk] = jnp.dot(
                act_buf[j, t], wd_ref[...], preferred_element_type=jnp.float32
            ).astype(term_buf.dtype)
            same_core = (blk // chips) == core

            @pl.when(jnp.logical_not(same_core))
            def _():
                to_sibling(blk).start()

            @pl.when(same_core)
            def _():
                to_sibling(blk).wait_recv()
                pair = term_buf[blk].astype(jnp.float32) + sib_buf[h].astype(jnp.float32)
                pre_buf[h] = pair.astype(pre_buf.dtype)

                @pl.when(h == chip)
                def _():
                    o_ref[...] += pre_buf[h].astype(jnp.float32)

                @pl.when(h != chip)
                def _():
                    piece_copy(h, chip).start()

        return carry

    lax.fori_loop(0, nf, band, 0)

    own_band = (core * chips + chip) // bands
    lift = chips * ((nf + 2 * chips) // chips)

    def take_piece(i, carry):
        h = lax.rem(own_band - f - i + lift, chips)

        @pl.when(h != chip)
        def _():
            piece_copy(h, chip).wait_send()
            piece_copy(h, h).wait_recv()
            o_ref[...] += in_buf[h].astype(jnp.float32)

        return carry

    lax.fori_loop(0, chips, take_piece, 0)

    def drain(h, carry):
        to_sibling((1 - core) * chips + h).wait_send()
        return carry

    lax.fori_loop(0, chips, drain, 0)


def _up_kernel(nf, chips, slot_ref, wg_ref, wu_ref, o_ref, sel_buf, out_buf, in_buf, acc,
               e_send, s_send, fwd_send, sel_recv, f_send, f_recv):
    bands = o_ref.shape[0]
    hidden = o_ref.shape[2]
    f = lax.axis_index("fsdp")
    e = lax.axis_index("ed")
    core = lax.rem(e, 2)
    chip = e // 2
    sib = e + 1 - 2 * core
    mine = core * chips + chip

    def fsdp_peer(i):
        return lax.rem(f + 1 + i, nf)

    def chip_peer(i):
        return lax.rem(chip + 1 + i, chips)

    def direct(h):
        return pltpu.make_async_remote_copy(
            src_ref=slot_ref,
            dst_ref=sel_buf.at[mine],
            send_sem=e_send.at[h],
            recv_sem=sel_recv.at[mine],
            device_id={"ed": h * 2 + core},
            device_id_type=MESH,
        )

    def forward(blk):
        return pltpu.make_async_remote_copy(
            src_ref=sel_buf.at[blk],
            dst_ref=sel_buf.at[blk],
            send_sem=fwd_send.at[lax.rem(blk, chips)],
            recv_sem=sel_recv.at[blk],
            device_id={"ed": sib},
            device_id_type=MESH,
        )

    def partial_copy(g, slot):
        return pltpu.make_async_remote_copy(
            src_ref=out_buf.at[g],
            dst_ref=in_buf.at[slot],
            send_sem=f_send.at[g],
            recv_sem=f_recv.at[slot],
            device_id={"fsdp": g},
            device_id_type=MESH,
        )

    barrier = pltpu.get_barrier_semaphore()

    def greet_fsdp(i, carry):
        pl.semaphore_signal(barrier, 1, device_id={"fsdp": fsdp_peer(i)}, device_id_type=MESH)
        return carry

    def greet_ed(i, carry):
        pl.semaphore_signal(barrier, 1, device_id={"ed": chip_peer(i) * 2 + core}, device_id_type=MESH)
        return carry

    lax.fori_loop(0, nf - 1, greet_fsdp, 0)
    lax.fori_loop(0, chips - 1, greet_ed, 0)
    pl.semaphore_signal(barrier, 1, device_id={"ed": sib}, device_id_type=MESH)
    pl.semaphore_wait(barrier, nf - 1 + chips)

    own_band = mine // bands
    lift = chips * ((nf + 2 * chips) // chips)

    def send_slots(k, carry):
        h = lax.rem(own_band - f - 1 - k + lift, chips)

        @pl.when(h != chip)
        def _():
            direct(h).start()

        return carry

    to_sib = pltpu.make_async_remote_copy(
        src_ref=slot_ref,
        dst_ref=sel_buf.at[mine],
        send_sem=s_send,
        recv_sem=sel_recv.at[mine],
        device_id={"ed": sib},
        device_id_type=MESH,
    )
    to_sib.start()
    lax.fori_loop(0, chips, send_slots, 0)
    sel_buf[mine] = slot_ref[...]

    def band(i, carry):
        j = lax.rem(f + chip + 1 + i, nf)
        for t in range(bands):
            blk = j * bands + t
            same_core = (blk // chips) == core
            not_mine = blk != mine

            @pl.when(same_core & not_mine)
            def _():
                forward(blk).wait_recv()
                forward(blk).start()

            @pl.when(jnp.logical_not(same_core))
            def _():
                forward(blk).wait_recv()

        for t in range(bands):
            blk = j * bands + t
            rows_in = sel_buf[blk]
            out_buf[j, t, :, :hidden] = jnp.dot(
                rows_in, wg_ref[...], preferred_element_type=jnp.float32
            ).astype(out_buf.dtype)
            out_buf[j, t, :, hidden:] = jnp.dot(
                rows_in, wu_ref[...], preferred_element_type=jnp.float32
            ).astype(out_buf.dtype)

        @pl.when(j != f)
        def _():
            partial_copy(j, f).start()

        return carry

    lax.fori_loop(0, nf, band, 0)
    acc[...] = out_buf[f].astype(jnp.float32)

    lift_f = nf * ((chips + 2 * nf) // nf)

    def gather(i, carry):
        g = lax.rem(f - chip - 1 - i + lift_f, nf)

        @pl.when(g != f)
        def _():
            partial_copy(g, f).wait_send()
            partial_copy(g, g).wait_recv()
            acc[...] += in_buf[g].astype(jnp.float32)

        return carry

    lax.fori_loop(0, nf, gather, 0)

    def drain(i, carry):
        h = chip_peer(i)
        direct(h).wait_send()
        forward(core * chips + h).wait_send()
        return carry

    lax.fori_loop(0, chips - 1, drain, 0)
    to_sib.wait_send()
    total = acc[...]
    o_ref[...] = (jax.nn.silu(total[..., :hidden]) * total[..., hidden:]).astype(o_ref.dtype)


def _layer_kernel(nf, chips, slot_ref, wg_ref, wu_ref, wd_ref, comb_ref, o_ref, *scratch):
    up_scratch, act_s, down_scratch, slot_out = scratch[:10], scratch[10], scratch[11:22], scratch[22]
    _up_kernel(nf, chips, slot_ref, wg_ref, wu_ref, act_s, *up_scratch)
    _down_kernel(nf, chips, act_s, wd_ref, slot_out, *down_scratch)
    o_ref[...] = jnp.dot(
        comb_ref[...], slot_out[...], precision=lax.Precision.HIGHEST,
        preferred_element_type=jnp.float32,
    ).astype(o_ref.dtype)


def moe_layer(slots, wg, wu, wd, comb, nf, chips, cid):
    rows, d = slots.shape
    hidden = wg.shape[1]
    bands = 2 * chips // nf
    blocks = nf * bands
    tok = comb.shape[0]
    return pl.pallas_call(
        functools.partial(_layer_kernel, nf, chips),
        out_shape=jax.ShapeDtypeStruct((tok, d), jnp.bfloat16),
        in_specs=[pl.BlockSpec(memory_space=pltpu.VMEM)] * 5,
        out_specs=pl.BlockSpec(memory_space=pltpu.VMEM),
        scratch_shapes=[
            pltpu.VMEM((2 * chips, rows, d), jnp.bfloat16),
            pltpu.VMEM((nf, bands, rows, 2 * hidden), jnp.bfloat16),
            pltpu.VMEM((nf, bands, rows, 2 * hidden), jnp.bfloat16),
            pltpu.VMEM((bands, rows, 2 * hidden), jnp.float32),
            pltpu.SemaphoreType.DMA((chips,)),
            pltpu.SemaphoreType.DMA,
            pltpu.SemaphoreType.DMA((chips,)),
            pltpu.SemaphoreType.DMA((2 * chips,)),
            pltpu.SemaphoreType.DMA((nf,)),
            pltpu.SemaphoreType.DMA((nf,)),
            pltpu.VMEM((bands, rows, hidden), jnp.bfloat16),
            pltpu.VMEM((nf, bands, rows, hidden), jnp.bfloat16),
            pltpu.VMEM((blocks, rows, d), jnp.bfloat16),
            pltpu.VMEM((chips, rows, d), jnp.bfloat16),
            pltpu.VMEM((chips, rows, d), jnp.bfloat16),
            pltpu.VMEM((chips, rows, d), jnp.bfloat16),
            pltpu.SemaphoreType.DMA((nf,)),
            pltpu.SemaphoreType.DMA((nf,)),
            pltpu.SemaphoreType.DMA((chips,)),
            pltpu.SemaphoreType.DMA((chips,)),
            pltpu.SemaphoreType.DMA((chips,)),
            pltpu.SemaphoreType.DMA((chips,)),
            pltpu.VMEM((rows, d), jnp.float32),
        ],
        compiler_params=pltpu.CompilerParams(collective_id=cid, has_side_effects=True),
    )(slots, wg, wu, wd, comb)


def local(tokens, expert_ids, route_weights, w_gate, w_up, w_down):
    window = w_gate.shape[0]
    features_dev = tokens.shape[1]
    hidden_dev = w_gate.shape[2]
    n_ed = lax.axis_size("ed")
    n_fsdp = lax.axis_size("fsdp")
    chips = n_ed // 2
    per_band = n_ed // n_fsdp
    tok_dev = tokens.shape[0]
    order = jnp.arange(tok_dev, dtype=jnp.int32)
    routed = jnp.any(expert_ids == 0, axis=1)
    lower = (order[:, None] >= order[None, :]).astype(jnp.bfloat16)
    count = jnp.dot(lower, routed.astype(jnp.bfloat16), preferred_element_type=jnp.float32)
    slot_ids = jnp.arange(CAP, dtype=jnp.float32)
    match = routed[None, :] & (count[None, :] - 1.0 == slot_ids[:, None])
    own_slots = jnp.dot(
        match.astype(jnp.bfloat16), tokens, preferred_element_type=jnp.float32
    ).astype(jnp.bfloat16)
    per_expert = jnp.sum(
        jnp.where(expert_ids == 0, route_weights, jnp.zeros_like(route_weights)), axis=1
    )
    weights_matrix = match.T.astype(jnp.float32) * per_expert[:, None]
    return moe_layer(own_slots, w_gate[0], w_up[0], w_down[0], weights_matrix, n_fsdp, chips, 2)


def solution(mesh):
    return jax.shard_map(
        local,
        mesh=mesh,
        in_specs=(
            P("ed", "fsdp"),
            P("ed", None),
            P("ed", None),
            P(None, "fsdp", "ed"),
            P(None, "fsdp", "ed"),
            P(None, "ed", "fsdp"),
        ),
        out_specs=P("ed", "fsdp"),
        check_vma=False,
    )
```

```python
import functools

import jax
import jax.numpy as jnp
from jax import lax
from jax.experimental import pallas as pl
from jax.experimental.pallas import tpu as pltpu
from jax.sharding import PartitionSpec as P

CAP = 81
MESH = pl.DeviceIdType.MESH


def slot_match(routes, window, capacity):
    window_ids = jnp.arange(window, dtype=jnp.int32)
    routed = jnp.any(routes[:, :, None, :] == window_ids[None, None, :, None], axis=3)
    position = jnp.cumsum(routed.astype(jnp.int32), axis=1) - 1
    slot_ids = jnp.arange(capacity, dtype=jnp.int32)
    hits = routed[:, :, :, None] & (position[:, :, :, None] == slot_ids[None, None, None, :])
    return hits.astype(jnp.int32)


def take_block(block_rows, row_list):
    return jnp.take(block_rows, row_list, axis=0)


def pick_rows(blocks, routes, window, capacity):
    match = slot_match(routes, window, capacity)
    row_numbers = jnp.arange(blocks.shape[1], dtype=jnp.int32)
    source_row = jnp.sum(match * row_numbers[None, :, None, None], axis=1).reshape(
        blocks.shape[0], window * capacity
    )
    filled = jnp.sum(match, axis=1).reshape(blocks.shape[0], window * capacity)
    picked = jax.vmap(take_block)(blocks, source_row)
    picked = jnp.where(filled[:, :, None] > 0, picked, jnp.zeros_like(picked))
    return picked.reshape(blocks.shape[0], window, capacity, blocks.shape[2])


def combine_matrix(routes, weights, window, capacity):
    match = slot_match(routes[None], window, capacity)[0]
    window_ids = jnp.arange(window, dtype=jnp.int32)
    per_expert = jnp.sum(
        jnp.where(
            routes[:, None, :] == window_ids[None, :, None],
            weights[:, None, :],
            jnp.zeros_like(weights[:, None, :]),
        ),
        axis=2,
    )
    return (per_expert[:, :, None] * match.astype(weights.dtype)).reshape(
        routes.shape[0], window * capacity
    )


def _down_kernel(nf, chips, act_ref, wd_ref, o_ref, act_buf, term_buf, sib_buf, pre_buf, in_buf,
                 a_send, a_recv, s_send, s_recv, e_send, e_recv):
    bands = act_ref.shape[0]
    f = lax.axis_index("fsdp")
    e = lax.axis_index("ed")
    core = lax.rem(e, 2)
    chip = e // 2
    sib = e + 1 - 2 * core

    def fsdp_peer(i):
        return lax.rem(f + 1 + i, nf)

    def chip_peer(i):
        return lax.rem(chip + 1 + i, chips)

    def act_copy(g, slot):
        return pltpu.make_async_remote_copy(
            src_ref=act_ref,
            dst_ref=act_buf.at[slot],
            send_sem=a_send.at[g],
            recv_sem=a_recv.at[slot],
            device_id={"fsdp": g},
            device_id_type=MESH,
        )

    def to_sibling(blk):
        h = lax.rem(blk, chips)
        return pltpu.make_async_remote_copy(
            src_ref=term_buf.at[blk],
            dst_ref=sib_buf.at[h],
            send_sem=s_send.at[h],
            recv_sem=s_recv.at[h],
            device_id={"ed": sib},
            device_id_type=MESH,
        )

    def piece_copy(h, slot):
        return pltpu.make_async_remote_copy(
            src_ref=pre_buf.at[h],
            dst_ref=in_buf.at[slot],
            send_sem=e_send.at[h],
            recv_sem=e_recv.at[slot],
            device_id={"ed": h * 2 + core},
            device_id_type=MESH,
        )

    shift = nf - lax.rem(chip, nf)

    def send_act(i, carry):
        g = lax.rem(f + shift + nf - i, nf)

        @pl.when(g != f)
        def _():
            act_copy(g, f).start()

        return carry

    lax.fori_loop(0, nf, send_act, 0)
    act_buf[f] = act_ref[...]
    o_ref[...] = jnp.zeros_like(o_ref)

    def band(i, carry):
        j = lax.rem(f + chip + i, nf)

        @pl.when(j != f)
        def _():
            act_copy(j, f).wait_send()
            act_copy(j, j).wait_recv()

        for t in range(bands):
            blk = j * bands + t
            h = lax.rem(blk, chips)
            term_buf[blk] = jnp.dot(
                act_buf[j, t], wd_ref[...], preferred_element_type=jnp.float32
            ).astype(term_buf.dtype)
            same_core = (blk // chips) == core

            @pl.when(jnp.logical_not(same_core))
            def _():
                to_sibling(blk).start()

            @pl.when(same_core)
            def _():
                to_sibling(blk).wait_recv()
                pair = term_buf[blk].astype(jnp.float32) + sib_buf[h].astype(jnp.float32)
                pre_buf[h] = pair.astype(pre_buf.dtype)

                @pl.when(h == chip)
                def _():
                    o_ref[...] += pre_buf[h].astype(jnp.float32)

                @pl.when(h != chip)
                def _():
                    piece_copy(h, chip).start()

        return carry

    lax.fori_loop(0, nf, band, 0)

    def take_piece(i, carry):
        h = chip_peer(i)
        piece_copy(h, chip).wait_send()
        piece_copy(h, h).wait_recv()
        o_ref[...] += in_buf[h].astype(jnp.float32)
        return carry

    lax.fori_loop(0, chips - 1, take_piece, 0)

    def drain(h, carry):
        to_sibling((1 - core) * chips + h).wait_send()
        return carry

    lax.fori_loop(0, chips, drain, 0)


def _up_kernel(nf, chips, slot_ref, wg_ref, wu_ref, o_ref, sel_buf, out_buf, in_buf, acc,
               e_send, s_send, fwd_send, sel_recv, f_send, f_recv):
    bands = o_ref.shape[0]
    hidden = o_ref.shape[2]
    f = lax.axis_index("fsdp")
    e = lax.axis_index("ed")
    core = lax.rem(e, 2)
    chip = e // 2
    sib = e + 1 - 2 * core
    mine = core * chips + chip

    def fsdp_peer(i):
        return lax.rem(f + 1 + i, nf)

    def chip_peer(i):
        return lax.rem(chip + 1 + i, chips)

    def direct(h):
        return pltpu.make_async_remote_copy(
            src_ref=slot_ref,
            dst_ref=sel_buf.at[mine],
            send_sem=e_send.at[h],
            recv_sem=sel_recv.at[mine],
            device_id={"ed": h * 2 + core},
            device_id_type=MESH,
        )

    def forward(blk):
        return pltpu.make_async_remote_copy(
            src_ref=sel_buf.at[blk],
            dst_ref=sel_buf.at[blk],
            send_sem=fwd_send.at[lax.rem(blk, chips)],
            recv_sem=sel_recv.at[blk],
            device_id={"ed": sib},
            device_id_type=MESH,
        )

    def partial_copy(g, slot):
        return pltpu.make_async_remote_copy(
            src_ref=out_buf.at[g],
            dst_ref=in_buf.at[slot],
            send_sem=f_send.at[g],
            recv_sem=f_recv.at[slot],
            device_id={"fsdp": g},
            device_id_type=MESH,
        )

    barrier = pltpu.get_barrier_semaphore()

    def greet_fsdp(i, carry):
        pl.semaphore_signal(barrier, 1, device_id={"fsdp": fsdp_peer(i)}, device_id_type=MESH)
        return carry

    def greet_ed(i, carry):
        pl.semaphore_signal(barrier, 1, device_id={"ed": chip_peer(i) * 2 + core}, device_id_type=MESH)
        return carry

    lax.fori_loop(0, nf - 1, greet_fsdp, 0)
    lax.fori_loop(0, chips - 1, greet_ed, 0)
    pl.semaphore_signal(barrier, 1, device_id={"ed": sib}, device_id_type=MESH)
    pl.semaphore_wait(barrier, nf - 1 + chips)

    own_band = mine // bands
    lift = chips * ((nf + 2 * chips) // chips)

    def send_slots(k, carry):
        h = lax.rem(own_band - f - 1 - k + lift, chips)

        @pl.when(h != chip)
        def _():
            direct(h).start()

        return carry

    to_sib = pltpu.make_async_remote_copy(
        src_ref=slot_ref,
        dst_ref=sel_buf.at[mine],
        send_sem=s_send,
        recv_sem=sel_recv.at[mine],
        device_id={"ed": sib},
        device_id_type=MESH,
    )
    to_sib.start()
    lax.fori_loop(0, chips, send_slots, 0)
    sel_buf[mine] = slot_ref[...]

    def band(i, carry):
        j = lax.rem(f + chip + 1 + i, nf)
        for t in range(bands):
            blk = j * bands + t
            same_core = (blk // chips) == core
            not_mine = blk != mine

            @pl.when(same_core & not_mine)
            def _():
                forward(blk).wait_recv()
                forward(blk).start()

            @pl.when(jnp.logical_not(same_core))
            def _():
                forward(blk).wait_recv()

        for t in range(bands):
            blk = j * bands + t
            rows_in = sel_buf[blk]
            out_buf[j, t, :, :hidden] = jnp.dot(
                rows_in, wg_ref[...], preferred_element_type=jnp.float32
            ).astype(out_buf.dtype)
            out_buf[j, t, :, hidden:] = jnp.dot(
                rows_in, wu_ref[...], preferred_element_type=jnp.float32
            ).astype(out_buf.dtype)

        @pl.when(j != f)
        def _():
            partial_copy(j, f).start()

        return carry

    lax.fori_loop(0, nf, band, 0)
    acc[...] = out_buf[f].astype(jnp.float32)

    lift_f = nf * ((chips + 2 * nf) // nf)

    def gather(i, carry):
        g = lax.rem(f - chip - 1 - i + lift_f, nf)

        @pl.when(g != f)
        def _():
            partial_copy(g, f).wait_send()
            partial_copy(g, g).wait_recv()
            acc[...] += in_buf[g].astype(jnp.float32)

        return carry

    lax.fori_loop(0, nf, gather, 0)

    def drain(i, carry):
        h = chip_peer(i)
        direct(h).wait_send()
        forward(core * chips + h).wait_send()
        return carry

    lax.fori_loop(0, chips - 1, drain, 0)
    to_sib.wait_send()
    total = acc[...]
    o_ref[...] = (jax.nn.silu(total[..., :hidden]) * total[..., hidden:]).astype(o_ref.dtype)


def _layer_kernel(nf, chips, tok_ref, match_ref, wg_ref, wu_ref, wd_hbm, comb_hbm, o_ref, *scratch):
    up_scratch, act_s, down_scratch, slot_out = scratch[:10], scratch[10], scratch[11:22], scratch[22]
    slot_s, wd_v, comb_v, local_sem = scratch[23:]
    wd_copy = pltpu.make_async_copy(wd_hbm, wd_v, local_sem.at[0])
    comb_copy = pltpu.make_async_copy(comb_hbm, comb_v, local_sem.at[1])
    wd_copy.start()
    comb_copy.start()
    slot_s[...] = jnp.dot(
        match_ref[...], tok_ref[...], preferred_element_type=jnp.float32
    ).astype(slot_s.dtype)
    _up_kernel(nf, chips, slot_s, wg_ref, wu_ref, act_s, *up_scratch)
    wd_copy.wait()
    _down_kernel(nf, chips, act_s, wd_v, slot_out, *down_scratch)
    comb_copy.wait()
    o_ref[...] = jnp.dot(
        comb_v[...], slot_out[...], precision=lax.Precision.HIGHEST,
        preferred_element_type=jnp.float32,
    ).astype(o_ref.dtype)


def moe_layer(tokens, match, wg, wu, wd, comb, nf, chips, cid):
    rows, tok = match.shape
    d = tokens.shape[1]
    hidden = wg.shape[1]
    bands = 2 * chips // nf
    blocks = nf * bands
    vmem = pl.BlockSpec(memory_space=pltpu.VMEM)
    anywhere = pl.BlockSpec(memory_space=pl.ANY)
    return pl.pallas_call(
        functools.partial(_layer_kernel, nf, chips),
        out_shape=jax.ShapeDtypeStruct((tok, d), jnp.bfloat16),
        in_specs=[vmem, vmem, vmem, vmem, anywhere, anywhere],
        out_specs=vmem,
        scratch_shapes=[
            pltpu.VMEM((2 * chips, rows, d), jnp.bfloat16),
            pltpu.VMEM((nf, bands, rows, 2 * hidden), jnp.bfloat16),
            pltpu.VMEM((nf, bands, rows, 2 * hidden), jnp.bfloat16),
            pltpu.VMEM((bands, rows, 2 * hidden), jnp.float32),
            pltpu.SemaphoreType.DMA((chips,)),
            pltpu.SemaphoreType.DMA,
            pltpu.SemaphoreType.DMA((chips,)),
            pltpu.SemaphoreType.DMA((2 * chips,)),
            pltpu.SemaphoreType.DMA((nf,)),
            pltpu.SemaphoreType.DMA((nf,)),
            pltpu.VMEM((bands, rows, hidden), jnp.bfloat16),
            pltpu.VMEM((nf, bands, rows, hidden), jnp.bfloat16),
            pltpu.VMEM((blocks, rows, d), jnp.bfloat16),
            pltpu.VMEM((chips, rows, d), jnp.bfloat16),
            pltpu.VMEM((chips, rows, d), jnp.bfloat16),
            pltpu.VMEM((chips, rows, d), jnp.bfloat16),
            pltpu.SemaphoreType.DMA((nf,)),
            pltpu.SemaphoreType.DMA((nf,)),
            pltpu.SemaphoreType.DMA((chips,)),
            pltpu.SemaphoreType.DMA((chips,)),
            pltpu.SemaphoreType.DMA((chips,)),
            pltpu.SemaphoreType.DMA((chips,)),
            pltpu.VMEM((rows, d), jnp.float32),
            pltpu.VMEM((rows, d), jnp.bfloat16),
            pltpu.VMEM((hidden, d), jnp.bfloat16),
            pltpu.VMEM((tok, rows), jnp.float32),
            pltpu.SemaphoreType.DMA((2,)),
        ],
        compiler_params=pltpu.CompilerParams(collective_id=cid, has_side_effects=True),
    )(tokens, match, wg, wu, wd, comb)


def local(tokens, expert_ids, route_weights, w_gate, w_up, w_down):
    window = w_gate.shape[0]
    features_dev = tokens.shape[1]
    hidden_dev = w_gate.shape[2]
    n_ed = lax.axis_size("ed")
    n_fsdp = lax.axis_size("fsdp")
    chips = n_ed // 2
    per_band = n_ed // n_fsdp
    tok_dev = tokens.shape[0]
    order = jnp.arange(tok_dev, dtype=jnp.int32)
    routed = jnp.any(expert_ids == 0, axis=1)
    lower = (order[:, None] >= order[None, :]).astype(jnp.bfloat16)
    count = jnp.dot(lower, routed.astype(jnp.bfloat16), preferred_element_type=jnp.float32)
    slot_ids = jnp.arange(CAP, dtype=jnp.float32)
    match = routed[None, :] & (count[None, :] - 1.0 == slot_ids[:, None])
    per_expert = jnp.sum(
        jnp.where(expert_ids == 0, route_weights, jnp.zeros_like(route_weights)), axis=1
    )
    weights_matrix = match.T.astype(jnp.float32) * per_expert[:, None]
    return moe_layer(
        tokens, match.astype(jnp.bfloat16), w_gate[0], w_up[0], w_down[0], weights_matrix,
        n_fsdp, chips, 2,
    )


def solution(mesh):
    return jax.shard_map(
        local,
        mesh=mesh,
        in_specs=(
            P("ed", "fsdp"),
            P("ed", None),
            P("ed", None),
            P(None, "fsdp", "ed"),
            P(None, "fsdp", "ed"),
            P(None, "ed", "fsdp"),
        ),
        out_specs=P("ed", "fsdp"),
        check_vma=False,
    )
```

```python
import functools

import jax
import jax.numpy as jnp
from jax import lax
from jax.experimental import pallas as pl
from jax.experimental.pallas import tpu as pltpu
from jax.sharding import PartitionSpec as P

CAP = 81
MESH = pl.DeviceIdType.MESH


def slot_match(routes, window, capacity):
    window_ids = jnp.arange(window, dtype=jnp.int32)
    routed = jnp.any(routes[:, :, None, :] == window_ids[None, None, :, None], axis=3)
    position = jnp.cumsum(routed.astype(jnp.int32), axis=1) - 1
    slot_ids = jnp.arange(capacity, dtype=jnp.int32)
    hits = routed[:, :, :, None] & (position[:, :, :, None] == slot_ids[None, None, None, :])
    return hits.astype(jnp.int32)


def take_block(block_rows, row_list):
    return jnp.take(block_rows, row_list, axis=0)


def pick_rows(blocks, routes, window, capacity):
    match = slot_match(routes, window, capacity)
    row_numbers = jnp.arange(blocks.shape[1], dtype=jnp.int32)
    source_row = jnp.sum(match * row_numbers[None, :, None, None], axis=1).reshape(
        blocks.shape[0], window * capacity
    )
    filled = jnp.sum(match, axis=1).reshape(blocks.shape[0], window * capacity)
    picked = jax.vmap(take_block)(blocks, source_row)
    picked = jnp.where(filled[:, :, None] > 0, picked, jnp.zeros_like(picked))
    return picked.reshape(blocks.shape[0], window, capacity, blocks.shape[2])


def combine_matrix(routes, weights, window, capacity):
    match = slot_match(routes[None], window, capacity)[0]
    window_ids = jnp.arange(window, dtype=jnp.int32)
    per_expert = jnp.sum(
        jnp.where(
            routes[:, None, :] == window_ids[None, :, None],
            weights[:, None, :],
            jnp.zeros_like(weights[:, None, :]),
        ),
        axis=2,
    )
    return (per_expert[:, :, None] * match.astype(weights.dtype)).reshape(
        routes.shape[0], window * capacity
    )


def _down_kernel(nf, chips, act_ref, wd_ref, o_ref, act_buf, term_buf, sib_buf, pre_buf, in_buf,
                 a_send, a_recv, s_send, s_recv, e_send, e_recv):
    bands = act_ref.shape[0]
    f = lax.axis_index("fsdp")
    e = lax.axis_index("ed")
    core = lax.rem(e, 2)
    chip = e // 2
    sib = e + 1 - 2 * core

    def fsdp_peer(i):
        return lax.rem(f + 1 + i, nf)

    def chip_peer(i):
        return lax.rem(chip + 1 + i, chips)

    def act_copy(g, slot):
        return pltpu.make_async_remote_copy(
            src_ref=act_ref,
            dst_ref=act_buf.at[slot],
            send_sem=a_send.at[g],
            recv_sem=a_recv.at[slot],
            device_id={"fsdp": g},
            device_id_type=MESH,
        )

    def to_sibling(blk):
        h = lax.rem(blk, chips)
        return pltpu.make_async_remote_copy(
            src_ref=term_buf.at[blk],
            dst_ref=sib_buf.at[h],
            send_sem=s_send.at[h],
            recv_sem=s_recv.at[h],
            device_id={"ed": sib},
            device_id_type=MESH,
        )

    def piece_copy(h, slot):
        return pltpu.make_async_remote_copy(
            src_ref=pre_buf.at[h],
            dst_ref=in_buf.at[slot],
            send_sem=e_send.at[h],
            recv_sem=e_recv.at[slot],
            device_id={"ed": h * 2 + core},
            device_id_type=MESH,
        )

    shift = nf - lax.rem(chip, nf)

    def send_act(i, carry):
        g = lax.rem(f + shift + nf - i, nf)

        @pl.when(g != f)
        def _():
            act_copy(g, f).start()

        return carry

    lax.fori_loop(0, nf, send_act, 0)
    act_buf[f] = act_ref[...]
    o_ref[...] = jnp.zeros_like(o_ref)

    def band(i, carry):
        j = lax.rem(f + chip + i, nf)

        @pl.when(j != f)
        def _():
            act_copy(j, j).wait_recv()

        for t in range(bands):
            blk = j * bands + t
            h = lax.rem(blk, chips)
            term_buf[blk] = jnp.dot(
                act_buf[j, t], wd_ref[...], preferred_element_type=jnp.float32
            ).astype(term_buf.dtype)
            same_core = (blk // chips) == core

            @pl.when(jnp.logical_not(same_core))
            def _():
                to_sibling(blk).start()

            @pl.when(same_core)
            def _():
                to_sibling(blk).wait_recv()
                pair = term_buf[blk].astype(jnp.float32) + sib_buf[h].astype(jnp.float32)
                pre_buf[h] = pair.astype(pre_buf.dtype)

                @pl.when(h == chip)
                def _():
                    o_ref[...] += pre_buf[h].astype(jnp.float32)

                @pl.when(h != chip)
                def _():
                    piece_copy(h, chip).start()

        return carry

    lax.fori_loop(0, nf, band, 0)

    def take_piece(i, carry):
        h = chip_peer(i)
        piece_copy(h, chip).wait_send()
        piece_copy(h, h).wait_recv()
        o_ref[...] += in_buf[h].astype(jnp.float32)
        return carry

    lax.fori_loop(0, chips - 1, take_piece, 0)

    def drain(h, carry):
        to_sibling((1 - core) * chips + h).wait_send()
        return carry

    lax.fori_loop(0, chips, drain, 0)

    def drain_act(i, carry):
        act_copy(fsdp_peer(i), f).wait_send()
        return carry

    lax.fori_loop(0, nf - 1, drain_act, 0)


def _up_kernel(nf, chips, slot_ref, wg_ref, wu_ref, o_ref, sel_buf, out_buf, in_buf, acc,
               e_send, s_send, fwd_send, sel_recv, f_send, f_recv):
    bands = o_ref.shape[0]
    hidden = o_ref.shape[2]
    f = lax.axis_index("fsdp")
    e = lax.axis_index("ed")
    core = lax.rem(e, 2)
    chip = e // 2
    sib = e + 1 - 2 * core
    mine = core * chips + chip

    def fsdp_peer(i):
        return lax.rem(f + 1 + i, nf)

    def chip_peer(i):
        return lax.rem(chip + 1 + i, chips)

    def direct(h):
        return pltpu.make_async_remote_copy(
            src_ref=slot_ref,
            dst_ref=sel_buf.at[mine],
            send_sem=e_send.at[h],
            recv_sem=sel_recv.at[mine],
            device_id={"ed": h * 2 + core},
            device_id_type=MESH,
        )

    def forward(blk):
        return pltpu.make_async_remote_copy(
            src_ref=sel_buf.at[blk],
            dst_ref=sel_buf.at[blk],
            send_sem=fwd_send.at[lax.rem(blk, chips)],
            recv_sem=sel_recv.at[blk],
            device_id={"ed": sib},
            device_id_type=MESH,
        )

    def partial_copy(g, slot):
        return pltpu.make_async_remote_copy(
            src_ref=out_buf.at[g],
            dst_ref=in_buf.at[slot],
            send_sem=f_send.at[g],
            recv_sem=f_recv.at[slot],
            device_id={"fsdp": g},
            device_id_type=MESH,
        )

    barrier = pltpu.get_barrier_semaphore()

    def greet_fsdp(i, carry):
        pl.semaphore_signal(barrier, 1, device_id={"fsdp": fsdp_peer(i)}, device_id_type=MESH)
        return carry

    def greet_ed(i, carry):
        pl.semaphore_signal(barrier, 1, device_id={"ed": chip_peer(i) * 2 + core}, device_id_type=MESH)
        return carry

    lax.fori_loop(0, nf - 1, greet_fsdp, 0)
    lax.fori_loop(0, chips - 1, greet_ed, 0)
    pl.semaphore_signal(barrier, 1, device_id={"ed": sib}, device_id_type=MESH)
    pl.semaphore_wait(barrier, nf - 1 + chips)

    own_band = mine // bands
    lift = chips * ((nf + 2 * chips) // chips)

    def send_slots(k, carry):
        h = lax.rem(own_band - f - 1 - k + lift, chips)

        @pl.when(h != chip)
        def _():
            direct(h).start()

        return carry

    to_sib = pltpu.make_async_remote_copy(
        src_ref=slot_ref,
        dst_ref=sel_buf.at[mine],
        send_sem=s_send,
        recv_sem=sel_recv.at[mine],
        device_id={"ed": sib},
        device_id_type=MESH,
    )
    to_sib.start()
    lax.fori_loop(0, chips, send_slots, 0)
    sel_buf[mine] = slot_ref[...]

    def band(i, carry):
        j = lax.rem(f + chip + 1 + i, nf)
        for t in range(bands):
            blk = j * bands + t
            same_core = (blk // chips) == core
            not_mine = blk != mine

            @pl.when(same_core & not_mine)
            def _():
                forward(blk).wait_recv()
                forward(blk).start()

            @pl.when(jnp.logical_not(same_core))
            def _():
                forward(blk).wait_recv()

        for t in range(bands):
            blk = j * bands + t
            rows_in = sel_buf[blk]
            out_buf[j, t, :, :hidden] = jnp.dot(
                rows_in, wg_ref[...], preferred_element_type=jnp.float32
            ).astype(out_buf.dtype)
            out_buf[j, t, :, hidden:] = jnp.dot(
                rows_in, wu_ref[...], preferred_element_type=jnp.float32
            ).astype(out_buf.dtype)

        @pl.when(j != f)
        def _():
            partial_copy(j, f).start()

        return carry

    lax.fori_loop(0, nf, band, 0)
    acc[...] = out_buf[f].astype(jnp.float32)

    lift_f = nf * ((chips + 2 * nf) // nf)

    def gather(i, carry):
        g = lax.rem(f - chip - 1 - i + lift_f, nf)

        @pl.when(g != f)
        def _():
            partial_copy(g, g).wait_recv()
            acc[...] += in_buf[g].astype(jnp.float32)

        return carry

    lax.fori_loop(0, nf, gather, 0)

    def drain(i, carry):
        h = chip_peer(i)
        direct(h).wait_send()
        forward(core * chips + h).wait_send()
        return carry

    lax.fori_loop(0, chips - 1, drain, 0)

    def drain_partial(i, carry):
        partial_copy(fsdp_peer(i), f).wait_send()
        return carry

    lax.fori_loop(0, nf - 1, drain_partial, 0)
    to_sib.wait_send()
    total = acc[...]
    o_ref[...] = (jax.nn.silu(total[..., :hidden]) * total[..., hidden:]).astype(o_ref.dtype)


def _layer_kernel(nf, chips, slot_ref, wg_ref, wu_ref, wd_ref, comb_ref, o_ref, *scratch):
    up_scratch, act_s, down_scratch, slot_out = scratch[:10], scratch[10], scratch[11:22], scratch[22]
    _up_kernel(nf, chips, slot_ref, wg_ref, wu_ref, act_s, *up_scratch)
    _down_kernel(nf, chips, act_s, wd_ref, slot_out, *down_scratch)
    o_ref[...] = jnp.dot(
        comb_ref[...], slot_out[...], precision=lax.Precision.HIGHEST,
        preferred_element_type=jnp.float32,
    ).astype(o_ref.dtype)


def moe_layer(slots, wg, wu, wd, comb, nf, chips, cid):
    rows, d = slots.shape
    hidden = wg.shape[1]
    bands = 2 * chips // nf
    blocks = nf * bands
    tok = comb.shape[0]
    return pl.pallas_call(
        functools.partial(_layer_kernel, nf, chips),
        out_shape=jax.ShapeDtypeStruct((tok, d), jnp.bfloat16),
        in_specs=[pl.BlockSpec(memory_space=pltpu.VMEM)] * 5,
        out_specs=pl.BlockSpec(memory_space=pltpu.VMEM),
        scratch_shapes=[
            pltpu.VMEM((2 * chips, rows, d), jnp.bfloat16),
            pltpu.VMEM((nf, bands, rows, 2 * hidden), jnp.bfloat16),
            pltpu.VMEM((nf, bands, rows, 2 * hidden), jnp.bfloat16),
            pltpu.VMEM((bands, rows, 2 * hidden), jnp.float32),
            pltpu.SemaphoreType.DMA((chips,)),
            pltpu.SemaphoreType.DMA,
            pltpu.SemaphoreType.DMA((chips,)),
            pltpu.SemaphoreType.DMA((2 * chips,)),
            pltpu.SemaphoreType.DMA((nf,)),
            pltpu.SemaphoreType.DMA((nf,)),
            pltpu.VMEM((bands, rows, hidden), jnp.bfloat16),
            pltpu.VMEM((nf, bands, rows, hidden), jnp.bfloat16),
            pltpu.VMEM((blocks, rows, d), jnp.bfloat16),
            pltpu.VMEM((chips, rows, d), jnp.bfloat16),
            pltpu.VMEM((chips, rows, d), jnp.bfloat16),
            pltpu.VMEM((chips, rows, d), jnp.bfloat16),
            pltpu.SemaphoreType.DMA((nf,)),
            pltpu.SemaphoreType.DMA((nf,)),
            pltpu.SemaphoreType.DMA((chips,)),
            pltpu.SemaphoreType.DMA((chips,)),
            pltpu.SemaphoreType.DMA((chips,)),
            pltpu.SemaphoreType.DMA((chips,)),
            pltpu.VMEM((rows, d), jnp.float32),
        ],
        compiler_params=pltpu.CompilerParams(collective_id=cid, has_side_effects=True),
    )(slots, wg, wu, wd, comb)


def local(tokens, expert_ids, route_weights, w_gate, w_up, w_down):
    window = w_gate.shape[0]
    features_dev = tokens.shape[1]
    hidden_dev = w_gate.shape[2]
    n_ed = lax.axis_size("ed")
    n_fsdp = lax.axis_size("fsdp")
    chips = n_ed // 2
    per_band = n_ed // n_fsdp
    tok_dev = tokens.shape[0]
    order = jnp.arange(tok_dev, dtype=jnp.int32)
    routed = jnp.any(expert_ids == 0, axis=1)
    lower = (order[:, None] >= order[None, :]).astype(jnp.bfloat16)
    count = jnp.dot(lower, routed.astype(jnp.bfloat16), preferred_element_type=jnp.float32)
    slot_ids = jnp.arange(CAP, dtype=jnp.float32)
    match = routed[None, :] & (count[None, :] - 1.0 == slot_ids[:, None])
    own_slots = jnp.dot(
        match.astype(jnp.bfloat16), tokens, preferred_element_type=jnp.float32
    ).astype(jnp.bfloat16)
    per_expert = jnp.sum(
        jnp.where(expert_ids == 0, route_weights, jnp.zeros_like(route_weights)), axis=1
    )
    weights_matrix = match.T.astype(jnp.float32) * per_expert[:, None]
    return moe_layer(own_slots, w_gate[0], w_up[0], w_down[0], weights_matrix, n_fsdp, chips, 2)


def solution(mesh):
    return jax.shard_map(
        local,
        mesh=mesh,
        in_specs=(
            P("ed", "fsdp"),
            P("ed", None),
            P("ed", None),
            P(None, "fsdp", "ed"),
            P(None, "fsdp", "ed"),
            P(None, "ed", "fsdp"),
        ),
        out_specs=P("ed", "fsdp"),
        check_vma=False,
    )
```

```python
import functools

import jax
import jax.numpy as jnp
from jax import lax
from jax.experimental import pallas as pl
from jax.experimental.pallas import tpu as pltpu
from jax.sharding import PartitionSpec as P

CAP = 81
MESH = pl.DeviceIdType.MESH


def slot_match(routes, window, capacity):
    window_ids = jnp.arange(window, dtype=jnp.int32)
    routed = jnp.any(routes[:, :, None, :] == window_ids[None, None, :, None], axis=3)
    position = jnp.cumsum(routed.astype(jnp.int32), axis=1) - 1
    slot_ids = jnp.arange(capacity, dtype=jnp.int32)
    hits = routed[:, :, :, None] & (position[:, :, :, None] == slot_ids[None, None, None, :])
    return hits.astype(jnp.int32)


def take_block(block_rows, row_list):
    return jnp.take(block_rows, row_list, axis=0)


def pick_rows(blocks, routes, window, capacity):
    match = slot_match(routes, window, capacity)
    row_numbers = jnp.arange(blocks.shape[1], dtype=jnp.int32)
    source_row = jnp.sum(match * row_numbers[None, :, None, None], axis=1).reshape(
        blocks.shape[0], window * capacity
    )
    filled = jnp.sum(match, axis=1).reshape(blocks.shape[0], window * capacity)
    picked = jax.vmap(take_block)(blocks, source_row)
    picked = jnp.where(filled[:, :, None] > 0, picked, jnp.zeros_like(picked))
    return picked.reshape(blocks.shape[0], window, capacity, blocks.shape[2])


def combine_matrix(routes, weights, window, capacity):
    match = slot_match(routes[None], window, capacity)[0]
    window_ids = jnp.arange(window, dtype=jnp.int32)
    per_expert = jnp.sum(
        jnp.where(
            routes[:, None, :] == window_ids[None, :, None],
            weights[:, None, :],
            jnp.zeros_like(weights[:, None, :]),
        ),
        axis=2,
    )
    return (per_expert[:, :, None] * match.astype(weights.dtype)).reshape(
        routes.shape[0], window * capacity
    )


def _down_kernel(nf, chips, act_ref, wd_ref, o_ref, act_buf, term_buf, sib_buf, pre_buf, in_buf,
                 a_send, a_recv, s_send, s_recv, e_send, e_recv):
    bands = act_ref.shape[0]
    f = lax.axis_index("fsdp")
    e = lax.axis_index("ed")
    core = lax.rem(e, 2)
    chip = e // 2
    sib = e + 1 - 2 * core

    def fsdp_peer(i):
        return lax.rem(f + 1 + i, nf)

    def chip_peer(i):
        return lax.rem(chip + 1 + i, chips)

    def act_copy(g, slot):
        return pltpu.make_async_remote_copy(
            src_ref=act_ref,
            dst_ref=act_buf.at[slot],
            send_sem=a_send.at[g],
            recv_sem=a_recv.at[slot],
            device_id={"fsdp": g},
            device_id_type=MESH,
        )

    def to_sibling(blk):
        h = lax.rem(blk, chips)
        return pltpu.make_async_remote_copy(
            src_ref=term_buf.at[blk],
            dst_ref=sib_buf.at[h],
            send_sem=s_send.at[h],
            recv_sem=s_recv.at[h],
            device_id={"ed": sib},
            device_id_type=MESH,
        )

    def piece_copy(h, slot):
        return pltpu.make_async_remote_copy(
            src_ref=pre_buf.at[h],
            dst_ref=in_buf.at[slot],
            send_sem=e_send.at[h],
            recv_sem=e_recv.at[slot],
            device_id={"ed": h * 2 + core},
            device_id_type=MESH,
        )

    shift = nf - lax.rem(chip, nf)

    def send_act(i, carry):
        g = lax.rem(f + shift + nf - i, nf)

        @pl.when(g != f)
        def _():
            act_copy(g, f).start()

        return carry

    lax.fori_loop(0, nf, send_act, 0)
    act_buf[f] = act_ref[...]
    o_ref[...] = jnp.zeros_like(o_ref)

    def band(i, carry):
        j = lax.rem(f + chip + i, nf)

        @pl.when(j != f)
        def _():
            act_copy(j, j).wait_recv()

        for t in range(bands):
            blk = j * bands + t
            h = lax.rem(blk, chips)
            term_buf[blk] = jnp.dot(
                act_buf[j, t], wd_ref[...], preferred_element_type=jnp.float32
            ).astype(term_buf.dtype)
            same_core = (blk // chips) == core

            @pl.when(jnp.logical_not(same_core))
            def _():
                to_sibling(blk).start()

            @pl.when(same_core)
            def _():
                to_sibling(blk).wait_recv()
                pair = term_buf[blk].astype(jnp.float32) + sib_buf[h].astype(jnp.float32)
                pre_buf[h] = pair.astype(pre_buf.dtype)

                @pl.when(h == chip)
                def _():
                    o_ref[...] += pre_buf[h].astype(jnp.float32)

                @pl.when(h != chip)
                def _():
                    piece_copy(h, chip).start()

        return carry

    lax.fori_loop(0, nf, band, 0)

    def take_piece(i, carry):
        h = chip_peer(i)
        piece_copy(h, h).wait_recv()
        o_ref[...] += in_buf[h].astype(jnp.float32)
        return carry

    lax.fori_loop(0, chips - 1, take_piece, 0)

    def drain_piece(i, carry):
        piece_copy(chip_peer(i), chip).wait_send()
        return carry

    lax.fori_loop(0, chips - 1, drain_piece, 0)

    def drain(h, carry):
        to_sibling((1 - core) * chips + h).wait_send()
        return carry

    lax.fori_loop(0, chips, drain, 0)

    def drain_act(i, carry):
        act_copy(fsdp_peer(i), f).wait_send()
        return carry

    lax.fori_loop(0, nf - 1, drain_act, 0)


def _up_kernel(nf, chips, slot_ref, wg_ref, wu_ref, o_ref, sel_buf, out_buf, in_buf, acc,
               e_send, s_send, fwd_send, sel_recv, f_send, f_recv):
    bands = o_ref.shape[0]
    hidden = o_ref.shape[2]
    f = lax.axis_index("fsdp")
    e = lax.axis_index("ed")
    core = lax.rem(e, 2)
    chip = e // 2
    sib = e + 1 - 2 * core
    mine = core * chips + chip

    def fsdp_peer(i):
        return lax.rem(f + 1 + i, nf)

    def chip_peer(i):
        return lax.rem(chip + 1 + i, chips)

    def direct(h):
        return pltpu.make_async_remote_copy(
            src_ref=slot_ref,
            dst_ref=sel_buf.at[mine],
            send_sem=e_send.at[h],
            recv_sem=sel_recv.at[mine],
            device_id={"ed": h * 2 + core},
            device_id_type=MESH,
        )

    def forward(blk):
        return pltpu.make_async_remote_copy(
            src_ref=sel_buf.at[blk],
            dst_ref=sel_buf.at[blk],
            send_sem=fwd_send.at[lax.rem(blk, chips)],
            recv_sem=sel_recv.at[blk],
            device_id={"ed": sib},
            device_id_type=MESH,
        )

    def partial_copy(g, slot):
        return pltpu.make_async_remote_copy(
            src_ref=out_buf.at[g],
            dst_ref=in_buf.at[slot],
            send_sem=f_send.at[g],
            recv_sem=f_recv.at[slot],
            device_id={"fsdp": g},
            device_id_type=MESH,
        )

    barrier = pltpu.get_barrier_semaphore()

    def greet_fsdp(i, carry):
        pl.semaphore_signal(barrier, 1, device_id={"fsdp": fsdp_peer(i)}, device_id_type=MESH)
        return carry

    def greet_ed(i, carry):
        pl.semaphore_signal(barrier, 1, device_id={"ed": chip_peer(i) * 2 + core}, device_id_type=MESH)
        return carry

    lax.fori_loop(0, nf - 1, greet_fsdp, 0)
    lax.fori_loop(0, chips - 1, greet_ed, 0)
    pl.semaphore_signal(barrier, 1, device_id={"ed": sib}, device_id_type=MESH)
    pl.semaphore_wait(barrier, nf - 1 + chips)

    own_band = mine // bands
    lift = chips * ((nf + 2 * chips) // chips)

    def send_slots(k, carry):
        h = lax.rem(own_band - f - 1 - k + lift, chips)

        @pl.when(h != chip)
        def _():
            direct(h).start()

        return carry

    to_sib = pltpu.make_async_remote_copy(
        src_ref=slot_ref,
        dst_ref=sel_buf.at[mine],
        send_sem=s_send,
        recv_sem=sel_recv.at[mine],
        device_id={"ed": sib},
        device_id_type=MESH,
    )
    to_sib.start()
    lax.fori_loop(0, chips, send_slots, 0)
    sel_buf[mine] = slot_ref[...]

    def band(i, carry):
        j = lax.rem(f + chip + 1 + i, nf)
        for t in range(bands):
            blk = j * bands + t
            same_core = (blk // chips) == core
            not_mine = blk != mine

            @pl.when(same_core & not_mine)
            def _():
                forward(blk).wait_recv()
                forward(blk).start()

            @pl.when(jnp.logical_not(same_core))
            def _():
                forward(blk).wait_recv()

        for t in range(bands):
            blk = j * bands + t
            rows_in = sel_buf[blk]
            out_buf[j, t, :, :hidden] = jnp.dot(
                rows_in, wg_ref[...], preferred_element_type=jnp.float32
            ).astype(out_buf.dtype)
            out_buf[j, t, :, hidden:] = jnp.dot(
                rows_in, wu_ref[...], preferred_element_type=jnp.float32
            ).astype(out_buf.dtype)

        @pl.when(j != f)
        def _():
            partial_copy(j, f).start()

        return carry

    lax.fori_loop(0, nf, band, 0)
    acc[...] = out_buf[f].astype(jnp.float32)

    lift_f = nf * ((chips + 2 * nf) // nf)

    def gather(i, carry):
        g = lax.rem(f - chip - 1 - i + lift_f, nf)

        @pl.when(g != f)
        def _():
            partial_copy(g, g).wait_recv()
            acc[...] += in_buf[g].astype(jnp.float32)

        return carry

    lax.fori_loop(0, nf, gather, 0)

    def drain(i, carry):
        h = chip_peer(i)
        direct(h).wait_send()
        forward(core * chips + h).wait_send()
        return carry

    def drain_partial(i, carry):
        partial_copy(fsdp_peer(i), f).wait_send()
        return carry

    total = acc[...]
    o_ref[...] = (jax.nn.silu(total[..., :hidden]) * total[..., hidden:]).astype(o_ref.dtype)

    def finish():
        lax.fori_loop(0, chips - 1, drain, 0)
        lax.fori_loop(0, nf - 1, drain_partial, 0)
        to_sib.wait_send()

    return finish


def _layer_kernel(nf, chips, slot_ref, wg_ref, wu_ref, wd_ref, comb_ref, o_ref, *scratch):
    up_scratch, act_s, down_scratch, slot_out = scratch[:10], scratch[10], scratch[11:22], scratch[22]
    finish_up = _up_kernel(nf, chips, slot_ref, wg_ref, wu_ref, act_s, *up_scratch)
    _down_kernel(nf, chips, act_s, wd_ref, slot_out, *down_scratch)
    finish_up()
    o_ref[...] = jnp.dot(
        comb_ref[...], slot_out[...], precision=lax.Precision.HIGHEST,
        preferred_element_type=jnp.float32,
    ).astype(o_ref.dtype)


def moe_layer(slots, wg, wu, wd, comb, nf, chips, cid):
    rows, d = slots.shape
    hidden = wg.shape[1]
    bands = 2 * chips // nf
    blocks = nf * bands
    tok = comb.shape[0]
    return pl.pallas_call(
        functools.partial(_layer_kernel, nf, chips),
        out_shape=jax.ShapeDtypeStruct((tok, d), jnp.bfloat16),
        in_specs=[pl.BlockSpec(memory_space=pltpu.VMEM)] * 5,
        out_specs=pl.BlockSpec(memory_space=pltpu.VMEM),
        scratch_shapes=[
            pltpu.VMEM((2 * chips, rows, d), jnp.bfloat16),
            pltpu.VMEM((nf, bands, rows, 2 * hidden), jnp.bfloat16),
            pltpu.VMEM((nf, bands, rows, 2 * hidden), jnp.bfloat16),
            pltpu.VMEM((bands, rows, 2 * hidden), jnp.float32),
            pltpu.SemaphoreType.DMA((chips,)),
            pltpu.SemaphoreType.DMA,
            pltpu.SemaphoreType.DMA((chips,)),
            pltpu.SemaphoreType.DMA((2 * chips,)),
            pltpu.SemaphoreType.DMA((nf,)),
            pltpu.SemaphoreType.DMA((nf,)),
            pltpu.VMEM((bands, rows, hidden), jnp.bfloat16),
            pltpu.VMEM((nf, bands, rows, hidden), jnp.bfloat16),
            pltpu.VMEM((blocks, rows, d), jnp.bfloat16),
            pltpu.VMEM((chips, rows, d), jnp.bfloat16),
            pltpu.VMEM((chips, rows, d), jnp.bfloat16),
            pltpu.VMEM((chips, rows, d), jnp.bfloat16),
            pltpu.SemaphoreType.DMA((nf,)),
            pltpu.SemaphoreType.DMA((nf,)),
            pltpu.SemaphoreType.DMA((chips,)),
            pltpu.SemaphoreType.DMA((chips,)),
            pltpu.SemaphoreType.DMA((chips,)),
            pltpu.SemaphoreType.DMA((chips,)),
            pltpu.VMEM((rows, d), jnp.float32),
        ],
        compiler_params=pltpu.CompilerParams(collective_id=cid, has_side_effects=True),
    )(slots, wg, wu, wd, comb)


def local(tokens, expert_ids, route_weights, w_gate, w_up, w_down):
    window = w_gate.shape[0]
    features_dev = tokens.shape[1]
    hidden_dev = w_gate.shape[2]
    n_ed = lax.axis_size("ed")
    n_fsdp = lax.axis_size("fsdp")
    chips = n_ed // 2
    per_band = n_ed // n_fsdp
    tok_dev = tokens.shape[0]
    order = jnp.arange(tok_dev, dtype=jnp.int32)
    routed = jnp.any(expert_ids == 0, axis=1)
    lower = (order[:, None] >= order[None, :]).astype(jnp.bfloat16)
    count = jnp.dot(lower, routed.astype(jnp.bfloat16), preferred_element_type=jnp.float32)
    slot_ids = jnp.arange(CAP, dtype=jnp.float32)
    match = routed[None, :] & (count[None, :] - 1.0 == slot_ids[:, None])
    own_slots = jnp.dot(
        match.astype(jnp.bfloat16), tokens, preferred_element_type=jnp.float32
    ).astype(jnp.bfloat16)
    per_expert = jnp.sum(
        jnp.where(expert_ids == 0, route_weights, jnp.zeros_like(route_weights)), axis=1
    )
    weights_matrix = match.T.astype(jnp.float32) * per_expert[:, None]
    return moe_layer(own_slots, w_gate[0], w_up[0], w_down[0], weights_matrix, n_fsdp, chips, 2)


def solution(mesh):
    return jax.shard_map(
        local,
        mesh=mesh,
        in_specs=(
            P("ed", "fsdp"),
            P("ed", None),
            P("ed", None),
            P(None, "fsdp", "ed"),
            P(None, "fsdp", "ed"),
            P(None, "ed", "fsdp"),
        ),
        out_specs=P("ed", "fsdp"),
        check_vma=False,
    )
```

```python
import functools

import jax
import jax.numpy as jnp
from jax import lax
from jax.experimental import pallas as pl
from jax.experimental.pallas import tpu as pltpu
from jax.sharding import PartitionSpec as P

CAP = 81
MESH = pl.DeviceIdType.MESH


def slot_match(routes, window, capacity):
    window_ids = jnp.arange(window, dtype=jnp.int32)
    routed = jnp.any(routes[:, :, None, :] == window_ids[None, None, :, None], axis=3)
    position = jnp.cumsum(routed.astype(jnp.int32), axis=1) - 1
    slot_ids = jnp.arange(capacity, dtype=jnp.int32)
    hits = routed[:, :, :, None] & (position[:, :, :, None] == slot_ids[None, None, None, :])
    return hits.astype(jnp.int32)


def take_block(block_rows, row_list):
    return jnp.take(block_rows, row_list, axis=0)


def pick_rows(blocks, routes, window, capacity):
    match = slot_match(routes, window, capacity)
    row_numbers = jnp.arange(blocks.shape[1], dtype=jnp.int32)
    source_row = jnp.sum(match * row_numbers[None, :, None, None], axis=1).reshape(
        blocks.shape[0], window * capacity
    )
    filled = jnp.sum(match, axis=1).reshape(blocks.shape[0], window * capacity)
    picked = jax.vmap(take_block)(blocks, source_row)
    picked = jnp.where(filled[:, :, None] > 0, picked, jnp.zeros_like(picked))
    return picked.reshape(blocks.shape[0], window, capacity, blocks.shape[2])


def combine_matrix(routes, weights, window, capacity):
    match = slot_match(routes[None], window, capacity)[0]
    window_ids = jnp.arange(window, dtype=jnp.int32)
    per_expert = jnp.sum(
        jnp.where(
            routes[:, None, :] == window_ids[None, :, None],
            weights[:, None, :],
            jnp.zeros_like(weights[:, None, :]),
        ),
        axis=2,
    )
    return (per_expert[:, :, None] * match.astype(weights.dtype)).reshape(
        routes.shape[0], window * capacity
    )


def _down_kernel(nf, chips, act_ref, wd_ref, o_ref, act_buf, term_buf, sib_buf, pre_buf, in_buf,
                 a_send, a_recv, s_send, s_recv, e_send, e_recv):
    bands = act_ref.shape[0]
    f = lax.axis_index("fsdp")
    e = lax.axis_index("ed")
    core = lax.rem(e, 2)
    chip = e // 2
    sib = e + 1 - 2 * core

    def fsdp_peer(i):
        return lax.rem(f + 1 + i, nf)

    def chip_peer(i):
        return lax.rem(chip + 1 + i, chips)

    def act_copy(g, slot):
        return pltpu.make_async_remote_copy(
            src_ref=act_ref,
            dst_ref=act_buf.at[slot],
            send_sem=a_send.at[g],
            recv_sem=a_recv.at[slot],
            device_id={"fsdp": g},
            device_id_type=MESH,
        )

    def to_sibling(blk):
        h = lax.rem(blk, chips)
        return pltpu.make_async_remote_copy(
            src_ref=term_buf.at[blk],
            dst_ref=sib_buf.at[h],
            send_sem=s_send.at[h],
            recv_sem=s_recv.at[h],
            device_id={"ed": sib},
            device_id_type=MESH,
        )

    def piece_copy(h, slot):
        return pltpu.make_async_remote_copy(
            src_ref=pre_buf.at[h],
            dst_ref=in_buf.at[slot],
            send_sem=e_send.at[h],
            recv_sem=e_recv.at[slot],
            device_id={"ed": h * 2 + core},
            device_id_type=MESH,
        )

    shift = nf - lax.rem(chip, nf)

    def send_act(i, carry):
        g = lax.rem(f + shift + nf - i, nf)

        @pl.when(g != f)
        def _():
            act_copy(g, f).start()

        return carry

    lax.fori_loop(0, nf, send_act, 0)
    act_buf[f] = act_ref[...]
    o_ref[...] = jnp.zeros_like(o_ref)

    def settle(j):
        for t in range(bands):
            blk = j * bands + t
            h = lax.rem(blk, chips)

            @pl.when((blk // chips) == core)
            def _():
                to_sibling(blk).wait_recv()
                pair = term_buf[blk].astype(jnp.float32) + sib_buf[h].astype(jnp.float32)
                pre_buf[h] = pair.astype(pre_buf.dtype)

                @pl.when(h == chip)
                def _():
                    o_ref[...] += pre_buf[h].astype(jnp.float32)

                @pl.when(h != chip)
                def _():
                    piece_copy(h, chip).start()

    def band(i, carry):
        j = lax.rem(f + chip + i, nf)

        @pl.when(j != f)
        def _():
            act_copy(j, j).wait_recv()

        for t in range(bands):
            blk = j * bands + t
            term_buf[blk] = jnp.dot(
                act_buf[j, t], wd_ref[...], preferred_element_type=jnp.float32
            ).astype(term_buf.dtype)

            @pl.when((blk // chips) != core)
            def _():
                to_sibling(blk).start()

        @pl.when(i > 0)
        def _():
            settle(lax.rem(f + chip + i - 1, nf))

        return carry

    lax.fori_loop(0, nf, band, 0)
    settle(lax.rem(f + chip + nf - 1, nf))

    def take_piece(i, carry):
        h = chip_peer(i)
        piece_copy(h, chip).wait_send()
        piece_copy(h, h).wait_recv()
        o_ref[...] += in_buf[h].astype(jnp.float32)
        return carry

    lax.fori_loop(0, chips - 1, take_piece, 0)

    def drain(h, carry):
        to_sibling((1 - core) * chips + h).wait_send()
        return carry

    lax.fori_loop(0, chips, drain, 0)

    def drain_act(i, carry):
        act_copy(fsdp_peer(i), f).wait_send()
        return carry

    lax.fori_loop(0, nf - 1, drain_act, 0)


def _up_kernel(nf, chips, slot_ref, wg_ref, wu_ref, o_ref, sel_buf, out_buf, in_buf, acc,
               e_send, s_send, fwd_send, sel_recv, f_send, f_recv):
    bands = o_ref.shape[0]
    hidden = o_ref.shape[2]
    f = lax.axis_index("fsdp")
    e = lax.axis_index("ed")
    core = lax.rem(e, 2)
    chip = e // 2
    sib = e + 1 - 2 * core
    mine = core * chips + chip

    def fsdp_peer(i):
        return lax.rem(f + 1 + i, nf)

    def chip_peer(i):
        return lax.rem(chip + 1 + i, chips)

    def direct(h):
        return pltpu.make_async_remote_copy(
            src_ref=slot_ref,
            dst_ref=sel_buf.at[mine],
            send_sem=e_send.at[h],
            recv_sem=sel_recv.at[mine],
            device_id={"ed": h * 2 + core},
            device_id_type=MESH,
        )

    def forward(blk):
        return pltpu.make_async_remote_copy(
            src_ref=sel_buf.at[blk],
            dst_ref=sel_buf.at[blk],
            send_sem=fwd_send.at[lax.rem(blk, chips)],
            recv_sem=sel_recv.at[blk],
            device_id={"ed": sib},
            device_id_type=MESH,
        )

    def partial_copy(g, slot):
        return pltpu.make_async_remote_copy(
            src_ref=out_buf.at[g],
            dst_ref=in_buf.at[slot],
            send_sem=f_send.at[g],
            recv_sem=f_recv.at[slot],
            device_id={"fsdp": g},
            device_id_type=MESH,
        )

    barrier = pltpu.get_barrier_semaphore()

    def greet_fsdp(i, carry):
        pl.semaphore_signal(barrier, 1, device_id={"fsdp": fsdp_peer(i)}, device_id_type=MESH)
        return carry

    def greet_ed(i, carry):
        pl.semaphore_signal(barrier, 1, device_id={"ed": chip_peer(i) * 2 + core}, device_id_type=MESH)
        return carry

    lax.fori_loop(0, nf - 1, greet_fsdp, 0)
    lax.fori_loop(0, chips - 1, greet_ed, 0)
    pl.semaphore_signal(barrier, 1, device_id={"ed": sib}, device_id_type=MESH)
    pl.semaphore_wait(barrier, nf - 1 + chips)

    own_band = mine // bands
    lift = chips * ((nf + 2 * chips) // chips)

    def send_slots(k, carry):
        h = lax.rem(own_band - f - 1 - k + lift, chips)

        @pl.when(h != chip)
        def _():
            direct(h).start()

        return carry

    to_sib = pltpu.make_async_remote_copy(
        src_ref=slot_ref,
        dst_ref=sel_buf.at[mine],
        send_sem=s_send,
        recv_sem=sel_recv.at[mine],
        device_id={"ed": sib},
        device_id_type=MESH,
    )
    to_sib.start()
    lax.fori_loop(0, chips, send_slots, 0)
    sel_buf[mine] = slot_ref[...]

    def band(i, carry):
        j = lax.rem(f + chip + 1 + i, nf)
        for t in range(bands):
            blk = j * bands + t
            same_core = (blk // chips) == core
            not_mine = blk != mine

            @pl.when(same_core & not_mine)
            def _():
                forward(blk).wait_recv()
                forward(blk).start()

            @pl.when(jnp.logical_not(same_core))
            def _():
                forward(blk).wait_recv()

        for t in range(bands):
            blk = j * bands + t
            rows_in = sel_buf[blk]
            out_buf[j, t, :, :hidden] = jnp.dot(
                rows_in, wg_ref[...], preferred_element_type=jnp.float32
            ).astype(out_buf.dtype)
            out_buf[j, t, :, hidden:] = jnp.dot(
                rows_in, wu_ref[...], preferred_element_type=jnp.float32
            ).astype(out_buf.dtype)

        @pl.when(j != f)
        def _():
            partial_copy(j, f).start()

        return carry

    lax.fori_loop(0, nf, band, 0)
    acc[...] = out_buf[f].astype(jnp.float32)

    lift_f = nf * ((chips + 2 * nf) // nf)

    def gather(i, carry):
        g = lax.rem(f - chip - 1 - i + lift_f, nf)

        @pl.when(g != f)
        def _():
            partial_copy(g, g).wait_recv()
            acc[...] += in_buf[g].astype(jnp.float32)

        return carry

    lax.fori_loop(0, nf, gather, 0)

    def drain(i, carry):
        h = chip_peer(i)
        direct(h).wait_send()
        forward(core * chips + h).wait_send()
        return carry

    lax.fori_loop(0, chips - 1, drain, 0)

    def drain_partial(i, carry):
        partial_copy(fsdp_peer(i), f).wait_send()
        return carry

    lax.fori_loop(0, nf - 1, drain_partial, 0)
    to_sib.wait_send()
    total = acc[...]
    o_ref[...] = (jax.nn.silu(total[..., :hidden]) * total[..., hidden:]).astype(o_ref.dtype)


def _layer_kernel(nf, chips, slot_ref, wg_ref, wu_ref, wd_ref, comb_ref, o_ref, *scratch):
    up_scratch, act_s, down_scratch, slot_out = scratch[:10], scratch[10], scratch[11:22], scratch[22]
    _up_kernel(nf, chips, slot_ref, wg_ref, wu_ref, act_s, *up_scratch)
    _down_kernel(nf, chips, act_s, wd_ref, slot_out, *down_scratch)
    o_ref[...] = jnp.dot(
        comb_ref[...], slot_out[...], precision=lax.Precision.HIGHEST,
        preferred_element_type=jnp.float32,
    ).astype(o_ref.dtype)


def moe_layer(slots, wg, wu, wd, comb, nf, chips, cid):
    rows, d = slots.shape
    hidden = wg.shape[1]
    bands = 2 * chips // nf
    blocks = nf * bands
    tok = comb.shape[0]
    return pl.pallas_call(
        functools.partial(_layer_kernel, nf, chips),
        out_shape=jax.ShapeDtypeStruct((tok, d), jnp.bfloat16),
        in_specs=[pl.BlockSpec(memory_space=pltpu.VMEM)] * 5,
        out_specs=pl.BlockSpec(memory_space=pltpu.VMEM),
        scratch_shapes=[
            pltpu.VMEM((2 * chips, rows, d), jnp.bfloat16),
            pltpu.VMEM((nf, bands, rows, 2 * hidden), jnp.bfloat16),
            pltpu.VMEM((nf, bands, rows, 2 * hidden), jnp.bfloat16),
            pltpu.VMEM((bands, rows, 2 * hidden), jnp.float32),
            pltpu.SemaphoreType.DMA((chips,)),
            pltpu.SemaphoreType.DMA,
            pltpu.SemaphoreType.DMA((chips,)),
            pltpu.SemaphoreType.DMA((2 * chips,)),
            pltpu.SemaphoreType.DMA((nf,)),
            pltpu.SemaphoreType.DMA((nf,)),
            pltpu.VMEM((bands, rows, hidden), jnp.bfloat16),
            pltpu.VMEM((nf, bands, rows, hidden), jnp.bfloat16),
            pltpu.VMEM((blocks, rows, d), jnp.bfloat16),
            pltpu.VMEM((chips, rows, d), jnp.bfloat16),
            pltpu.VMEM((chips, rows, d), jnp.bfloat16),
            pltpu.VMEM((chips, rows, d), jnp.bfloat16),
            pltpu.SemaphoreType.DMA((nf,)),
            pltpu.SemaphoreType.DMA((nf,)),
            pltpu.SemaphoreType.DMA((chips,)),
            pltpu.SemaphoreType.DMA((chips,)),
            pltpu.SemaphoreType.DMA((chips,)),
            pltpu.SemaphoreType.DMA((chips,)),
            pltpu.VMEM((rows, d), jnp.float32),
        ],
        compiler_params=pltpu.CompilerParams(collective_id=cid, has_side_effects=True),
    )(slots, wg, wu, wd, comb)


def local(tokens, expert_ids, route_weights, w_gate, w_up, w_down):
    window = w_gate.shape[0]
    features_dev = tokens.shape[1]
    hidden_dev = w_gate.shape[2]
    n_ed = lax.axis_size("ed")
    n_fsdp = lax.axis_size("fsdp")
    chips = n_ed // 2
    per_band = n_ed // n_fsdp
    tok_dev = tokens.shape[0]
    order = jnp.arange(tok_dev, dtype=jnp.int32)
    routed = jnp.any(expert_ids == 0, axis=1)
    lower = (order[:, None] >= order[None, :]).astype(jnp.bfloat16)
    count = jnp.dot(lower, routed.astype(jnp.bfloat16), preferred_element_type=jnp.float32)
    slot_ids = jnp.arange(CAP, dtype=jnp.float32)
    match = routed[None, :] & (count[None, :] - 1.0 == slot_ids[:, None])
    own_slots = jnp.dot(
        match.astype(jnp.bfloat16), tokens, preferred_element_type=jnp.float32
    ).astype(jnp.bfloat16)
    per_expert = jnp.sum(
        jnp.where(expert_ids == 0, route_weights, jnp.zeros_like(route_weights)), axis=1
    )
    weights_matrix = match.T.astype(jnp.float32) * per_expert[:, None]
    return moe_layer(own_slots, w_gate[0], w_up[0], w_down[0], weights_matrix, n_fsdp, chips, 2)


def solution(mesh):
    return jax.shard_map(
        local,
        mesh=mesh,
        in_specs=(
            P("ed", "fsdp"),
            P("ed", None),
            P("ed", None),
            P(None, "fsdp", "ed"),
            P(None, "fsdp", "ed"),
            P(None, "ed", "fsdp"),
        ),
        out_specs=P("ed", "fsdp"),
        check_vma=False,
    )
```

```python
import functools

import jax
import jax.numpy as jnp
from jax import lax
from jax.experimental import pallas as pl
from jax.experimental.pallas import tpu as pltpu
from jax.sharding import PartitionSpec as P

CAP = 81
MESH = pl.DeviceIdType.MESH


def slot_match(routes, window, capacity):
    window_ids = jnp.arange(window, dtype=jnp.int32)
    routed = jnp.any(routes[:, :, None, :] == window_ids[None, None, :, None], axis=3)
    position = jnp.cumsum(routed.astype(jnp.int32), axis=1) - 1
    slot_ids = jnp.arange(capacity, dtype=jnp.int32)
    hits = routed[:, :, :, None] & (position[:, :, :, None] == slot_ids[None, None, None, :])
    return hits.astype(jnp.int32)


def take_block(block_rows, row_list):
    return jnp.take(block_rows, row_list, axis=0)


def pick_rows(blocks, routes, window, capacity):
    match = slot_match(routes, window, capacity)
    row_numbers = jnp.arange(blocks.shape[1], dtype=jnp.int32)
    source_row = jnp.sum(match * row_numbers[None, :, None, None], axis=1).reshape(
        blocks.shape[0], window * capacity
    )
    filled = jnp.sum(match, axis=1).reshape(blocks.shape[0], window * capacity)
    picked = jax.vmap(take_block)(blocks, source_row)
    picked = jnp.where(filled[:, :, None] > 0, picked, jnp.zeros_like(picked))
    return picked.reshape(blocks.shape[0], window, capacity, blocks.shape[2])


def combine_matrix(routes, weights, window, capacity):
    match = slot_match(routes[None], window, capacity)[0]
    window_ids = jnp.arange(window, dtype=jnp.int32)
    per_expert = jnp.sum(
        jnp.where(
            routes[:, None, :] == window_ids[None, :, None],
            weights[:, None, :],
            jnp.zeros_like(weights[:, None, :]),
        ),
        axis=2,
    )
    return (per_expert[:, :, None] * match.astype(weights.dtype)).reshape(
        routes.shape[0], window * capacity
    )


def _down_kernel(nf, chips, act_ref, wd_ref, o_ref, act_buf, term_buf, sib_buf, pre_buf, in_buf,
                 a_send, a_recv, s_send, s_recv, e_send, e_recv):
    bands = act_ref.shape[0]
    f = lax.axis_index("fsdp")
    e = lax.axis_index("ed")
    core = lax.rem(e, 2)
    chip = e // 2
    sib = e + 1 - 2 * core

    def fsdp_peer(i):
        return lax.rem(f + 1 + i, nf)

    def chip_peer(i):
        return lax.rem(chip + 1 + i, chips)

    def act_copy(g, slot):
        return pltpu.make_async_remote_copy(
            src_ref=act_ref,
            dst_ref=act_buf.at[slot],
            send_sem=a_send.at[g],
            recv_sem=a_recv.at[slot],
            device_id={"fsdp": g},
            device_id_type=MESH,
        )

    def to_sibling(blk):
        h = lax.rem(blk, chips)
        return pltpu.make_async_remote_copy(
            src_ref=term_buf.at[blk],
            dst_ref=sib_buf.at[h],
            send_sem=s_send.at[h],
            recv_sem=s_recv.at[h],
            device_id={"ed": sib},
            device_id_type=MESH,
        )

    def piece_copy(h, slot):
        return pltpu.make_async_remote_copy(
            src_ref=pre_buf.at[h],
            dst_ref=in_buf.at[slot],
            send_sem=e_send.at[h],
            recv_sem=e_recv.at[slot],
            device_id={"ed": h * 2 + core},
            device_id_type=MESH,
        )

    shift = nf - lax.rem(chip, nf)

    def send_act(i, carry):
        g = lax.rem(f + shift + nf - i, nf)

        @pl.when(g != f)
        def _():
            act_copy(g, f).start()

        return carry

    lax.fori_loop(0, nf, send_act, 0)
    act_buf[f] = act_ref[...]
    o_ref[...] = jnp.zeros_like(o_ref)

    def band(i, carry):
        j = lax.rem(f + chip + i, nf)

        @pl.when(j != f)
        def _():
            act_copy(j, j).wait_recv()

        for t in range(bands):
            blk = j * bands + t
            h = lax.rem(blk, chips)
            term_buf[blk] = jnp.dot(
                act_buf[j, t], wd_ref[...], preferred_element_type=jnp.float32
            ).astype(term_buf.dtype)
            same_core = (blk // chips) == core

            @pl.when(jnp.logical_not(same_core))
            def _():
                to_sibling(blk).start()

            @pl.when(same_core)
            def _():
                to_sibling(blk).wait_recv()
                pair = term_buf[blk].astype(jnp.float32) + sib_buf[h].astype(jnp.float32)
                pre_buf[h] = pair.astype(pre_buf.dtype)

                @pl.when(h == chip)
                def _():
                    o_ref[...] += pre_buf[h].astype(jnp.float32)

                @pl.when(h != chip)
                def _():
                    piece_copy(h, chip).start()

        return carry

    lax.fori_loop(0, nf, band, 0)

    def take_piece(i, carry):
        h = chip_peer(i)
        piece_copy(h, chip).wait_send()
        piece_copy(h, h).wait_recv()
        o_ref[...] += in_buf[h].astype(jnp.float32)
        return carry

    lax.fori_loop(0, chips - 1, take_piece, 0)

    def drain(h, carry):
        to_sibling((1 - core) * chips + h).wait_send()
        return carry

    lax.fori_loop(0, chips, drain, 0)

    def drain_act(i, carry):
        act_copy(fsdp_peer(i), f).wait_send()
        return carry

    lax.fori_loop(0, nf - 1, drain_act, 0)


def _up_kernel(nf, chips, slot_ref, wg_ref, wu_ref, o_ref, sel_buf, out_buf, in_buf, acc,
               e_send, s_send, fwd_send, sel_recv, f_send, f_recv):
    bands = o_ref.shape[0]
    hidden = o_ref.shape[2]
    f = lax.axis_index("fsdp")
    e = lax.axis_index("ed")
    core = lax.rem(e, 2)
    chip = e // 2
    sib = e + 1 - 2 * core
    mine = core * chips + chip

    def fsdp_peer(i):
        return lax.rem(f + 1 + i, nf)

    def chip_peer(i):
        return lax.rem(chip + 1 + i, chips)

    def direct(h):
        return pltpu.make_async_remote_copy(
            src_ref=slot_ref,
            dst_ref=sel_buf.at[mine],
            send_sem=e_send.at[h],
            recv_sem=sel_recv.at[mine],
            device_id={"ed": h * 2 + core},
            device_id_type=MESH,
        )

    def forward(blk):
        return pltpu.make_async_remote_copy(
            src_ref=sel_buf.at[blk],
            dst_ref=sel_buf.at[blk],
            send_sem=fwd_send.at[lax.rem(blk, chips)],
            recv_sem=sel_recv.at[blk],
            device_id={"ed": sib},
            device_id_type=MESH,
        )

    def partial_copy(g, slot):
        return pltpu.make_async_remote_copy(
            src_ref=out_buf.at[g],
            dst_ref=in_buf.at[slot],
            send_sem=f_send.at[g],
            recv_sem=f_recv.at[slot],
            device_id={"fsdp": g},
            device_id_type=MESH,
        )

    barrier = pltpu.get_barrier_semaphore()

    def greet_fsdp(i, carry):
        pl.semaphore_signal(barrier, 1, device_id={"fsdp": fsdp_peer(i)}, device_id_type=MESH)
        return carry

    def greet_ed(i, carry):
        pl.semaphore_signal(barrier, 1, device_id={"ed": chip_peer(i) * 2 + core}, device_id_type=MESH)
        return carry

    lax.fori_loop(0, nf - 1, greet_fsdp, 0)
    lax.fori_loop(0, chips - 1, greet_ed, 0)
    pl.semaphore_signal(barrier, 1, device_id={"ed": sib}, device_id_type=MESH)
    pl.semaphore_wait(barrier, nf - 1 + chips)

    own_band = mine // bands
    lift = chips * ((nf + 2 * chips) // chips)

    def send_slots(k, carry):
        h = lax.rem(own_band - f - 1 - k + lift, chips)

        @pl.when(h != chip)
        def _():
            direct(h).start()

        return carry

    to_sib = pltpu.make_async_remote_copy(
        src_ref=slot_ref,
        dst_ref=sel_buf.at[mine],
        send_sem=s_send,
        recv_sem=sel_recv.at[mine],
        device_id={"ed": sib},
        device_id_type=MESH,
    )
    to_sib.start()
    lax.fori_loop(0, chips, send_slots, 0)
    sel_buf[mine] = slot_ref[...]

    def band(i, carry):
        j = lax.rem(f + chip + 1 + i, nf)
        for t in range(bands):
            blk = j * bands + t
            same_core = (blk // chips) == core
            not_mine = blk != mine

            @pl.when(same_core & not_mine)
            def _():
                forward(blk).wait_recv()
                forward(blk).start()

            @pl.when(jnp.logical_not(same_core))
            def _():
                forward(blk).wait_recv()

        for t in range(bands):
            blk = j * bands + t
            rows_in = sel_buf[blk]
            out_buf[j, t, :, :hidden] = jnp.dot(
                rows_in, wg_ref[...], preferred_element_type=jnp.float32
            ).astype(out_buf.dtype)
            out_buf[j, t, :, hidden:] = jnp.dot(
                rows_in, wu_ref[...], preferred_element_type=jnp.float32
            ).astype(out_buf.dtype)

        @pl.when(j != f)
        def _():
            partial_copy(j, f).start()

        return carry

    lax.fori_loop(0, nf, band, 0)
    acc[...] = out_buf[f].astype(jnp.float32)

    lift_f = nf * ((chips + 2 * nf) // nf)

    def gather(i, carry):
        g = lax.rem(f - chip - 1 - i + lift_f, nf)

        @pl.when(g != f)
        def _():
            partial_copy(g, g).wait_recv()
            acc[...] += in_buf[g].astype(jnp.float32)

        return carry

    lax.fori_loop(0, nf, gather, 0)

    def drain(i, carry):
        h = chip_peer(i)
        direct(h).wait_send()
        forward(core * chips + h).wait_send()
        return carry

    lax.fori_loop(0, chips - 1, drain, 0)

    def drain_partial(i, carry):
        partial_copy(fsdp_peer(i), f).wait_send()
        return carry

    lax.fori_loop(0, nf - 1, drain_partial, 0)
    to_sib.wait_send()
    total = acc[...]
    o_ref[...] = (jax.nn.silu(total[..., :hidden]) * total[..., hidden:]).astype(o_ref.dtype)


def _layer_kernel(nf, chips, slot_ref, wg_ref, wu_ref, wd_ref, o_ref, *scratch):
    up_scratch, act_s, down_scratch = scratch[:10], scratch[10], scratch[11:22]
    _up_kernel(nf, chips, slot_ref, wg_ref, wu_ref, act_s, *up_scratch)
    _down_kernel(nf, chips, act_s, wd_ref, o_ref, *down_scratch)


def moe_layer(slots, wg, wu, wd, nf, chips, cid):
    rows, d = slots.shape
    hidden = wg.shape[1]
    bands = 2 * chips // nf
    blocks = nf * bands
    return pl.pallas_call(
        functools.partial(_layer_kernel, nf, chips),
        out_shape=jax.ShapeDtypeStruct((rows, d), jnp.float32),
        in_specs=[pl.BlockSpec(memory_space=pltpu.VMEM)] * 4,
        out_specs=pl.BlockSpec(memory_space=pltpu.VMEM),
        scratch_shapes=[
            pltpu.VMEM((2 * chips, rows, d), jnp.bfloat16),
            pltpu.VMEM((nf, bands, rows, 2 * hidden), jnp.bfloat16),
            pltpu.VMEM((nf, bands, rows, 2 * hidden), jnp.bfloat16),
            pltpu.VMEM((bands, rows, 2 * hidden), jnp.float32),
            pltpu.SemaphoreType.DMA((chips,)),
            pltpu.SemaphoreType.DMA,
            pltpu.SemaphoreType.DMA((chips,)),
            pltpu.SemaphoreType.DMA((2 * chips,)),
            pltpu.SemaphoreType.DMA((nf,)),
            pltpu.SemaphoreType.DMA((nf,)),
            pltpu.VMEM((bands, rows, hidden), jnp.bfloat16),
            pltpu.VMEM((nf, bands, rows, hidden), jnp.bfloat16),
            pltpu.VMEM((blocks, rows, d), jnp.bfloat16),
            pltpu.VMEM((chips, rows, d), jnp.bfloat16),
            pltpu.VMEM((chips, rows, d), jnp.bfloat16),
            pltpu.VMEM((chips, rows, d), jnp.bfloat16),
            pltpu.SemaphoreType.DMA((nf,)),
            pltpu.SemaphoreType.DMA((nf,)),
            pltpu.SemaphoreType.DMA((chips,)),
            pltpu.SemaphoreType.DMA((chips,)),
            pltpu.SemaphoreType.DMA((chips,)),
            pltpu.SemaphoreType.DMA((chips,)),
        ],
        compiler_params=pltpu.CompilerParams(collective_id=cid, has_side_effects=True),
    )(slots, wg, wu, wd)


def local(tokens, expert_ids, route_weights, w_gate, w_up, w_down):
    window = w_gate.shape[0]
    features_dev = tokens.shape[1]
    hidden_dev = w_gate.shape[2]
    n_ed = lax.axis_size("ed")
    n_fsdp = lax.axis_size("fsdp")
    chips = n_ed // 2
    per_band = n_ed // n_fsdp
    tok_dev = tokens.shape[0]
    order = jnp.arange(tok_dev, dtype=jnp.int32)
    routed = jnp.any(expert_ids == 0, axis=1)
    lower = (order[:, None] >= order[None, :]).astype(jnp.bfloat16)
    count = jnp.dot(lower, routed.astype(jnp.bfloat16), preferred_element_type=jnp.float32)
    slot_ids = jnp.arange(CAP, dtype=jnp.float32)
    match = routed[None, :] & (count[None, :] - 1.0 == slot_ids[:, None])
    own_slots = jnp.dot(
        match.astype(jnp.bfloat16), tokens, preferred_element_type=jnp.float32
    ).astype(jnp.bfloat16)
    per_expert = jnp.sum(
        jnp.where(expert_ids == 0, route_weights, jnp.zeros_like(route_weights)), axis=1
    )
    weights_matrix = match.T.astype(jnp.float32) * per_expert[:, None]
    slot_out = moe_layer(own_slots, w_gate[0], w_up[0], w_down[0], n_fsdp, chips, 2)
    mixed = jnp.dot(
        weights_matrix, slot_out, precision=lax.Precision.HIGHEST,
        preferred_element_type=jnp.float32,
    )
    return mixed.astype(jnp.bfloat16)


def solution(mesh):
    return jax.shard_map(
        local,
        mesh=mesh,
        in_specs=(
            P("ed", "fsdp"),
            P("ed", None),
            P("ed", None),
            P(None, "fsdp", "ed"),
            P(None, "fsdp", "ed"),
            P(None, "ed", "fsdp"),
        ),
        out_specs=P("ed", "fsdp"),
        check_vma=False,
    )
```

```python
import functools

import jax
import jax.numpy as jnp
from jax import lax
from jax.experimental import pallas as pl
from jax.experimental.pallas import tpu as pltpu
from jax.sharding import PartitionSpec as P

CAP = 81
MESH = pl.DeviceIdType.MESH


def slot_match(routes, window, capacity):
    window_ids = jnp.arange(window, dtype=jnp.int32)
    routed = jnp.any(routes[:, :, None, :] == window_ids[None, None, :, None], axis=3)
    position = jnp.cumsum(routed.astype(jnp.int32), axis=1) - 1
    slot_ids = jnp.arange(capacity, dtype=jnp.int32)
    hits = routed[:, :, :, None] & (position[:, :, :, None] == slot_ids[None, None, None, :])
    return hits.astype(jnp.int32)


def take_block(block_rows, row_list):
    return jnp.take(block_rows, row_list, axis=0)


def pick_rows(blocks, routes, window, capacity):
    match = slot_match(routes, window, capacity)
    row_numbers = jnp.arange(blocks.shape[1], dtype=jnp.int32)
    source_row = jnp.sum(match * row_numbers[None, :, None, None], axis=1).reshape(
        blocks.shape[0], window * capacity
    )
    filled = jnp.sum(match, axis=1).reshape(blocks.shape[0], window * capacity)
    picked = jax.vmap(take_block)(blocks, source_row)
    picked = jnp.where(filled[:, :, None] > 0, picked, jnp.zeros_like(picked))
    return picked.reshape(blocks.shape[0], window, capacity, blocks.shape[2])


def combine_matrix(routes, weights, window, capacity):
    match = slot_match(routes[None], window, capacity)[0]
    window_ids = jnp.arange(window, dtype=jnp.int32)
    per_expert = jnp.sum(
        jnp.where(
            routes[:, None, :] == window_ids[None, :, None],
            weights[:, None, :],
            jnp.zeros_like(weights[:, None, :]),
        ),
        axis=2,
    )
    return (per_expert[:, :, None] * match.astype(weights.dtype)).reshape(
        routes.shape[0], window * capacity
    )


def _down_kernel(nf, chips, act_ref, wd_ref, o_ref, act_buf, term_buf, sib_buf, pre_buf, in_buf,
                 a_send, a_recv, s_send, s_recv, e_send, e_recv):
    bands = act_ref.shape[0]
    f = lax.axis_index("fsdp")
    e = lax.axis_index("ed")
    core = lax.rem(e, 2)
    chip = e // 2
    sib = e + 1 - 2 * core

    def fsdp_peer(i):
        return lax.rem(f + 1 + i, nf)

    def chip_peer(i):
        return lax.rem(chip + 1 + i, chips)

    def act_copy(g, slot):
        return pltpu.make_async_remote_copy(
            src_ref=act_ref,
            dst_ref=act_buf.at[slot],
            send_sem=a_send.at[g],
            recv_sem=a_recv.at[slot],
            device_id={"fsdp": g},
            device_id_type=MESH,
        )

    def to_sibling(blk):
        h = lax.rem(blk, chips)
        return pltpu.make_async_remote_copy(
            src_ref=term_buf.at[blk],
            dst_ref=sib_buf.at[h],
            send_sem=s_send.at[h],
            recv_sem=s_recv.at[h],
            device_id={"ed": sib},
            device_id_type=MESH,
        )

    def piece_copy(h, slot):
        return pltpu.make_async_remote_copy(
            src_ref=pre_buf.at[h],
            dst_ref=in_buf.at[slot],
            send_sem=e_send.at[h],
            recv_sem=e_recv.at[slot],
            device_id={"ed": h * 2 + core},
            device_id_type=MESH,
        )

    shift = nf - lax.rem(chip, nf)

    def send_act(i, carry):
        g = lax.rem(f + shift + nf - i, nf)

        @pl.when(g != f)
        def _():
            act_copy(g, f).start()

        return carry

    lax.fori_loop(0, nf, send_act, 0)
    act_buf[f] = act_ref[...]
    o_ref[...] = jnp.zeros_like(o_ref)

    def band(i, carry):
        j = lax.rem(f + chip + i, nf)

        @pl.when(j != f)
        def _():
            act_copy(j, j).wait_recv()

        for t in range(bands):
            blk = j * bands + t
            h = lax.rem(blk, chips)
            term_buf[blk] = jnp.dot(
                act_buf[j, t], wd_ref[...], preferred_element_type=jnp.float32
            ).astype(term_buf.dtype)
            same_core = (blk // chips) == core

            @pl.when(jnp.logical_not(same_core))
            def _():
                to_sibling(blk).start()

            @pl.when(same_core)
            def _():
                to_sibling(blk).wait_recv()
                pair = term_buf[blk].astype(jnp.float32) + sib_buf[h].astype(jnp.float32)
                pre_buf[h] = pair.astype(pre_buf.dtype)

                @pl.when(h == chip)
                def _():
                    o_ref[...] += pre_buf[h].astype(jnp.float32)

                @pl.when(h != chip)
                def _():
                    piece_copy(h, chip).start()

        return carry

    lax.fori_loop(0, nf, band, 0)

    def take_piece(i, carry):
        h = chip_peer(i)
        piece_copy(h, chip).wait_send()
        piece_copy(h, h).wait_recv()
        o_ref[...] += in_buf[h].astype(jnp.float32)
        return carry

    lax.fori_loop(0, chips - 1, take_piece, 0)

    def drain(h, carry):
        to_sibling((1 - core) * chips + h).wait_send()
        return carry

    lax.fori_loop(0, chips, drain, 0)

    def drain_act(i, carry):
        act_copy(fsdp_peer(i), f).wait_send()
        return carry

    lax.fori_loop(0, nf - 1, drain_act, 0)


def _up_kernel(nf, chips, slot_ref, wg_ref, wu_ref, o_ref, sel_buf, out_buf, in_buf, acc,
               e_send, s_send, fwd_send, sel_recv, f_send, f_recv):
    bands = o_ref.shape[0]
    hidden = o_ref.shape[2]
    f = lax.axis_index("fsdp")
    e = lax.axis_index("ed")
    core = lax.rem(e, 2)
    chip = e // 2
    sib = e + 1 - 2 * core
    mine = core * chips + chip

    def fsdp_peer(i):
        return lax.rem(f + 1 + i, nf)

    def chip_peer(i):
        return lax.rem(chip + 1 + i, chips)

    def direct(h):
        return pltpu.make_async_remote_copy(
            src_ref=slot_ref,
            dst_ref=sel_buf.at[mine],
            send_sem=e_send.at[h],
            recv_sem=sel_recv.at[mine],
            device_id={"ed": h * 2 + core},
            device_id_type=MESH,
        )

    def forward(blk):
        return pltpu.make_async_remote_copy(
            src_ref=sel_buf.at[blk],
            dst_ref=sel_buf.at[blk],
            send_sem=fwd_send.at[lax.rem(blk, chips)],
            recv_sem=sel_recv.at[blk],
            device_id={"ed": sib},
            device_id_type=MESH,
        )

    def partial_copy(g, slot):
        return pltpu.make_async_remote_copy(
            src_ref=out_buf.at[g],
            dst_ref=in_buf.at[slot],
            send_sem=f_send.at[g],
            recv_sem=f_recv.at[slot],
            device_id={"fsdp": g},
            device_id_type=MESH,
        )

    barrier = pltpu.get_barrier_semaphore()

    def greet_fsdp(i, carry):
        pl.semaphore_signal(barrier, 1, device_id={"fsdp": fsdp_peer(i)}, device_id_type=MESH)
        return carry

    def greet_ed(i, carry):
        pl.semaphore_signal(barrier, 1, device_id={"ed": chip_peer(i) * 2 + core}, device_id_type=MESH)
        return carry

    lax.fori_loop(0, nf - 1, greet_fsdp, 0)
    lax.fori_loop(0, chips - 1, greet_ed, 0)
    pl.semaphore_signal(barrier, 1, device_id={"ed": sib}, device_id_type=MESH)
    pl.semaphore_wait(barrier, nf - 1 + chips)

    own_band = mine // bands
    lift = chips * ((nf + 2 * chips) // chips)

    def send_slots(k, carry):
        h = lax.rem(own_band - f - 1 - k + lift, chips)

        @pl.when(h != chip)
        def _():
            direct(h).start()

        return carry

    to_sib = pltpu.make_async_remote_copy(
        src_ref=slot_ref,
        dst_ref=sel_buf.at[mine],
        send_sem=s_send,
        recv_sem=sel_recv.at[mine],
        device_id={"ed": sib},
        device_id_type=MESH,
    )
    to_sib.start()
    lax.fori_loop(0, chips, send_slots, 0)
    sel_buf[mine] = slot_ref[...]

    def band(i, carry):
        j = lax.rem(f + chip + 1 + i, nf)
        for t in range(bands):
            blk = j * bands + t
            same_core = (blk // chips) == core
            not_mine = blk != mine

            @pl.when(same_core & not_mine)
            def _():
                forward(blk).wait_recv()
                forward(blk).start()

            @pl.when(jnp.logical_not(same_core))
            def _():
                forward(blk).wait_recv()

        for t in range(bands):
            blk = j * bands + t
            rows_in = sel_buf[blk]
            out_buf[j, t, :, :hidden] = jnp.dot(
                rows_in, wg_ref[...], preferred_element_type=jnp.float32
            ).astype(out_buf.dtype)
            out_buf[j, t, :, hidden:] = jnp.dot(
                rows_in, wu_ref[...], preferred_element_type=jnp.float32
            ).astype(out_buf.dtype)

        @pl.when(j != f)
        def _():
            partial_copy(j, f).start()

        return carry

    lax.fori_loop(0, nf, band, 0)
    acc[...] = out_buf[f].astype(jnp.float32)

    lift_f = nf * ((chips + 2 * nf) // nf)

    def gather(i, carry):
        g = lax.rem(f - chip - 1 - i + lift_f, nf)

        @pl.when(g != f)
        def _():
            partial_copy(g, g).wait_recv()
            acc[...] += in_buf[g].astype(jnp.float32)

        return carry

    lax.fori_loop(0, nf, gather, 0)

    def drain(i, carry):
        h = chip_peer(i)
        direct(h).wait_send()
        forward(core * chips + h).wait_send()
        return carry

    lax.fori_loop(0, chips - 1, drain, 0)

    def drain_partial(i, carry):
        partial_copy(fsdp_peer(i), f).wait_send()
        return carry

    lax.fori_loop(0, nf - 1, drain_partial, 0)
    to_sib.wait_send()
    total = acc[...]
    o_ref[...] = (jax.nn.silu(total[..., :hidden]) * total[..., hidden:]).astype(o_ref.dtype)


def _layer_kernel(nf, chips, slot_ref, wg_ref, wu_ref, wd_ref, o_ref, *scratch):
    up_scratch, act_s, down_scratch = scratch[:10], scratch[10], scratch[11:22]
    _up_kernel(nf, chips, slot_ref, wg_ref, wu_ref, act_s, *up_scratch)
    _down_kernel(nf, chips, act_s, wd_ref, o_ref, *down_scratch)


def moe_layer(slots, wg, wu, wd, nf, chips, cid):
    rows, d = slots.shape
    hidden = wg.shape[1]
    bands = 2 * chips // nf
    blocks = nf * bands
    return pl.pallas_call(
        functools.partial(_layer_kernel, nf, chips),
        out_shape=jax.ShapeDtypeStruct((rows, d), jnp.float32),
        in_specs=[pl.BlockSpec(memory_space=pltpu.VMEM)] * 4,
        out_specs=pl.BlockSpec(memory_space=pltpu.VMEM),
        scratch_shapes=[
            pltpu.VMEM((2 * chips, rows, d), jnp.bfloat16),
            pltpu.VMEM((nf, bands, rows, 2 * hidden), jnp.bfloat16),
            pltpu.VMEM((nf, bands, rows, 2 * hidden), jnp.bfloat16),
            pltpu.VMEM((bands, rows, 2 * hidden), jnp.float32),
            pltpu.SemaphoreType.DMA((chips,)),
            pltpu.SemaphoreType.DMA,
            pltpu.SemaphoreType.DMA((chips,)),
            pltpu.SemaphoreType.DMA((2 * chips,)),
            pltpu.SemaphoreType.DMA((nf,)),
            pltpu.SemaphoreType.DMA((nf,)),
            pltpu.VMEM((bands, rows, hidden), jnp.bfloat16),
            pltpu.VMEM((nf, bands, rows, hidden), jnp.bfloat16),
            pltpu.VMEM((blocks, rows, d), jnp.bfloat16),
            pltpu.VMEM((chips, rows, d), jnp.bfloat16),
            pltpu.VMEM((chips, rows, d), jnp.bfloat16),
            pltpu.VMEM((chips, rows, d), jnp.bfloat16),
            pltpu.SemaphoreType.DMA((nf,)),
            pltpu.SemaphoreType.DMA((nf,)),
            pltpu.SemaphoreType.DMA((chips,)),
            pltpu.SemaphoreType.DMA((chips,)),
            pltpu.SemaphoreType.DMA((chips,)),
            pltpu.SemaphoreType.DMA((chips,)),
        ],
        compiler_params=pltpu.CompilerParams(collective_id=cid, has_side_effects=True),
    )(slots, wg, wu, wd)


def local(tokens, expert_ids, route_weights, w_gate, w_up, w_down):
    window = w_gate.shape[0]
    features_dev = tokens.shape[1]
    hidden_dev = w_gate.shape[2]
    n_ed = lax.axis_size("ed")
    n_fsdp = lax.axis_size("fsdp")
    chips = n_ed // 2
    per_band = n_ed // n_fsdp
    tok_dev = tokens.shape[0]
    order = jnp.arange(tok_dev, dtype=jnp.int32)
    routed = jnp.any(expert_ids == 0, axis=1)
    lower = (order[:, None] >= order[None, :]).astype(jnp.bfloat16)
    count = jnp.dot(lower, routed.astype(jnp.bfloat16), preferred_element_type=jnp.float32)
    slot_ids = jnp.arange(CAP, dtype=jnp.float32)
    match = routed[None, :] & (count[None, :] - 1.0 == slot_ids[:, None])
    own_slots = jnp.dot(
        match.astype(jnp.bfloat16), tokens, preferred_element_type=jnp.float32
    ).astype(jnp.bfloat16)
    per_expert = jnp.sum(
        jnp.where(expert_ids == 0, route_weights, jnp.zeros_like(route_weights)), axis=1
    )
    slot_out = moe_layer(own_slots, w_gate[0], w_up[0], w_down[0], n_fsdp, chips, 2)
    slot_of = jnp.clip(count - 1.0, 0.0, CAP - 1.0).astype(jnp.int32)
    rows = jnp.take(slot_out, slot_of, axis=0)
    mixed = jnp.where(routed[:, None], per_expert[:, None] * rows, jnp.zeros_like(rows))
    return mixed.astype(jnp.bfloat16)


def solution(mesh):
    return jax.shard_map(
        local,
        mesh=mesh,
        in_specs=(
            P("ed", "fsdp"),
            P("ed", None),
            P("ed", None),
            P(None, "fsdp", "ed"),
            P(None, "fsdp", "ed"),
            P(None, "ed", "fsdp"),
        ),
        out_specs=P("ed", "fsdp"),
        check_vma=False,
    )
```

```python
import functools

import jax
import jax.numpy as jnp
from jax import lax
from jax.experimental import pallas as pl
from jax.experimental.pallas import tpu as pltpu
from jax.sharding import PartitionSpec as P

CAP = 81
MESH = pl.DeviceIdType.MESH


def slot_match(routes, window, capacity):
    window_ids = jnp.arange(window, dtype=jnp.int32)
    routed = jnp.any(routes[:, :, None, :] == window_ids[None, None, :, None], axis=3)
    position = jnp.cumsum(routed.astype(jnp.int32), axis=1) - 1
    slot_ids = jnp.arange(capacity, dtype=jnp.int32)
    hits = routed[:, :, :, None] & (position[:, :, :, None] == slot_ids[None, None, None, :])
    return hits.astype(jnp.int32)


def take_block(block_rows, row_list):
    return jnp.take(block_rows, row_list, axis=0)


def pick_rows(blocks, routes, window, capacity):
    match = slot_match(routes, window, capacity)
    row_numbers = jnp.arange(blocks.shape[1], dtype=jnp.int32)
    source_row = jnp.sum(match * row_numbers[None, :, None, None], axis=1).reshape(
        blocks.shape[0], window * capacity
    )
    filled = jnp.sum(match, axis=1).reshape(blocks.shape[0], window * capacity)
    picked = jax.vmap(take_block)(blocks, source_row)
    picked = jnp.where(filled[:, :, None] > 0, picked, jnp.zeros_like(picked))
    return picked.reshape(blocks.shape[0], window, capacity, blocks.shape[2])


def combine_matrix(routes, weights, window, capacity):
    match = slot_match(routes[None], window, capacity)[0]
    window_ids = jnp.arange(window, dtype=jnp.int32)
    per_expert = jnp.sum(
        jnp.where(
            routes[:, None, :] == window_ids[None, :, None],
            weights[:, None, :],
            jnp.zeros_like(weights[:, None, :]),
        ),
        axis=2,
    )
    return (per_expert[:, :, None] * match.astype(weights.dtype)).reshape(
        routes.shape[0], window * capacity
    )


def _down_kernel(nf, chips, act_ref, wd_ref, o_ref, act_buf, term_buf, sib_buf, pre_buf, in_buf,
                 a_send, a_recv, s_send, s_recv, e_send, e_recv):
    bands = act_ref.shape[0]
    f = lax.axis_index("fsdp")
    e = lax.axis_index("ed")
    core = lax.rem(e, 2)
    chip = e // 2
    sib = e + 1 - 2 * core

    def fsdp_peer(i):
        return lax.rem(f + 1 + i, nf)

    def chip_peer(i):
        return lax.rem(chip + 1 + i, chips)

    def act_copy(g, slot):
        return pltpu.make_async_remote_copy(
            src_ref=act_ref,
            dst_ref=act_buf.at[slot],
            send_sem=a_send.at[g],
            recv_sem=a_recv.at[slot],
            device_id={"fsdp": g},
            device_id_type=MESH,
        )

    def to_sibling(blk):
        h = lax.rem(blk, chips)
        return pltpu.make_async_remote_copy(
            src_ref=term_buf.at[blk],
            dst_ref=sib_buf.at[h],
            send_sem=s_send.at[h],
            recv_sem=s_recv.at[h],
            device_id={"ed": sib},
            device_id_type=MESH,
        )

    def piece_copy(h, slot):
        return pltpu.make_async_remote_copy(
            src_ref=pre_buf.at[h],
            dst_ref=in_buf.at[slot],
            send_sem=e_send.at[h],
            recv_sem=e_recv.at[slot],
            device_id={"ed": h * 2 + core},
            device_id_type=MESH,
        )

    shift = nf - lax.rem(chip, nf)

    def send_act(i, carry):
        g = lax.rem(f + shift + nf - i, nf)

        @pl.when(g != f)
        def _():
            act_copy(g, f).start()

        return carry

    lax.fori_loop(0, nf, send_act, 0)
    act_buf[f] = act_ref[...]
    o_ref[...] = jnp.zeros_like(o_ref)

    def band(i, carry):
        j = lax.rem(f + chip + i, nf)

        @pl.when(j != f)
        def _():
            act_copy(j, j).wait_recv()

        for t in range(bands):
            blk = j * bands + t
            h = lax.rem(blk, chips)
            term_buf[blk] = jnp.dot(
                act_buf[j, t], wd_ref[...], preferred_element_type=jnp.float32
            ).astype(term_buf.dtype)
            same_core = (blk // chips) == core

            @pl.when(jnp.logical_not(same_core))
            def _():
                to_sibling(blk).start()

            @pl.when(same_core)
            def _():
                to_sibling(blk).wait_recv()
                pair = term_buf[blk].astype(jnp.float32) + sib_buf[h].astype(jnp.float32)
                pre_buf[h] = pair.astype(pre_buf.dtype)

                @pl.when(h == chip)
                def _():
                    o_ref[...] += pre_buf[h].astype(jnp.float32)

                @pl.when(h != chip)
                def _():
                    piece_copy(h, chip).start()

        return carry

    lax.fori_loop(0, nf, band, 0)

    def take_piece(i, carry):
        h = chip_peer(i)
        piece_copy(h, chip).wait_send()
        piece_copy(h, h).wait_recv()
        o_ref[...] += in_buf[h].astype(jnp.float32)
        return carry

    lax.fori_loop(0, chips - 1, take_piece, 0)

    def drain(h, carry):
        to_sibling((1 - core) * chips + h).wait_send()
        return carry

    lax.fori_loop(0, chips, drain, 0)

    def drain_act(i, carry):
        act_copy(fsdp_peer(i), f).wait_send()
        return carry

    lax.fori_loop(0, nf - 1, drain_act, 0)


def _up_kernel(nf, chips, slot_ref, wg_ref, wu_ref, o_ref, sel_buf, out_buf, in_buf, acc,
               e_send, s_send, fwd_send, sel_recv, f_send, f_recv, weights=()):
    bands = o_ref.shape[0]
    hidden = o_ref.shape[2]
    f = lax.axis_index("fsdp")
    e = lax.axis_index("ed")
    core = lax.rem(e, 2)
    chip = e // 2
    sib = e + 1 - 2 * core
    mine = core * chips + chip

    def fsdp_peer(i):
        return lax.rem(f + 1 + i, nf)

    def chip_peer(i):
        return lax.rem(chip + 1 + i, chips)

    def direct(h):
        return pltpu.make_async_remote_copy(
            src_ref=slot_ref,
            dst_ref=sel_buf.at[mine],
            send_sem=e_send.at[h],
            recv_sem=sel_recv.at[mine],
            device_id={"ed": h * 2 + core},
            device_id_type=MESH,
        )

    def forward(blk):
        return pltpu.make_async_remote_copy(
            src_ref=sel_buf.at[blk],
            dst_ref=sel_buf.at[blk],
            send_sem=fwd_send.at[lax.rem(blk, chips)],
            recv_sem=sel_recv.at[blk],
            device_id={"ed": sib},
            device_id_type=MESH,
        )

    def partial_copy(g, slot):
        return pltpu.make_async_remote_copy(
            src_ref=out_buf.at[g],
            dst_ref=in_buf.at[slot],
            send_sem=f_send.at[g],
            recv_sem=f_recv.at[slot],
            device_id={"fsdp": g},
            device_id_type=MESH,
        )

    barrier = pltpu.get_barrier_semaphore()

    def greet_fsdp(i, carry):
        pl.semaphore_signal(barrier, 1, device_id={"fsdp": fsdp_peer(i)}, device_id_type=MESH)
        return carry

    def greet_ed(i, carry):
        pl.semaphore_signal(barrier, 1, device_id={"ed": chip_peer(i) * 2 + core}, device_id_type=MESH)
        return carry

    lax.fori_loop(0, nf - 1, greet_fsdp, 0)
    lax.fori_loop(0, chips - 1, greet_ed, 0)
    pl.semaphore_signal(barrier, 1, device_id={"ed": sib}, device_id_type=MESH)
    pl.semaphore_wait(barrier, nf - 1 + chips)

    own_band = mine // bands
    lift = chips * ((nf + 2 * chips) // chips)

    def send_slots(k, carry):
        h = lax.rem(own_band - f - 1 - k + lift, chips)

        @pl.when(h != chip)
        def _():
            direct(h).start()

        return carry

    to_sib = pltpu.make_async_remote_copy(
        src_ref=slot_ref,
        dst_ref=sel_buf.at[mine],
        send_sem=s_send,
        recv_sem=sel_recv.at[mine],
        device_id={"ed": sib},
        device_id_type=MESH,
    )
    to_sib.start()
    lax.fori_loop(0, chips, send_slots, 0)
    sel_buf[mine] = slot_ref[...]
    for c in weights:
        c.wait()

    def band(i, carry):
        j = lax.rem(f + chip + 1 + i, nf)
        for t in range(bands):
            blk = j * bands + t
            same_core = (blk // chips) == core
            not_mine = blk != mine

            @pl.when(same_core & not_mine)
            def _():
                forward(blk).wait_recv()
                forward(blk).start()

            @pl.when(jnp.logical_not(same_core))
            def _():
                forward(blk).wait_recv()

        for t in range(bands):
            blk = j * bands + t
            rows_in = sel_buf[blk]
            out_buf[j, t, :, :hidden] = jnp.dot(
                rows_in, wg_ref[...], preferred_element_type=jnp.float32
            ).astype(out_buf.dtype)
            out_buf[j, t, :, hidden:] = jnp.dot(
                rows_in, wu_ref[...], preferred_element_type=jnp.float32
            ).astype(out_buf.dtype)

        @pl.when(j != f)
        def _():
            partial_copy(j, f).start()

        return carry

    lax.fori_loop(0, nf, band, 0)
    acc[...] = out_buf[f].astype(jnp.float32)

    lift_f = nf * ((chips + 2 * nf) // nf)

    def gather(i, carry):
        g = lax.rem(f - chip - 1 - i + lift_f, nf)

        @pl.when(g != f)
        def _():
            partial_copy(g, g).wait_recv()
            acc[...] += in_buf[g].astype(jnp.float32)

        return carry

    lax.fori_loop(0, nf, gather, 0)

    def drain(i, carry):
        h = chip_peer(i)
        direct(h).wait_send()
        forward(core * chips + h).wait_send()
        return carry

    lax.fori_loop(0, chips - 1, drain, 0)

    def drain_partial(i, carry):
        partial_copy(fsdp_peer(i), f).wait_send()
        return carry

    lax.fori_loop(0, nf - 1, drain_partial, 0)
    to_sib.wait_send()
    total = acc[...]
    o_ref[...] = (jax.nn.silu(total[..., :hidden]) * total[..., hidden:]).astype(o_ref.dtype)


def _layer_kernel(nf, chips, slot_ref, wg_hbm, wu_hbm, wd_hbm, o_ref, *scratch):
    up_scratch, act_s, down_scratch = scratch[:10], scratch[10], scratch[11:22]
    wg_v, wu_v, wd_v, local_sem = scratch[22:]
    copies = [
        pltpu.make_async_copy(src, dst, local_sem.at[k])
        for k, (src, dst) in enumerate(((wg_hbm, wg_v), (wu_hbm, wu_v), (wd_hbm, wd_v)))
    ]
    for c in copies:
        c.start()
    _up_kernel(nf, chips, slot_ref, wg_v, wu_v, act_s, *up_scratch, weights=copies[:2])
    copies[2].wait()
    _down_kernel(nf, chips, act_s, wd_v, o_ref, *down_scratch)


def moe_layer(slots, wg, wu, wd, nf, chips, cid):
    rows, d = slots.shape
    hidden = wg.shape[1]
    bands = 2 * chips // nf
    blocks = nf * bands
    return pl.pallas_call(
        functools.partial(_layer_kernel, nf, chips),
        out_shape=jax.ShapeDtypeStruct((rows, d), jnp.float32),
        in_specs=[pl.BlockSpec(memory_space=pltpu.VMEM)] + [pl.BlockSpec(memory_space=pl.ANY)] * 3,
        out_specs=pl.BlockSpec(memory_space=pltpu.VMEM),
        scratch_shapes=[
            pltpu.VMEM((2 * chips, rows, d), jnp.bfloat16),
            pltpu.VMEM((nf, bands, rows, 2 * hidden), jnp.bfloat16),
            pltpu.VMEM((nf, bands, rows, 2 * hidden), jnp.bfloat16),
            pltpu.VMEM((bands, rows, 2 * hidden), jnp.float32),
            pltpu.SemaphoreType.DMA((chips,)),
            pltpu.SemaphoreType.DMA,
            pltpu.SemaphoreType.DMA((chips,)),
            pltpu.SemaphoreType.DMA((2 * chips,)),
            pltpu.SemaphoreType.DMA((nf,)),
            pltpu.SemaphoreType.DMA((nf,)),
            pltpu.VMEM((bands, rows, hidden), jnp.bfloat16),
            pltpu.VMEM((nf, bands, rows, hidden), jnp.bfloat16),
            pltpu.VMEM((blocks, rows, d), jnp.bfloat16),
            pltpu.VMEM((chips, rows, d), jnp.bfloat16),
            pltpu.VMEM((chips, rows, d), jnp.bfloat16),
            pltpu.VMEM((chips, rows, d), jnp.bfloat16),
            pltpu.SemaphoreType.DMA((nf,)),
            pltpu.SemaphoreType.DMA((nf,)),
            pltpu.SemaphoreType.DMA((chips,)),
            pltpu.SemaphoreType.DMA((chips,)),
            pltpu.SemaphoreType.DMA((chips,)),
            pltpu.SemaphoreType.DMA((chips,)),
            pltpu.VMEM((d, hidden), jnp.bfloat16),
            pltpu.VMEM((d, hidden), jnp.bfloat16),
            pltpu.VMEM((hidden, d), jnp.bfloat16),
            pltpu.SemaphoreType.DMA((3,)),
        ],
        compiler_params=pltpu.CompilerParams(collective_id=cid, has_side_effects=True),
    )(slots, wg, wu, wd)


def local(tokens, expert_ids, route_weights, w_gate, w_up, w_down):
    window = w_gate.shape[0]
    features_dev = tokens.shape[1]
    hidden_dev = w_gate.shape[2]
    n_ed = lax.axis_size("ed")
    n_fsdp = lax.axis_size("fsdp")
    chips = n_ed // 2
    per_band = n_ed // n_fsdp
    tok_dev = tokens.shape[0]
    order = jnp.arange(tok_dev, dtype=jnp.int32)
    routed = jnp.any(expert_ids == 0, axis=1)
    lower = (order[:, None] >= order[None, :]).astype(jnp.bfloat16)
    count = jnp.dot(lower, routed.astype(jnp.bfloat16), preferred_element_type=jnp.float32)
    slot_ids = jnp.arange(CAP, dtype=jnp.float32)
    match = routed[None, :] & (count[None, :] - 1.0 == slot_ids[:, None])
    own_slots = jnp.dot(
        match.astype(jnp.bfloat16), tokens, preferred_element_type=jnp.float32
    ).astype(jnp.bfloat16)
    per_expert = jnp.sum(
        jnp.where(expert_ids == 0, route_weights, jnp.zeros_like(route_weights)), axis=1
    )
    weights_matrix = match.T.astype(jnp.float32) * per_expert[:, None]
    slot_out = moe_layer(own_slots, w_gate[0], w_up[0], w_down[0], n_fsdp, chips, 2)
    mixed = jnp.dot(
        weights_matrix, slot_out, precision=lax.Precision.HIGHEST,
        preferred_element_type=jnp.float32,
    )
    return mixed.astype(jnp.bfloat16)


def solution(mesh):
    return jax.shard_map(
        local,
        mesh=mesh,
        in_specs=(
            P("ed", "fsdp"),
            P("ed", None),
            P("ed", None),
            P(None, "fsdp", "ed"),
            P(None, "fsdp", "ed"),
            P(None, "ed", "fsdp"),
        ),
        out_specs=P("ed", "fsdp"),
        check_vma=False,
    )
```

```python
import functools

import jax
import jax.numpy as jnp
from jax import lax
from jax.experimental import pallas as pl
from jax.experimental.pallas import tpu as pltpu
from jax.sharding import PartitionSpec as P

CAP = 81
MESH = pl.DeviceIdType.MESH


def slot_match(routes, window, capacity):
    window_ids = jnp.arange(window, dtype=jnp.int32)
    routed = jnp.any(routes[:, :, None, :] == window_ids[None, None, :, None], axis=3)
    position = jnp.cumsum(routed.astype(jnp.int32), axis=1) - 1
    slot_ids = jnp.arange(capacity, dtype=jnp.int32)
    hits = routed[:, :, :, None] & (position[:, :, :, None] == slot_ids[None, None, None, :])
    return hits.astype(jnp.int32)


def take_block(block_rows, row_list):
    return jnp.take(block_rows, row_list, axis=0)


def pick_rows(blocks, routes, window, capacity):
    match = slot_match(routes, window, capacity)
    row_numbers = jnp.arange(blocks.shape[1], dtype=jnp.int32)
    source_row = jnp.sum(match * row_numbers[None, :, None, None], axis=1).reshape(
        blocks.shape[0], window * capacity
    )
    filled = jnp.sum(match, axis=1).reshape(blocks.shape[0], window * capacity)
    picked = jax.vmap(take_block)(blocks, source_row)
    picked = jnp.where(filled[:, :, None] > 0, picked, jnp.zeros_like(picked))
    return picked.reshape(blocks.shape[0], window, capacity, blocks.shape[2])


def combine_matrix(routes, weights, window, capacity):
    match = slot_match(routes[None], window, capacity)[0]
    window_ids = jnp.arange(window, dtype=jnp.int32)
    per_expert = jnp.sum(
        jnp.where(
            routes[:, None, :] == window_ids[None, :, None],
            weights[:, None, :],
            jnp.zeros_like(weights[:, None, :]),
        ),
        axis=2,
    )
    return (per_expert[:, :, None] * match.astype(weights.dtype)).reshape(
        routes.shape[0], window * capacity
    )


def _down_kernel(nf, chips, act_ref, wd_ref, o_ref, act_buf, term_buf, sib_buf, pre_buf, in_buf,
                 a_send, a_recv, s_send, s_recv, e_send, e_recv):
    bands = act_ref.shape[0]
    f = lax.axis_index("fsdp")
    e = lax.axis_index("ed")
    core = lax.rem(e, 2)
    chip = e // 2
    sib = e + 1 - 2 * core

    def fsdp_peer(i):
        return lax.rem(f + 1 + i, nf)

    def chip_peer(i):
        return lax.rem(chip + 1 + i, chips)

    def act_copy(g, slot):
        return pltpu.make_async_remote_copy(
            src_ref=act_ref,
            dst_ref=act_buf.at[slot],
            send_sem=a_send.at[g],
            recv_sem=a_recv.at[slot],
            device_id={"fsdp": g},
            device_id_type=MESH,
        )

    def to_sibling(blk):
        h = lax.rem(blk, chips)
        return pltpu.make_async_remote_copy(
            src_ref=term_buf.at[blk],
            dst_ref=sib_buf.at[h],
            send_sem=s_send.at[h],
            recv_sem=s_recv.at[h],
            device_id={"ed": sib},
            device_id_type=MESH,
        )

    def piece_copy(h, slot):
        return pltpu.make_async_remote_copy(
            src_ref=pre_buf.at[h],
            dst_ref=in_buf.at[slot],
            send_sem=e_send.at[h],
            recv_sem=e_recv.at[slot],
            device_id={"ed": h * 2 + core},
            device_id_type=MESH,
        )

    shift = nf - lax.rem(chip, nf)

    def send_act(i, carry):
        g = lax.rem(f + shift + nf - i, nf)

        @pl.when(g != f)
        def _():
            act_copy(g, f).start()

        return carry

    lax.fori_loop(0, nf, send_act, 0)
    act_buf[f] = act_ref[...]
    o_ref[...] = jnp.zeros_like(o_ref)

    def band(i, carry):
        j = lax.rem(f + chip + i, nf)

        @pl.when(j != f)
        def _():
            act_copy(j, j).wait_recv()

        for t in range(bands):
            blk = j * bands + t
            h = lax.rem(blk, chips)
            term_buf[blk] = jnp.dot(
                act_buf[j, t], wd_ref[...], preferred_element_type=jnp.float32
            ).astype(term_buf.dtype)
            same_core = (blk // chips) == core

            @pl.when(jnp.logical_not(same_core))
            def _():
                to_sibling(blk).start()

            @pl.when(same_core)
            def _():
                to_sibling(blk).wait_recv()
                pair = term_buf[blk].astype(jnp.float32) + sib_buf[h].astype(jnp.float32)
                pre_buf[h] = pair.astype(pre_buf.dtype)

                @pl.when(h == chip)
                def _():
                    o_ref[...] += pre_buf[h].astype(jnp.float32)

                @pl.when(h != chip)
                def _():
                    piece_copy(h, chip).start()

        return carry

    lax.fori_loop(0, nf, band, 0)

    def take_piece(i, carry):
        h = chip_peer(i)
        piece_copy(h, chip).wait_send()
        piece_copy(h, h).wait_recv()
        o_ref[...] += in_buf[h].astype(jnp.float32)
        return carry

    lax.fori_loop(0, chips - 1, take_piece, 0)

    def drain(h, carry):
        to_sibling((1 - core) * chips + h).wait_send()
        return carry

    lax.fori_loop(0, chips, drain, 0)

    def drain_act(i, carry):
        act_copy(fsdp_peer(i), f).wait_send()
        return carry

    lax.fori_loop(0, nf - 1, drain_act, 0)


def _up_kernel(nf, chips, slot_ref, wg_ref, wu_ref, o_ref, sel_buf, out_buf, in_buf, acc,
               e_send, s_send, fwd_send, sel_recv, f_send, f_recv, weights=()):
    bands = o_ref.shape[0]
    hidden = o_ref.shape[2]
    f = lax.axis_index("fsdp")
    e = lax.axis_index("ed")
    core = lax.rem(e, 2)
    chip = e // 2
    sib = e + 1 - 2 * core
    mine = core * chips + chip

    def fsdp_peer(i):
        return lax.rem(f + 1 + i, nf)

    def chip_peer(i):
        return lax.rem(chip + 1 + i, chips)

    def direct(h):
        return pltpu.make_async_remote_copy(
            src_ref=slot_ref,
            dst_ref=sel_buf.at[mine],
            send_sem=e_send.at[h],
            recv_sem=sel_recv.at[mine],
            device_id={"ed": h * 2 + core},
            device_id_type=MESH,
        )

    def forward(blk):
        return pltpu.make_async_remote_copy(
            src_ref=sel_buf.at[blk],
            dst_ref=sel_buf.at[blk],
            send_sem=fwd_send.at[lax.rem(blk, chips)],
            recv_sem=sel_recv.at[blk],
            device_id={"ed": sib},
            device_id_type=MESH,
        )

    def partial_copy(g, slot):
        return pltpu.make_async_remote_copy(
            src_ref=out_buf.at[g],
            dst_ref=in_buf.at[slot],
            send_sem=f_send.at[g],
            recv_sem=f_recv.at[slot],
            device_id={"fsdp": g},
            device_id_type=MESH,
        )

    barrier = pltpu.get_barrier_semaphore()

    def greet_fsdp(i, carry):
        pl.semaphore_signal(barrier, 1, device_id={"fsdp": fsdp_peer(i)}, device_id_type=MESH)
        return carry

    def greet_ed(i, carry):
        pl.semaphore_signal(barrier, 1, device_id={"ed": chip_peer(i) * 2 + core}, device_id_type=MESH)
        return carry

    lax.fori_loop(0, nf - 1, greet_fsdp, 0)
    lax.fori_loop(0, chips - 1, greet_ed, 0)
    pl.semaphore_signal(barrier, 1, device_id={"ed": sib}, device_id_type=MESH)
    pl.semaphore_wait(barrier, nf - 1 + chips)

    own_band = mine // bands
    lift = chips * ((nf + 2 * chips) // chips)

    def send_slots(k, carry):
        h = lax.rem(own_band - f - 1 - k + lift, chips)

        @pl.when(h != chip)
        def _():
            direct(h).start()

        return carry

    to_sib = pltpu.make_async_remote_copy(
        src_ref=slot_ref,
        dst_ref=sel_buf.at[mine],
        send_sem=s_send,
        recv_sem=sel_recv.at[mine],
        device_id={"ed": sib},
        device_id_type=MESH,
    )
    lax.fori_loop(0, chips, send_slots, 0)
    to_sib.start()
    sel_buf[mine] = slot_ref[...]
    for c in weights:
        c.wait()

    def band(i, carry):
        j = lax.rem(f + chip + 1 + i, nf)
        for t in range(bands):
            blk = j * bands + t
            same_core = (blk // chips) == core
            not_mine = blk != mine

            @pl.when(same_core & not_mine)
            def _():
                forward(blk).wait_recv()
                forward(blk).start()

            @pl.when(jnp.logical_not(same_core))
            def _():
                forward(blk).wait_recv()

        for t in range(bands):
            blk = j * bands + t
            rows_in = sel_buf[blk]
            out_buf[j, t, :, :hidden] = jnp.dot(
                rows_in, wg_ref[...], preferred_element_type=jnp.float32
            ).astype(out_buf.dtype)
            out_buf[j, t, :, hidden:] = jnp.dot(
                rows_in, wu_ref[...], preferred_element_type=jnp.float32
            ).astype(out_buf.dtype)

        @pl.when(j != f)
        def _():
            partial_copy(j, f).start()

        return carry

    lax.fori_loop(0, nf, band, 0)
    acc[...] = out_buf[f].astype(jnp.float32)

    lift_f = nf * ((chips + 2 * nf) // nf)

    def gather(i, carry):
        g = lax.rem(f - chip - 1 - i + lift_f, nf)

        @pl.when(g != f)
        def _():
            partial_copy(g, g).wait_recv()
            acc[...] += in_buf[g].astype(jnp.float32)

        return carry

    lax.fori_loop(0, nf, gather, 0)

    def drain(i, carry):
        h = chip_peer(i)
        direct(h).wait_send()
        forward(core * chips + h).wait_send()
        return carry

    lax.fori_loop(0, chips - 1, drain, 0)

    def drain_partial(i, carry):
        partial_copy(fsdp_peer(i), f).wait_send()
        return carry

    lax.fori_loop(0, nf - 1, drain_partial, 0)
    to_sib.wait_send()
    total = acc[...]
    o_ref[...] = (jax.nn.silu(total[..., :hidden]) * total[..., hidden:]).astype(o_ref.dtype)


def _layer_kernel(nf, chips, slot_ref, wg_hbm, wu_hbm, wd_hbm, o_ref, *scratch):
    up_scratch, act_s, down_scratch = scratch[:10], scratch[10], scratch[11:22]
    wg_v, wu_v, wd_v, local_sem = scratch[22:]
    copies = [
        pltpu.make_async_copy(src, dst, local_sem.at[k])
        for k, (src, dst) in enumerate(((wg_hbm, wg_v), (wu_hbm, wu_v), (wd_hbm, wd_v)))
    ]
    for c in copies:
        c.start()
    _up_kernel(nf, chips, slot_ref, wg_v, wu_v, act_s, *up_scratch, weights=copies[:2])
    copies[2].wait()
    _down_kernel(nf, chips, act_s, wd_v, o_ref, *down_scratch)


def moe_layer(slots, wg, wu, wd, nf, chips, cid):
    rows, d = slots.shape
    hidden = wg.shape[1]
    bands = 2 * chips // nf
    blocks = nf * bands
    return pl.pallas_call(
        functools.partial(_layer_kernel, nf, chips),
        out_shape=jax.ShapeDtypeStruct((rows, d), jnp.float32),
        in_specs=[pl.BlockSpec(memory_space=pltpu.VMEM)] + [pl.BlockSpec(memory_space=pl.ANY)] * 3,
        out_specs=pl.BlockSpec(memory_space=pltpu.VMEM),
        scratch_shapes=[
            pltpu.VMEM((2 * chips, rows, d), jnp.bfloat16),
            pltpu.VMEM((nf, bands, rows, 2 * hidden), jnp.bfloat16),
            pltpu.VMEM((nf, bands, rows, 2 * hidden), jnp.bfloat16),
            pltpu.VMEM((bands, rows, 2 * hidden), jnp.float32),
            pltpu.SemaphoreType.DMA((chips,)),
            pltpu.SemaphoreType.DMA,
            pltpu.SemaphoreType.DMA((chips,)),
            pltpu.SemaphoreType.DMA((2 * chips,)),
            pltpu.SemaphoreType.DMA((nf,)),
            pltpu.SemaphoreType.DMA((nf,)),
            pltpu.VMEM((bands, rows, hidden), jnp.bfloat16),
            pltpu.VMEM((nf, bands, rows, hidden), jnp.bfloat16),
            pltpu.VMEM((blocks, rows, d), jnp.bfloat16),
            pltpu.VMEM((chips, rows, d), jnp.bfloat16),
            pltpu.VMEM((chips, rows, d), jnp.bfloat16),
            pltpu.VMEM((chips, rows, d), jnp.bfloat16),
            pltpu.SemaphoreType.DMA((nf,)),
            pltpu.SemaphoreType.DMA((nf,)),
            pltpu.SemaphoreType.DMA((chips,)),
            pltpu.SemaphoreType.DMA((chips,)),
            pltpu.SemaphoreType.DMA((chips,)),
            pltpu.SemaphoreType.DMA((chips,)),
            pltpu.VMEM((d, hidden), jnp.bfloat16),
            pltpu.VMEM((d, hidden), jnp.bfloat16),
            pltpu.VMEM((hidden, d), jnp.bfloat16),
            pltpu.SemaphoreType.DMA((3,)),
        ],
        compiler_params=pltpu.CompilerParams(collective_id=cid, has_side_effects=True),
    )(slots, wg, wu, wd)


def local(tokens, expert_ids, route_weights, w_gate, w_up, w_down):
    window = w_gate.shape[0]
    features_dev = tokens.shape[1]
    hidden_dev = w_gate.shape[2]
    n_ed = lax.axis_size("ed")
    n_fsdp = lax.axis_size("fsdp")
    chips = n_ed // 2
    per_band = n_ed // n_fsdp
    tok_dev = tokens.shape[0]
    order = jnp.arange(tok_dev, dtype=jnp.int32)
    routed = jnp.any(expert_ids == 0, axis=1)
    lower = (order[:, None] >= order[None, :]).astype(jnp.bfloat16)
    count = jnp.dot(lower, routed.astype(jnp.bfloat16), preferred_element_type=jnp.float32)
    slot_ids = jnp.arange(CAP, dtype=jnp.float32)
    match = routed[None, :] & (count[None, :] - 1.0 == slot_ids[:, None])
    own_slots = jnp.dot(
        match.astype(jnp.bfloat16), tokens, preferred_element_type=jnp.float32
    ).astype(jnp.bfloat16)
    per_expert = jnp.sum(
        jnp.where(expert_ids == 0, route_weights, jnp.zeros_like(route_weights)), axis=1
    )
    weights_matrix = match.T.astype(jnp.float32) * per_expert[:, None]
    slot_out = moe_layer(own_slots, w_gate[0], w_up[0], w_down[0], n_fsdp, chips, 2)
    mixed = jnp.dot(
        weights_matrix, slot_out, precision=lax.Precision.HIGHEST,
        preferred_element_type=jnp.float32,
    )
    return mixed.astype(jnp.bfloat16)


def solution(mesh):
    return jax.shard_map(
        local,
        mesh=mesh,
        in_specs=(
            P("ed", "fsdp"),
            P("ed", None),
            P("ed", None),
            P(None, "fsdp", "ed"),
            P(None, "fsdp", "ed"),
            P(None, "ed", "fsdp"),
        ),
        out_specs=P("ed", "fsdp"),
        check_vma=False,
    )
```
